32 devices in a mesh: seq: 2 (over y), ctx: 4 (over z), tp: 4 (over x, core).
Axes of the slice: x: 2, y: 2, z: 4, core: 2. Of those that a mesh axis runs over, the one named last changes fastest.
Arguments:
- tokens: bfloat16 [2048, 2048], P(('seq', 'ctx')), may hold values from -6 to 6
- query_weight: bfloat16 [2048, 2048], P(('seq', 'ctx'), 'tp'), may hold values from -0.125 to 0.125
- key_weight: bfloat16 [2048, 2048], P(('seq', 'ctx'), 'tp'), may hold values from -0.125 to 0.125
- value_weight: bfloat16 [2048, 2048], P(('seq', 'ctx'), 'tp'), may hold values from -0.125 to 0.125
- output_weight: bfloat16 [2048, 2048], P('tp', ('seq', 'ctx')), may hold values from -1.5 to 1.5
- gate_weight: bfloat16 [2048, 8192], P(('seq', 'ctx'), 'tp'), may hold values from -0.125 to 0.125
- up_weight: bfloat16 [2048, 8192], P(('seq', 'ctx'), 'tp'), may hold values from -0.125 to 0.125
- down_weight: bfloat16 [8192, 2048], P('tp', ('seq', 'ctx')), may hold values from -0.0625 to 0.0625
- attention_gain: bfloat16 [2048], P(('seq', 'ctx')), may hold values from 0.25 to 1.75
- feedforward_gain: bfloat16 [2048], P(('seq', 'ctx')), may hold values from 0.25 to 1.75
- order: int32 [8], replicated, may hold values from 0 to 7, each once
- cotangent: bfloat16 [2048, 2048], P(('seq', 'ctx')), may hold values from -6 to 6
Outputs:
- block_output: bfloat16 [2048, 2048], P(('seq', 'ctx'))
- input_grad: float32 [2048, 2048], P(('seq', 'ctx'))
- query_weight_grad: float32 [2048, 2048], P(('seq', 'ctx'), 'tp')
- key_weight_grad: float32 [2048, 2048], P(('seq', 'ctx'), 'tp')
- value_weight_grad: float32 [2048, 2048], P(('seq', 'ctx'), 'tp')
- output_weight_grad: float32 [2048, 2048], P('tp', ('seq', 'ctx'))
- gate_weight_grad: float32 [2048, 8192], P(('seq', 'ctx'), 'tp')
- up_weight_grad: float32 [2048, 8192], P(('seq', 'ctx'), 'tp')
- down_weight_grad: float32 [8192, 2048], P('tp', ('seq', 'ctx'))
- attention_gain_grad: float32 [2048], P(('seq', 'ctx'))
- feedforward_gain_grad: float32 [2048], P(('seq', 'ctx'))
The draws below stay inside these ranges and needn't reach their ends.
Inputs may be any that keep to these rules, and one draw needn't show every extreme that they name: order holds every block position of a sequence once; the device of ctx index c stores blocks 2c and 2c + 1 of each sequence.
All inputs are finite; a program needn't handle non-finite values.
Results may differ from the reference program's by a relative error of at most 0.02.
Values may be sent and summed in bfloat16 or wider, within the bound.
No kernel may reach another device: no remote copies, remote signals or barrier semaphores. Data moves between devices by JAX's collectives and lax.ppermute only.
A program may use at most 128 MiB of HBM per device.

```python
import jax
import jax.numpy as jnp
from jax import lax

D = 2048
H = 32
HD = 64
FF = 8192
BLOCK = 128
BLOCKS = 8
LEN = 1024
SEQS = 2
TOKENS = 2048


def block_scale(key, extent, split, low, top_value):
    def one(dim, shards_of):
        steps = jax.random.uniform(jax.random.fold_in(jax.random.fold_in(key, 6), dim), (shards_of,), jnp.float32, low / len(split), top_value / len(split))
        return jnp.repeat(jnp.exp(steps), extent[dim] // shards_of).reshape((-1,) + (1,) * (len(extent) - dim - 1))

    level = one(*split[0])
    for cut in split[1:]:
        level = level * one(*cut)
    return level


def gaussian(key, extent, deviation, most, cuts=(), held_as=jnp.bfloat16):
    entries = deviation * jax.random.normal(key, extent, jnp.float32)
    if cuts:
        entries = entries * block_scale(key, extent, cuts, -0.22, 0.18)
    return jnp.clip(entries, -most, most).astype(held_as)


def setup_inputs(seed: int = 0) -> dict:
    streams_of = jax.random.split(jax.random.key(seed), 13)
    tokens = gaussian(streams_of[0], (TOKENS, D), 1.0, 6.0, ((0, 8),))
    query_weight = gaussian(streams_of[1], (D, H * HD), D ** -0.5, 0.125, ((0, 8), (1, 4)))
    key_weight = gaussian(streams_of[2], (D, H * HD), D ** -0.5, 0.125, ((0, 8), (1, 4)))
    value_weight = gaussian(streams_of[3], (D, H * HD), D ** -0.5, 0.125, ((0, 8), (1, 4)))
    output_weight = gaussian(streams_of[4], (H * HD, D), (H * HD // BLOCK) ** -0.5, 1.5, ((0, 4), (1, 8)))
    gate_weight = gaussian(streams_of[5], (D, FF), D ** -0.5, 0.125, ((0, 8), (1, 4)))
    up_weight = gaussian(streams_of[6], (D, FF), D ** -0.5, 0.125, ((0, 8), (1, 4)))
    down_weight = gaussian(streams_of[7], (FF, D), FF ** -0.5, 0.0625, ((0, 4), (1, 8)))
    attention_gain = jnp.clip(1.0 + 0.15 * jax.random.normal(streams_of[8], (D,), jnp.float32), 0.25, 1.75).astype(jnp.bfloat16)
    feedforward_gain = jnp.clip(1.0 + 0.15 * jax.random.normal(streams_of[9], (D,), jnp.float32), 0.25, 1.75).astype(jnp.bfloat16)
    order = jax.random.permutation(streams_of[10], BLOCKS).astype(jnp.int32)
    cotangent = gaussian(streams_of[11], (TOKENS, D), 1.0, 6.0, ((0, 8),))
    return dict(tokens=tokens, query_weight=query_weight, key_weight=key_weight, value_weight=value_weight, output_weight=output_weight, gate_weight=gate_weight, up_weight=up_weight, down_weight=down_weight, attention_gain=attention_gain, feedforward_gain=feedforward_gain, order=order, cotangent=cotangent)


THETA = 130000.0
EPS = 1e-05
HIGH = lax.Precision.HIGHEST

@jax.custom_vjp
def low(v):
    return lax.optimization_barrier(v.astype(jnp.bfloat16)).astype(jnp.float32)

@jax.custom_vjp
def low_back(v):
    return v

def low_keep(v):
    return (low(v), None)

def low_pass(kept, grad):
    return (grad,)

def back_keep(v):
    return (v, None)

def back_low(kept, grad):
    return (low(grad),)
low.defvjp(low_keep, low_pass)
low_back.defvjp(back_keep, back_low)

def matmul(left, right):
    return jnp.dot(left, right, precision=HIGH, preferred_element_type=jnp.float32)

def rms_norm(hidden, gain):
    return hidden * lax.rsqrt(lax.optimization_barrier(jnp.mean(hidden * hidden, axis=-1, keepdims=True)) + EPS) * gain

def positions(order):
    stored = jnp.arange(LEN, dtype=jnp.int32)
    return (order[(stored // BLOCK).astype(jnp.int32)] * BLOCK + stored % BLOCK).astype(jnp.int32)

def rotary(values, places):
    row_count = values.shape[0]
    by_heads = values.reshape(row_count, -1, HD)
    halfway = HD // 2
    inverse = THETA ** (-(jnp.arange(halfway, dtype=jnp.float32) * 2.0) / HD)
    angle = places.astype(jnp.float32)[:, None] * inverse[None, :]
    angle = jnp.concatenate([angle, angle], axis=1)
    cosine = jnp.cos(angle)[:, None, :]
    sine = jnp.sin(angle)[:, None, :]
    turned = jnp.concatenate([-by_heads[..., halfway:], by_heads[..., :halfway]], axis=-1)
    return (by_heads * cosine + turned * sine).reshape(row_count, -1)

def attention(queries, keys, values, allowed):

    def one_head(parts):
        query_head, key_head, value_head = parts
        scores = low_back(matmul(query_head, key_head.T) * 0.125)
        weights = jnp.where(allowed, jnp.exp(scores), 0.0)
        totals = lax.optimization_barrier(jnp.sum(weights, axis=-1, keepdims=True))
        numerator = low_back(matmul(low(weights), value_head))
        return low(numerator / totals)

    def per_head(table):
        return table.reshape(LEN, H, HD).transpose(1, 0, 2)
    mixed = lax.map(jax.checkpoint(one_head), (per_head(queries), per_head(keys), per_head(values)))
    return mixed.transpose(1, 0, 2).reshape(LEN, H * HD)

def forward(inputs, w_query, w_key, w_value, w_output, w_gate, w_up, w_down, gain_first, gain_second, places, allowed):
    normed = low(rms_norm(inputs, gain_first))
    query_proj = low_back(matmul(normed, w_query))
    key_proj = low_back(matmul(normed, w_key))
    values = low(low_back(matmul(normed, w_value)))
    every_place = jnp.tile(places, SEQS)
    queries = low(rotary(query_proj, every_place))
    keys = low(rotary(key_proj, every_place))
    mixed = jnp.concatenate([attention(queries[sequence * LEN:(sequence + 1) * LEN], keys[sequence * LEN:(sequence + 1) * LEN], values[sequence * LEN:(sequence + 1) * LEN], allowed) for sequence in range(SEQS)], axis=0)
    middle = inputs + low_back(matmul(mixed, w_output))
    normed_two = low(rms_norm(middle, gain_second))
    gate = low_back(matmul(normed_two, w_gate))
    upward = low_back(matmul(normed_two, w_up))
    hidden = low(jax.nn.silu(gate) * upward)
    return middle + low_back(matmul(hidden, w_down))

def reference(tokens, query_weight, key_weight, value_weight, output_weight, gate_weight, up_weight, down_weight, attention_gain, feedforward_gain, order, cotangent):
    places = positions(order)
    allowed = places[:, None] >= places[None, :]
    inputs = tuple((item.astype(jnp.float32) for item in (tokens, query_weight, key_weight, value_weight, output_weight, gate_weight, up_weight, down_weight, attention_gain, feedforward_gain)))

    def closed(*operands):
        return forward(*operands, places, allowed)
    result, pullback = jax.vjp(closed, *inputs)
    gradients = pullback(cotangent.astype(jnp.float32))
    return (result.astype(jnp.bfloat16), gradients[0], gradients[1], gradients[2], gradients[3], gradients[4], gradients[5], gradients[6], gradients[7], gradients[8], gradients[9])
```

```python
from functools import partial

import jax
import jax.numpy as jnp
from jax import lax
from jax.sharding import Mesh, PartitionSpec as P

HD = 64
BLOCK = 128


THETA = 130000.0
EPS = 1e-05


def shifted(block, axis, distance):
    devices = range(lax.axis_size(axis))
    route = [((i - distance) % len(devices), i) for i in devices]
    return lax.ppermute(block, axis, route)


def rms_norm(hidden, gain):
    return hidden * lax.rsqrt(jnp.mean(hidden * hidden, axis=-1, keepdims=True) + EPS) * gain


def rotary(values, places):
    row_count = values.shape[0]
    by_heads = values.reshape(row_count, -1, HD)
    halfway = HD // 2
    inverse = THETA ** (-(jnp.arange(halfway, dtype=jnp.float32) * 2.0) / HD)
    angle = places.astype(jnp.float32)[:, None] * inverse[None, :]
    angle = jnp.concatenate([angle, angle], axis=1)
    cosine = jnp.cos(angle)[:, None, :]
    sine = jnp.sin(angle)[:, None, :]
    turned = jnp.concatenate([-by_heads[..., halfway:], by_heads[..., :halfway]], axis=-1)
    return (by_heads * cosine + turned * sine).reshape(row_count, -1)


def gated(gate, upward):
    return jax.nn.silu(gate) * upward


def product(left, right):
    return jnp.dot(left, right, preferred_element_type=jnp.float32)


def contract_rows(left, right):
    return lax.dot_general(
        left, right, (((0,), (0,)), ((), ())), preferred_element_type=jnp.float32
    )


def contract_cols(left, right):
    return lax.dot_general(
        left, right, (((1,), (1,)), ((), ())), preferred_element_type=jnp.float32
    )


def key_places(order, first_row, row_total):
    stored = first_row + jnp.arange(row_total, dtype=jnp.int32)
    group_slot = stored // BLOCK
    slot_table = jnp.arange(order.shape[0], dtype=jnp.int32)
    block_place = jnp.sum(
        jnp.where(group_slot[:, None] == slot_table[None, :], order[None, :], 0), axis=1
    )
    return block_place * BLOCK + stored % BLOCK


def exp_scores(query_heads, query_places, key_rows, key_pos):
    row_total = key_rows.shape[0]
    key_heads = key_rows.reshape(row_total, -1, HD)
    scores = (
        jnp.einsum("qhd,khd->hqk", query_heads, key_heads, preferred_element_type=jnp.float32)
        * 0.125
    )
    allowed = query_places[:, None] >= key_pos[None, :]
    return (jnp.where(allowed[None], jnp.exp(scores), 0.0), key_heads)


def general_device(
    tokens,
    query_weight,
    key_weight,
    value_weight,
    output_weight,
    gate_weight,
    up_weight,
    down_weight,
    attention_gain,
    feedforward_gain,
    order,
    cotangent,
):
    rows_local = tokens.shape[0]
    ctx_index = lax.axis_index("ctx")
    ctx_total = lax.axis_size("ctx")
    gathered = (
        lax.all_gather(query_weight, ("seq", "ctx"), axis=0, tiled=True),
        lax.all_gather(key_weight, ("seq", "ctx"), axis=0, tiled=True),
        lax.all_gather(value_weight, ("seq", "ctx"), axis=0, tiled=True),
        lax.all_gather(output_weight, ("seq", "ctx"), axis=1, tiled=True),
        lax.all_gather(gate_weight, ("seq", "ctx"), axis=0, tiled=True),
        lax.all_gather(up_weight, ("seq", "ctx"), axis=0, tiled=True),
        lax.all_gather(down_weight, ("seq", "ctx"), axis=1, tiled=True),
        lax.all_gather(attention_gain, ("seq", "ctx"), axis=0, tiled=True),
        lax.all_gather(feedforward_gain, ("seq", "ctx"), axis=0, tiled=True),
    )
    (
        full_query,
        full_key,
        full_value,
        full_output,
        full_gate,
        full_up,
        full_down,
        gain_first,
        gain_second,
    ) = gathered
    inputs = tokens.astype(jnp.float32)
    query_places = key_places(order, ctx_index * rows_local, rows_local)
    normed_value, norm_back_first = jax.vjp(rms_norm, inputs, gain_first.astype(jnp.float32))
    normed = normed_value.astype(jnp.bfloat16)
    rope_here = partial(rotary, places=query_places)
    query_rot, query_back = jax.vjp(rope_here, product(normed, full_query))
    key_rot, key_back = jax.vjp(rope_here, product(normed, full_key))
    value_rows = product(normed, full_value).astype(jnp.bfloat16)
    query_rows = query_rot.astype(jnp.bfloat16)
    key_rows = key_rot.astype(jnp.bfloat16)
    width = query_rows.shape[1]
    head_count = width // HD
    query_heads = query_rows.reshape(rows_local, head_count, HD)
    packed = jnp.stack([key_rows, value_rows])
    empty_totals = jnp.zeros((rows_local, head_count), jnp.float32)
    empty_numerator = jnp.zeros((rows_local, width), jnp.float32)
    arrived = lax.all_gather(packed, "ctx", axis=1, tiled=True)
    row_total = arrived.shape[1]

    def one_block(block_index, partial_state):
        first_row = block_index * rows_local
        section = lax.dynamic_slice_in_dim(arrived, first_row, rows_local, 1)
        key_pos = key_places(order, first_row, rows_local)
        weights, key_heads = exp_scores(query_heads, query_places, section[0], key_pos)
        value_heads = section[1].reshape(rows_local, -1, HD)
        totals, numerator = partial_state
        totals = totals + jnp.sum(weights, axis=2).T
        numerator = numerator + jnp.einsum(
            "hqk,khd->qhd",
            weights.astype(jnp.bfloat16),
            value_heads,
            preferred_element_type=jnp.float32,
        ).reshape(rows_local, width)
        return (totals, numerator)

    totals, numerator = lax.fori_loop(
        0, row_total // rows_local, one_block, (empty_totals, empty_numerator)
    )
    numerator_heads = numerator.reshape(rows_local, head_count, HD)
    mixed = (numerator_heads / totals[:, :, None]).astype(jnp.bfloat16).reshape(rows_local, width)
    middle = inputs + lax.psum(product(mixed, full_output), "tp")
    normed_two_value, norm_back_second = jax.vjp(rms_norm, middle, gain_second.astype(jnp.float32))
    normed_two = normed_two_value.astype(jnp.bfloat16)
    activated, gated_back = jax.vjp(
        gated, product(normed_two, full_gate), product(normed_two, full_up)
    )
    hidden = activated.astype(jnp.bfloat16)
    block_output = middle + lax.psum(product(hidden, full_down).astype(jnp.bfloat16), "tp").astype(
        jnp.float32
    )
    back_weights = (
        lax.all_gather(query_weight, ("seq", "ctx"), axis=0, tiled=True),
        lax.all_gather(key_weight, ("seq", "ctx"), axis=0, tiled=True),
        lax.all_gather(value_weight, ("seq", "ctx"), axis=0, tiled=True),
        lax.all_gather(output_weight, ("seq", "ctx"), axis=1, tiled=True),
        lax.all_gather(gate_weight, ("seq", "ctx"), axis=0, tiled=True),
        lax.all_gather(up_weight, ("seq", "ctx"), axis=0, tiled=True),
        lax.all_gather(down_weight, ("seq", "ctx"), axis=1, tiled=True),
        lax.all_gather(attention_gain, ("seq", "ctx"), axis=0, tiled=True),
        lax.all_gather(feedforward_gain, ("seq", "ctx"), axis=0, tiled=True),
    )
    (
        back_query,
        back_key,
        back_value,
        back_output,
        back_gate,
        back_up,
        back_down,
        gain_unused,
        gain_spare,
    ) = back_weights
    down_grad = contract_rows(hidden, cotangent)
    hidden_grad = contract_cols(cotangent, back_down)
    gate_grad, upward_grad = gated_back(hidden_grad)
    gate_grad = gate_grad.astype(jnp.bfloat16)
    upward_grad = upward_grad.astype(jnp.bfloat16)
    gate_wgrad = contract_rows(normed_two, gate_grad)
    upward_wgrad = contract_rows(normed_two, upward_grad)
    normed_two_grad = lax.psum(
        contract_cols(gate_grad, back_gate) + contract_cols(upward_grad, back_up), "tp"
    )
    middle_norm_grad, second_gain_grad = norm_back_second(normed_two_grad)
    middle_grad = cotangent.astype(jnp.float32) + middle_norm_grad
    branch_grad = middle_grad.astype(jnp.bfloat16)
    output_wgrad = contract_rows(mixed, branch_grad)
    mixed_grad = contract_cols(branch_grad, back_output).reshape(rows_local, head_count, HD)
    numerator_grad = (mixed_grad / totals[:, :, None]).astype(jnp.bfloat16)
    totals_grad = -jnp.sum(mixed_grad * numerator_heads, axis=2) / (totals * totals)
    totals_grad_heads = totals_grad.T[:, :, None]

    def visit(turn_index, state):
        visiting, carried, query_acc = state
        source = (ctx_index - turn_index) % ctx_total
        key_pos = key_places(order, source * rows_local, rows_local)
        weights, key_heads = exp_scores(query_heads, query_places, visiting[0], key_pos)
        value_heads = visiting[1].reshape(rows_local, -1, HD)
        through = jnp.einsum(
            "qhd,khd->hqk", numerator_grad, value_heads, preferred_element_type=jnp.float32
        )
        slopes = (weights * (through + totals_grad_heads)).astype(jnp.bfloat16)
        query_acc = (
            query_acc
            + jnp.einsum("hqk,khd->qhd", slopes, key_heads, preferred_element_type=jnp.float32)
            * 0.125
        )
        key_term = (
            jnp.einsum("hqk,qhd->khd", slopes, query_heads, preferred_element_type=jnp.float32)
            * 0.125
        )
        value_term = jnp.einsum(
            "hqk,qhd->khd",
            weights.astype(jnp.bfloat16),
            numerator_grad,
            preferred_element_type=jnp.float32,
        )
        carried = carried + jnp.stack(
            [key_term.reshape(rows_local, width), value_term.reshape(rows_local, width)]
        )
        visiting = shifted(visiting, "ctx", 1)
        carried = shifted(carried, "ctx", 1)
        return (visiting, carried, query_acc)

    start_state = (
        packed,
        jnp.zeros((2, rows_local, width), jnp.float32),
        jnp.zeros((rows_local, head_count, HD), jnp.float32),
    )
    ended, key_value_grad, query_acc = lax.fori_loop(0, ctx_total, visit, start_state)
    query_proj_grad = query_back(query_acc.reshape(rows_local, width))[0].astype(jnp.bfloat16)
    key_proj_grad = key_back(key_value_grad[0])[0].astype(jnp.bfloat16)
    value_grad = key_value_grad[1].astype(jnp.bfloat16)
    query_wgrad = contract_rows(normed, query_proj_grad)
    key_wgrad = contract_rows(normed, key_proj_grad)
    value_wgrad = contract_rows(normed, value_grad)
    normed_grad = lax.psum(
        (
            contract_cols(query_proj_grad, back_query)
            + contract_cols(key_proj_grad, back_key)
            + contract_cols(value_grad, back_value)
        ).astype(jnp.bfloat16),
        "tp",
    ).astype(jnp.float32)
    input_norm_grad, first_gain_grad = norm_back_first(normed_grad)
    input_grad = middle_grad + input_norm_grad
    scattered = (
        lax.psum_scatter(
            query_wgrad.astype(jnp.bfloat16), ("seq", "ctx"), scatter_dimension=0, tiled=True
        ).astype(jnp.float32),
        lax.psum_scatter(
            key_wgrad.astype(jnp.bfloat16), ("seq", "ctx"), scatter_dimension=0, tiled=True
        ).astype(jnp.float32),
        lax.psum_scatter(
            value_wgrad.astype(jnp.bfloat16), ("seq", "ctx"), scatter_dimension=0, tiled=True
        ).astype(jnp.float32),
        lax.psum_scatter(
            output_wgrad.astype(jnp.bfloat16), ("seq", "ctx"), scatter_dimension=1, tiled=True
        ).astype(jnp.float32),
        lax.psum_scatter(
            gate_wgrad.astype(jnp.bfloat16), ("seq", "ctx"), scatter_dimension=0, tiled=True
        ).astype(jnp.float32),
        lax.psum_scatter(
            upward_wgrad.astype(jnp.bfloat16), ("seq", "ctx"), scatter_dimension=0, tiled=True
        ).astype(jnp.float32),
        lax.psum_scatter(
            down_grad.astype(jnp.bfloat16), ("seq", "ctx"), scatter_dimension=1, tiled=True
        ).astype(jnp.float32),
        lax.psum_scatter(
            first_gain_grad.astype(jnp.bfloat16), ("seq", "ctx"), scatter_dimension=0, tiled=True
        ).astype(jnp.float32),
        lax.psum_scatter(
            second_gain_grad.astype(jnp.bfloat16), ("seq", "ctx"), scatter_dimension=0, tiled=True
        ).astype(jnp.float32),
    )
    return (
        block_output.astype(jnp.bfloat16),
        input_grad,
        scattered[0],
        scattered[1],
        scattered[2],
        scattered[3],
        scattered[4],
        scattered[5],
        scattered[6],
        scattered[7],
        scattered[8],
    )


def general_solution(mesh):
    placed = (
        P(("seq", "ctx"), None),
        P(("seq", "ctx"), "tp"),
        P(("seq", "ctx"), "tp"),
        P(("seq", "ctx"), "tp"),
        P("tp", ("seq", "ctx")),
        P(("seq", "ctx"), "tp"),
        P(("seq", "ctx"), "tp"),
        P("tp", ("seq", "ctx")),
        P(("seq", "ctx")),
        P(("seq", "ctx")),
        P(),
        P(("seq", "ctx"), None),
    )
    return jax.shard_map(
        general_device,
        mesh=mesh,
        in_specs=placed,
        out_specs=(
            P(("seq", "ctx"), None),
            P(("seq", "ctx"), None),
            P(("seq", "ctx"), "tp"),
            P(("seq", "ctx"), "tp"),
            P(("seq", "ctx"), "tp"),
            P("tp", ("seq", "ctx")),
            P(("seq", "ctx"), "tp"),
            P(("seq", "ctx"), "tp"),
            P("tp", ("seq", "ctx")),
            P(("seq", "ctx")),
            P(("seq", "ctx")),
        ),
        check_vma=False,
    )


LOW = jnp.bfloat16


def swap(value, axis, mask=1):
    pairs = [(i, i ^ mask) for i in range(lax.axis_size(axis))]
    return lax.ppermute(value, axis, pairs)


def after(value, *earlier):
    return lax.optimization_barrier((value, earlier))[0]


def gather_rows(shard):
    near = swap(shard, "ctx", 1)
    far = swap(shard, "ctx", 2)
    last = swap(far, "ctx", 1)
    line = [shard, near, far, last]
    line = jnp.concatenate(line + [swap(piece, "x") for piece in line])
    return jnp.concatenate([line, swap(line, "core")])


def gather_local_rows(local, x, core):
    count = local.shape[0] // 4

    def own(a, b):
        return lax.dynamic_slice_in_dim(local, ((x ^ a) * 2 + (core ^ b)) * count, count, 0)

    shard = own(0, 0)
    near = swap(shard, "ctx", 1)
    far = swap(shard, "ctx", 2)
    last = swap(far, "ctx", 1)
    line = [near, far, last]
    line_x = [swap(piece, "x") for piece in line]
    other = swap(jnp.concatenate(line + line_x), "core")
    three = 3 * count
    return jnp.concatenate(
        [own(0, 0)]
        + line
        + [own(1, 0)]
        + line_x
        + [own(0, 1), other[:three], own(1, 1), other[three:]]
    )


def scatter_rows(keep, give):
    mine = keep + swap(give.astype(LOW), "core").astype(jnp.float32)
    half = mine.shape[0] // 2
    count = half // 4
    away = mine[half:].astype(LOW)
    piece = [
        mine[j * count : (j + 1) * count]
        + swap(away[j * count : (j + 1) * count], "x").astype(jnp.float32)
        for j in (3, 2, 1, 0)
    ][::-1]
    last = swap(piece[3].astype(LOW), "ctx", 1)
    near = swap(piece[1].astype(LOW), "ctx", 1)
    far = swap((piece[2] + last.astype(jnp.float32)).astype(LOW), "ctx", 2)
    return piece[0] + near.astype(jnp.float32) + far.astype(jnp.float32)


def spread(pieces, base, axis):
    got = [pieces[0], swap(pieces[1], "ctx", 1), swap(pieces[2], "ctx", 2), swap(pieces[3], "ctx", 3)]
    got = got + [swap(piece, "seq") for piece in got]
    extent = pieces[0].shape[axis]
    shape = list(pieces[0].shape)
    shape[axis] = extent * 8
    whole = jnp.zeros(shape, pieces[0].dtype)
    for j, piece in enumerate(got):
        whole = lax.dynamic_update_slice_in_dim(whole, piece, (base ^ j) * extent, axis)
    return whole


def collect(grad, seq, ctx, axis):
    half = grad.shape[axis] // 2
    extent = half // 4
    give = lax.dynamic_slice_in_dim(grad, (1 - seq) * half, half, axis).astype(LOW)
    keep = lax.dynamic_slice_in_dim(grad, seq * half, half, axis)
    total = (keep + swap(give, "seq").astype(jnp.float32)).astype(LOW)
    pieces = [
        lax.dynamic_slice_in_dim(total, (ctx ^ j) * extent, extent, axis) for j in range(4)
    ]
    return [pieces[0]] + [swap(pieces[j], "ctx", j) for j in (1, 2, 3)]


def place(pieces, ctx, axis):
    extent = pieces[0].shape[axis]
    shape = list(pieces[0].shape)
    shape[axis] = extent * 4
    whole = jnp.zeros(shape, jnp.float32)
    for j, piece in enumerate(pieces):
        whole = lax.dynamic_update_slice_in_dim(
            whole, piece.astype(jnp.float32), (ctx ^ j) * extent, axis
        )
    return whole


def place_rows(shard, x, core):
    line = [shard, swap(shard, "x")]
    line = line + [swap(piece, "core") for piece in line]
    count = shard.shape[0]
    whole = jnp.zeros((4 * count, shard.shape[1]), shard.dtype)
    for j, piece in enumerate(line):
        whole = lax.dynamic_update_slice_in_dim(
            whole, piece, ((x ^ (j & 1)) * 2 + (core ^ (j >> 1))) * count, 0
        )
    return whole


def turn(values, cosine, sine):
    halfway = HD // 2
    parts = []
    for first in range(0, values.shape[1], HD):
        low, high = values[:, first : first + halfway], values[:, first + halfway : first + HD]
        parts += [low * cosine - high * sine, high * cosine + low * sine]
    return jnp.concatenate(parts, axis=1)


def fast_device(
    tokens,
    query_weight,
    key_weight,
    value_weight,
    output_weight,
    gate_weight,
    up_weight,
    down_weight,
    attention_gain,
    feedforward_gain,
    order,
    cotangent,
):
    f32 = jnp.float32
    seq, ctx = lax.axis_index("seq"), lax.axis_index("ctx")
    x, core = lax.axis_index("x"), lax.axis_index("core")
    base = seq * 4 + ctx
    local_rows = tokens.shape[0]
    count = local_rows // 4
    width = query_weight.shape[1] // 4
    unit = gate_weight.shape[1] // 4
    depth = query_weight.shape[0]

    def columns(weight, j, extent):
        return lax.dynamic_slice_in_dim(weight, (ctx ^ j) * extent, extent, 1)

    def rows_of(weight, j, extent):
        return lax.dynamic_slice_in_dim(weight, (ctx ^ j) * extent, extent, 0)

    gains = jnp.zeros((16, 3 * width), LOW)
    gains = gains.at[0, :depth].set(attention_gain).at[1, :depth].set(feedforward_gain)
    qkv_pieces = [
        jnp.concatenate(
            [
                jnp.concatenate(
                    [columns(w, j, width) for w in (query_weight, key_weight, value_weight)], axis=1
                ),
                gains,
            ]
        )[None]
        for j in range(4)
    ]
    every_token = gather_local_rows(tokens, x, core)
    qkv_blocks = spread(qkv_pieces, base, 0)
    qkv_full = qkv_blocks[:, :depth].reshape(8 * depth, 3 * width)
    gain_first = qkv_blocks[:, depth, :depth].reshape(1, 8 * depth).astype(f32)
    gain_second = qkv_blocks[:, depth + 1, :depth].reshape(1, 8 * depth).astype(f32)

    output_full = spread([rows_of(output_weight, j, width) for j in range(4)], base, 1)
    gate_up_full = spread(
        [
            jnp.concatenate([columns(gate_weight, j, unit), columns(up_weight, j, unit)], axis=1)
            for j in range(4)
        ],
        base,
        0,
    )
    down_full = spread([rows_of(down_weight, j, unit) for j in range(4)], base, 1)
    every_cotangent = gather_local_rows(cotangent, x, core)

    blocks = jnp.arange(16, dtype=jnp.int32)
    stored = (
        (ctx ^ (blocks & 3)) * local_rows
        + (x ^ ((blocks >> 2) & 1)) * (2 * count)
        + (core ^ (blocks >> 3)) * count
    )
    stored = (stored[:, None] + jnp.arange(count, dtype=jnp.int32)[None, :]).reshape(-1)
    slots = jnp.arange(order.shape[0], dtype=jnp.int32)
    places = jnp.sum(
        jnp.where((stored // BLOCK)[:, None] == slots[None, :], order[None, :], 0), axis=1
    )
    places = places * BLOCK + stored % BLOCK
    inverse = THETA ** (-(jnp.arange(HD // 2, dtype=f32) * 2.0) / HD)
    angle = places.astype(f32)[:, None] * inverse[None, :]
    cosine, sine = jnp.cos(angle), jnp.sin(angle)
    allowed = places[:, None] >= places[None, :]

    every_input = every_token.astype(f32)
    scale_first = lax.rsqrt(jnp.mean(every_input * every_input, axis=1, keepdims=True) + EPS)
    normed = (every_input * scale_first * gain_first).astype(LOW)
    projected = product(normed, qkv_full)
    queries = turn(projected[:, :width], cosine, sine).astype(LOW)
    keys = turn(projected[:, width : 2 * width], cosine, sine).astype(LOW)
    values = projected[:, 2 * width :].astype(LOW)
    heads = [slice(first, first + HD) for first in range(0, width, HD)]
    weights, totals, numerator, mixed = [], [], [], []
    for head in heads:
        scores = contract_cols(queries[:, head], keys[:, head]) * 0.125
        weight = jnp.where(allowed, jnp.exp(scores), 0.0)
        total = jnp.sum(weight, axis=1, keepdims=True)
        summed = product(weight.astype(LOW), values[:, head])
        weights.append(weight)
        totals.append(total)
        numerator.append(summed)
        mixed.append((summed / total).astype(LOW))
    mixed = jnp.concatenate(mixed, axis=1)
    half = mixed.shape[0] // 2

    give = product(mixed[half:], output_full)
    keep = product(mixed[:half], output_full)
    own_input = lax.dynamic_slice_in_dim(tokens, (x * 2 + core) * count, count, 0).astype(f32)
    own_cotangent = lax.dynamic_slice_in_dim(cotangent, (x * 2 + core) * count, count, 0)
    own_cotangent = own_cotangent.astype(f32)
    middle = own_input + scatter_rows(keep, give)
    scale_second = lax.rsqrt(jnp.mean(middle * middle, axis=1, keepdims=True) + EPS)
    normed_two = gather_rows((middle * scale_second * gain_second).astype(LOW))

    gate_up = product(normed_two, gate_up_full)
    hidden_grad = contract_cols(every_cotangent, down_full)
    gate, up = gate_up[:, :unit], gate_up[:, unit:]
    sigmoid = 1.0 / (1.0 + jnp.exp(-gate))
    silu = gate * sigmoid
    hidden = (silu * up).astype(LOW)
    gate_grad = hidden_grad * up * (sigmoid * (1.0 + gate * (1.0 - sigmoid)))
    gate_up_grad = jnp.concatenate([gate_grad, hidden_grad * silu], axis=1).astype(LOW)
    give = contract_cols(gate_up_grad[half:], gate_up_full)
    keep = contract_cols(gate_up_grad[:half], gate_up_full)
    normed_two_grad = scatter_rows(keep, give)
    second_gain_part = jnp.sum(normed_two_grad * middle * scale_second, axis=0)
    scaled = normed_two_grad * gain_second
    middle_grad = (
        own_cotangent
        + scale_second * scaled
        - middle * scale_second**3 * jnp.mean(scaled * middle, axis=1, keepdims=True)
    )
    branch_grad = gather_rows(middle_grad.astype(LOW))

    down_pieces = collect(contract_rows(hidden, every_cotangent), seq, ctx, 1)
    gate_up_pieces = collect(contract_rows(normed_two, gate_up_grad), seq, ctx, 0)
    produced = scatter_rows(product(hidden[:half], down_full), product(hidden[half:], down_full))
    block_output = place_rows((middle + produced).astype(LOW), x, core)

    mixed_grad = contract_cols(branch_grad, output_full)
    output_pieces = collect(contract_rows(mixed, branch_grad), seq, ctx, 1)
    query_grad, key_grad, value_grad = [], [], []
    for index, head in enumerate(heads):
        grad = mixed_grad[:, head]
        numerator_grad = (grad / totals[index]).astype(LOW)
        total_grad = -jnp.sum(grad * numerator[index], axis=1, keepdims=True) / (
            totals[index] * totals[index]
        )
        through = contract_cols(numerator_grad, values[:, head])
        slopes = (weights[index] * (through + total_grad)).astype(LOW)
        query_grad.append(product(slopes, keys[:, head]) * 0.125)
        key_grad.append(contract_rows(slopes, queries[:, head]) * 0.125)
        value_grad.append(contract_rows(weights[index].astype(LOW), numerator_grad))
    projected_grad = jnp.concatenate(
        [
            turn(jnp.concatenate(query_grad, axis=1), cosine, -sine),
            turn(jnp.concatenate(key_grad, axis=1), cosine, -sine),
            jnp.concatenate(value_grad, axis=1),
        ],
        axis=1,
    ).astype(LOW)
    give = contract_cols(projected_grad[half:], qkv_full)
    keep = contract_cols(projected_grad[:half], qkv_full)
    normed_grad = scatter_rows(keep, give)
    scale_own = lax.rsqrt(jnp.mean(own_input * own_input, axis=1, keepdims=True) + EPS)
    first_gain_part = jnp.sum(normed_grad * own_input * scale_own, axis=0)
    scaled = normed_grad * gain_first
    input_grad = (
        middle_grad
        + scale_own * scaled
        - own_input * scale_own**3 * jnp.mean(scaled * own_input, axis=1, keepdims=True)
    )
    input_grad = place_rows(input_grad.astype(LOW), x, core).astype(f32)
    qkv_pieces = collect(contract_rows(normed, projected_grad), seq, ctx, 0)

    part = jnp.stack([first_gain_part, second_gain_part])
    part = part + swap(part, "core")
    part = part + swap(part, "x")
    extent = part.shape[1] // 2
    part = lax.dynamic_slice_in_dim(part, seq * extent, extent, 1) + swap(
        lax.dynamic_slice_in_dim(part, (1 - seq) * extent, extent, 1), "seq"
    )
    share = [lax.dynamic_slice_in_dim(part, (ctx ^ j) * depth, depth, 1) for j in range(4)]
    gain_grads = share[0] + swap(share[1], "ctx", 1)
    gain_grads = gain_grads + swap(share[2], "ctx", 2) + swap(share[3], "ctx", 3)

    def cut(pieces, first, extent):
        return place([piece[:, first : first + extent] for piece in pieces], ctx, 1)

    return (
        block_output,
        input_grad,
        cut(qkv_pieces, 0, width),
        cut(qkv_pieces, width, width),
        cut(qkv_pieces, 2 * width, width),
        place(output_pieces, ctx, 0),
        cut(gate_up_pieces, 0, unit),
        cut(gate_up_pieces, unit, unit),
        place(down_pieces, ctx, 0),
        gain_grads[0],
        gain_grads[1],
    )


def fast_solution(mesh):
    sizes = mesh.shape
    lines = Mesh(
        mesh.devices.reshape(sizes["seq"], sizes["ctx"], 2, 2), ("seq", "ctx", "x", "core")
    )
    rows, heads = ("seq", "ctx"), ("x", "core")
    wide, tall = P(rows, heads), P(heads, rows)
    return jax.shard_map(
        fast_device,
        mesh=lines,
        in_specs=(
            P(rows, None),
            wide,
            wide,
            wide,
            tall,
            wide,
            wide,
            tall,
            P(rows),
            P(rows),
            P(),
            P(rows, None),
        ),
        out_specs=(
            P(rows, None),
            P(rows, None),
            wide,
            wide,
            wide,
            tall,
            wide,
            wide,
            tall,
            P(rows),
            P(rows),
        ),
        check_vma=False,
    )


def solution(mesh):
    sizes = mesh.shape
    if mesh.axis_names == ("seq", "ctx", "tp") and tuple(sizes.values()) == (2, 4, 4):
        return fast_solution(mesh)
    return general_solution(mesh)
```

```python
from functools import partial

import jax
import jax.numpy as jnp
from jax import lax
from jax.experimental import pallas as pl
from jax.experimental.pallas import tpu as pltpu
from jax.sharding import Mesh, PartitionSpec as P

HD = 64
SEQ, CTX, TP, X, CORE = ("seq", "ctx", "tp", "x", "core")
BLOCK = 128


THETA = 130000.0
EPS = 1e-05


def shifted(block, axis, distance):
    devices = range(lax.axis_size(axis))
    route = [((i - distance) % len(devices), i) for i in devices]
    return lax.ppermute(block, axis, route)


def rms_norm(hidden, gain):
    return hidden * lax.rsqrt(jnp.mean(hidden * hidden, axis=-1, keepdims=True) + EPS) * gain


def rotary(values, places):
    row_count = values.shape[0]
    by_heads = values.reshape(row_count, -1, HD)
    halfway = HD // 2
    inverse = THETA ** (-(jnp.arange(halfway, dtype=jnp.float32) * 2.0) / HD)
    angle = places.astype(jnp.float32)[:, None] * inverse[None, :]
    angle = jnp.concatenate([angle, angle], axis=1)
    cosine = jnp.cos(angle)[:, None, :]
    sine = jnp.sin(angle)[:, None, :]
    turned = jnp.concatenate([-by_heads[..., halfway:], by_heads[..., :halfway]], axis=-1)
    return (by_heads * cosine + turned * sine).reshape(row_count, -1)


def gated(gate, upward):
    return jax.nn.silu(gate) * upward


def product(left, right):
    return jnp.dot(left, right, preferred_element_type=jnp.float32)


def contract_rows(left, right):
    return lax.dot_general(
        left, right, (((0,), (0,)), ((), ())), preferred_element_type=jnp.float32
    )


def contract_cols(left, right):
    return lax.dot_general(
        left, right, (((1,), (1,)), ((), ())), preferred_element_type=jnp.float32
    )


def key_places(order, first_row, row_total):
    stored = first_row + jnp.arange(row_total, dtype=jnp.int32)
    group_slot = stored // BLOCK
    slot_table = jnp.arange(order.shape[0], dtype=jnp.int32)
    block_place = jnp.sum(
        jnp.where(group_slot[:, None] == slot_table[None, :], order[None, :], 0), axis=1
    )
    return block_place * BLOCK + stored % BLOCK


def exp_scores(query_heads, query_places, key_rows, key_pos):
    row_total = key_rows.shape[0]
    key_heads = key_rows.reshape(row_total, -1, HD)
    scores = (
        jnp.einsum("qhd,khd->hqk", query_heads, key_heads, preferred_element_type=jnp.float32)
        * 0.125
    )
    allowed = query_places[:, None] >= key_pos[None, :]
    return (jnp.where(allowed[None], jnp.exp(scores), 0.0), key_heads)


def general_device(
    tokens,
    query_weight,
    key_weight,
    value_weight,
    output_weight,
    gate_weight,
    up_weight,
    down_weight,
    attention_gain,
    feedforward_gain,
    order,
    cotangent,
):
    rows_local = tokens.shape[0]
    ctx_index = lax.axis_index(CTX)
    ctx_total = lax.axis_size(CTX)
    gathered = (
        lax.all_gather(query_weight, (SEQ, CTX), axis=0, tiled=True),
        lax.all_gather(key_weight, (SEQ, CTX), axis=0, tiled=True),
        lax.all_gather(value_weight, (SEQ, CTX), axis=0, tiled=True),
        lax.all_gather(output_weight, (SEQ, CTX), axis=1, tiled=True),
        lax.all_gather(gate_weight, (SEQ, CTX), axis=0, tiled=True),
        lax.all_gather(up_weight, (SEQ, CTX), axis=0, tiled=True),
        lax.all_gather(down_weight, (SEQ, CTX), axis=1, tiled=True),
        lax.all_gather(attention_gain, (SEQ, CTX), axis=0, tiled=True),
        lax.all_gather(feedforward_gain, (SEQ, CTX), axis=0, tiled=True),
    )
    (
        full_query,
        full_key,
        full_value,
        full_output,
        full_gate,
        full_up,
        full_down,
        gain_first,
        gain_second,
    ) = gathered
    inputs = tokens.astype(jnp.float32)
    query_places = key_places(order, ctx_index * rows_local, rows_local)
    normed_value, norm_back_first = jax.vjp(rms_norm, inputs, gain_first.astype(jnp.float32))
    normed = normed_value.astype(jnp.bfloat16)
    rope_here = partial(rotary, places=query_places)
    query_rot, query_back = jax.vjp(rope_here, product(normed, full_query))
    key_rot, key_back = jax.vjp(rope_here, product(normed, full_key))
    value_rows = product(normed, full_value).astype(jnp.bfloat16)
    query_rows = query_rot.astype(jnp.bfloat16)
    key_rows = key_rot.astype(jnp.bfloat16)
    width = query_rows.shape[1]
    head_count = width // HD
    query_heads = query_rows.reshape(rows_local, head_count, HD)
    packed = jnp.stack([key_rows, value_rows])
    empty_totals = jnp.zeros((rows_local, head_count), jnp.float32)
    empty_numerator = jnp.zeros((rows_local, width), jnp.float32)
    arrived = lax.all_gather(packed, CTX, axis=1, tiled=True)
    row_total = arrived.shape[1]

    def one_block(block_index, partial_state):
        first_row = block_index * rows_local
        section = lax.dynamic_slice_in_dim(arrived, first_row, rows_local, 1)
        key_pos = key_places(order, first_row, rows_local)
        weights, key_heads = exp_scores(query_heads, query_places, section[0], key_pos)
        value_heads = section[1].reshape(rows_local, -1, HD)
        totals, numerator = partial_state
        totals = totals + jnp.sum(weights, axis=2).T
        numerator = numerator + jnp.einsum(
            "hqk,khd->qhd",
            weights.astype(jnp.bfloat16),
            value_heads,
            preferred_element_type=jnp.float32,
        ).reshape(rows_local, width)
        return (totals, numerator)

    totals, numerator = lax.fori_loop(
        0, row_total // rows_local, one_block, (empty_totals, empty_numerator)
    )
    numerator_heads = numerator.reshape(rows_local, head_count, HD)
    mixed = (numerator_heads / totals[:, :, None]).astype(jnp.bfloat16).reshape(rows_local, width)
    middle = inputs + lax.psum(product(mixed, full_output), TP)
    normed_two_value, norm_back_second = jax.vjp(rms_norm, middle, gain_second.astype(jnp.float32))
    normed_two = normed_two_value.astype(jnp.bfloat16)
    activated, gated_back = jax.vjp(
        gated, product(normed_two, full_gate), product(normed_two, full_up)
    )
    hidden = activated.astype(jnp.bfloat16)
    block_output = middle + lax.psum(product(hidden, full_down).astype(jnp.bfloat16), TP).astype(
        jnp.float32
    )
    back_weights = (
        lax.all_gather(query_weight, (SEQ, CTX), axis=0, tiled=True),
        lax.all_gather(key_weight, (SEQ, CTX), axis=0, tiled=True),
        lax.all_gather(value_weight, (SEQ, CTX), axis=0, tiled=True),
        lax.all_gather(output_weight, (SEQ, CTX), axis=1, tiled=True),
        lax.all_gather(gate_weight, (SEQ, CTX), axis=0, tiled=True),
        lax.all_gather(up_weight, (SEQ, CTX), axis=0, tiled=True),
        lax.all_gather(down_weight, (SEQ, CTX), axis=1, tiled=True),
        lax.all_gather(attention_gain, (SEQ, CTX), axis=0, tiled=True),
        lax.all_gather(feedforward_gain, (SEQ, CTX), axis=0, tiled=True),
    )
    (
        back_query,
        back_key,
        back_value,
        back_output,
        back_gate,
        back_up,
        back_down,
        gain_unused,
        gain_spare,
    ) = back_weights
    down_grad = contract_rows(hidden, cotangent)
    hidden_grad = contract_cols(cotangent, back_down)
    gate_grad, upward_grad = gated_back(hidden_grad)
    gate_grad = gate_grad.astype(jnp.bfloat16)
    upward_grad = upward_grad.astype(jnp.bfloat16)
    gate_wgrad = contract_rows(normed_two, gate_grad)
    upward_wgrad = contract_rows(normed_two, upward_grad)
    normed_two_grad = lax.psum(
        contract_cols(gate_grad, back_gate) + contract_cols(upward_grad, back_up), TP
    )
    middle_norm_grad, second_gain_grad = norm_back_second(normed_two_grad)
    middle_grad = cotangent.astype(jnp.float32) + middle_norm_grad
    branch_grad = middle_grad.astype(jnp.bfloat16)
    output_wgrad = contract_rows(mixed, branch_grad)
    mixed_grad = contract_cols(branch_grad, back_output).reshape(rows_local, head_count, HD)
    numerator_grad = (mixed_grad / totals[:, :, None]).astype(jnp.bfloat16)
    totals_grad = -jnp.sum(mixed_grad * numerator_heads, axis=2) / (totals * totals)
    totals_grad_heads = totals_grad.T[:, :, None]

    def visit(turn_index, state):
        visiting, carried, query_acc = state
        source = (ctx_index - turn_index) % ctx_total
        key_pos = key_places(order, source * rows_local, rows_local)
        weights, key_heads = exp_scores(query_heads, query_places, visiting[0], key_pos)
        value_heads = visiting[1].reshape(rows_local, -1, HD)
        through = jnp.einsum(
            "qhd,khd->hqk", numerator_grad, value_heads, preferred_element_type=jnp.float32
        )
        slopes = (weights * (through + totals_grad_heads)).astype(jnp.bfloat16)
        query_acc = (
            query_acc
            + jnp.einsum("hqk,khd->qhd", slopes, key_heads, preferred_element_type=jnp.float32)
            * 0.125
        )
        key_term = (
            jnp.einsum("hqk,qhd->khd", slopes, query_heads, preferred_element_type=jnp.float32)
            * 0.125
        )
        value_term = jnp.einsum(
            "hqk,qhd->khd",
            weights.astype(jnp.bfloat16),
            numerator_grad,
            preferred_element_type=jnp.float32,
        )
        carried = carried + jnp.stack(
            [key_term.reshape(rows_local, width), value_term.reshape(rows_local, width)]
        )
        visiting = shifted(visiting, CTX, 1)
        carried = shifted(carried, CTX, 1)
        return (visiting, carried, query_acc)

    start_state = (
        packed,
        jnp.zeros((2, rows_local, width), jnp.float32),
        jnp.zeros((rows_local, head_count, HD), jnp.float32),
    )
    ended, key_value_grad, query_acc = lax.fori_loop(0, ctx_total, visit, start_state)
    query_proj_grad = query_back(query_acc.reshape(rows_local, width))[0].astype(jnp.bfloat16)
    key_proj_grad = key_back(key_value_grad[0])[0].astype(jnp.bfloat16)
    value_grad = key_value_grad[1].astype(jnp.bfloat16)
    query_wgrad = contract_rows(normed, query_proj_grad)
    key_wgrad = contract_rows(normed, key_proj_grad)
    value_wgrad = contract_rows(normed, value_grad)
    normed_grad = lax.psum(
        (
            contract_cols(query_proj_grad, back_query)
            + contract_cols(key_proj_grad, back_key)
            + contract_cols(value_grad, back_value)
        ).astype(jnp.bfloat16),
        TP,
    ).astype(jnp.float32)
    input_norm_grad, first_gain_grad = norm_back_first(normed_grad)
    input_grad = middle_grad + input_norm_grad
    scattered = (
        lax.psum_scatter(
            query_wgrad.astype(jnp.bfloat16), (SEQ, CTX), scatter_dimension=0, tiled=True
        ).astype(jnp.float32),
        lax.psum_scatter(
            key_wgrad.astype(jnp.bfloat16), (SEQ, CTX), scatter_dimension=0, tiled=True
        ).astype(jnp.float32),
        lax.psum_scatter(
            value_wgrad.astype(jnp.bfloat16), (SEQ, CTX), scatter_dimension=0, tiled=True
        ).astype(jnp.float32),
        lax.psum_scatter(
            output_wgrad.astype(jnp.bfloat16), (SEQ, CTX), scatter_dimension=1, tiled=True
        ).astype(jnp.float32),
        lax.psum_scatter(
            gate_wgrad.astype(jnp.bfloat16), (SEQ, CTX), scatter_dimension=0, tiled=True
        ).astype(jnp.float32),
        lax.psum_scatter(
            upward_wgrad.astype(jnp.bfloat16), (SEQ, CTX), scatter_dimension=0, tiled=True
        ).astype(jnp.float32),
        lax.psum_scatter(
            down_grad.astype(jnp.bfloat16), (SEQ, CTX), scatter_dimension=1, tiled=True
        ).astype(jnp.float32),
        lax.psum_scatter(
            first_gain_grad.astype(jnp.bfloat16), (SEQ, CTX), scatter_dimension=0, tiled=True
        ).astype(jnp.float32),
        lax.psum_scatter(
            second_gain_grad.astype(jnp.bfloat16), (SEQ, CTX), scatter_dimension=0, tiled=True
        ).astype(jnp.float32),
    )
    return (
        block_output.astype(jnp.bfloat16),
        input_grad,
        scattered[0],
        scattered[1],
        scattered[2],
        scattered[3],
        scattered[4],
        scattered[5],
        scattered[6],
        scattered[7],
        scattered[8],
    )


def general_solution(mesh):
    placed = (
        P((SEQ, CTX), None),
        P((SEQ, CTX), TP),
        P((SEQ, CTX), TP),
        P((SEQ, CTX), TP),
        P(TP, (SEQ, CTX)),
        P((SEQ, CTX), TP),
        P((SEQ, CTX), TP),
        P(TP, (SEQ, CTX)),
        P((SEQ, CTX)),
        P((SEQ, CTX)),
        P(),
        P((SEQ, CTX), None),
    )
    return jax.shard_map(
        general_device,
        mesh=mesh,
        in_specs=placed,
        out_specs=(
            P((SEQ, CTX), None),
            P((SEQ, CTX), None),
            P((SEQ, CTX), TP),
            P((SEQ, CTX), TP),
            P((SEQ, CTX), TP),
            P(TP, (SEQ, CTX)),
            P((SEQ, CTX), TP),
            P((SEQ, CTX), TP),
            P(TP, (SEQ, CTX)),
            P((SEQ, CTX)),
            P((SEQ, CTX)),
        ),
        check_vma=False,
    )


LOW = jnp.bfloat16


def swap(value, axis, mask=1):
    pairs = [(i, i ^ mask) for i in range(lax.axis_size(axis))]
    return lax.ppermute(value, axis, pairs)


def tie(*values):
    return lax.optimization_barrier(values)


def in_main(value):
    return pltpu.with_memory_space_constraint(value, pltpu.HBM)


def stack_rows(pieces, local=None, places=None):
    pieces = list(pieces)
    own = [i for i, piece in enumerate(pieces) if piece is None]
    given = [piece for piece in pieces if piece is not None]
    like = given[0]
    total, count = len(pieces), like.shape[0]
    shape = jax.ShapeDtypeStruct((total * count, like.shape[1]), like.dtype)

    def kernel(*refs):
        at_ref, *refs = refs
        *ins, out, sems = refs
        source = iter(ins)
        copies = []
        for i in range(total):
            if i in own:
                first = pl.multiple_of(at_ref[own.index(i)] * count, count)
                block = ins[-1].at[pl.ds(first, count)]
            else:
                block = next(source)
            copies.append(
                pltpu.make_async_copy(block, out.at[pl.ds(i * count, count)], sems.at[i])
            )
        for copy in copies:
            copy.start()
        for copy in copies:
            copy.wait()

    operands = given + ([local] if own else [])
    at = places if own else jnp.zeros((1,), jnp.int32)
    size = shape.size * shape.dtype.itemsize
    return pl.pallas_call(
        kernel,
        out_shape=shape,
        in_specs=[pl.BlockSpec(memory_space=pltpu.SMEM)]
        + [pl.BlockSpec(memory_space=pltpu.HBM)] * len(operands),
        out_specs=pl.BlockSpec(memory_space=pltpu.VMEM),
        scratch_shapes=[pltpu.SemaphoreType.DMA((total,))],
        cost_estimate=pl.CostEstimate(flops=0, transcendentals=0, bytes_accessed=2 * size),
    )(at.astype(jnp.int32), *(in_main(operand) for operand in operands))


def first_pieces(query, key, value, gain_one, gain_two):
    depth, width = query.shape[0], query.shape[1] // 4
    f32 = jnp.float32

    def kernel(q_ref, k_ref, v_ref, one_ref, two_ref, out_ref):
        line = lax.broadcasted_iota(jnp.int32, (16, depth), 0)
        one, two = (
            jnp.broadcast_to(ref[...].astype(f32)[None], (16, depth)) for ref in (one_ref, two_ref)
        )
        gains = jnp.where(line == 0, one, jnp.where(line == 1, two, 0.0)).astype(LOW)
        for j in range(4):
            for i, ref in enumerate((q_ref, k_ref, v_ref)):
                out_ref[j, :depth, i * width : (i + 1) * width] = ref[:, j * width : (j + 1) * width]
            out_ref[j, depth:, :depth] = gains
            out_ref[j, depth:, depth:] = jnp.zeros((16, 3 * width - depth), LOW)

    whole = pl.BlockSpec(memory_space=pltpu.VMEM)
    size = 4 * (depth + 16) * 3 * width
    return pl.pallas_call(
        kernel,
        out_shape=jax.ShapeDtypeStruct((4, depth + 16, 3 * width), LOW),
        in_specs=[whole] * 5,
        out_specs=whole,
        cost_estimate=pl.CostEstimate(flops=0, transcendentals=0, bytes_accessed=4 * size),
    )(query, key, value, gain_one, gain_two)


def feed_forward(pieces, cotangent, gates, ups, downs):
    rows, features = cotangent.shape
    unit, count, steps = gates[0].shape[1], pieces[0].shape[0], 4
    part = features // 2
    block, group = rows // steps, len(pieces) // steps
    f32 = jnp.float32

    def kernel(*refs):
        ins, refs = refs[: len(pieces)], refs[len(pieces) :]
        cot_ref, *weights = refs[:7]
        gate_refs, up_refs, down_refs = weights[:2], weights[2:4], weights[4:]
        rows_ref, hidden_ref, gate_grad_ref, up_grad_ref, held, sems = refs[7:]
        step = pl.program_id(0)

        def copy(i):
            return pltpu.make_async_copy(ins[i], held.at[pl.ds(i * count, count)], sems.at[i])

        for at in range(steps):

            @pl.when(step == at)
            def _(at=at):
                if at == 0:
                    for i in range(len(pieces)):
                        copy(i).start()
                for i in range(at * group, (at + 1) * group):
                    copy(i).wait()

        values = held[pl.ds(pl.multiple_of(step * block, block), block), :]
        rows_ref[...] = values
        gate, up = (
            product(values[:, :part], first[...]) + product(values[:, part:], second[...])
            for first, second in (gate_refs, up_refs)
        )
        cot = cot_ref[...]
        hidden_grad = product(cot[:, :part], down_refs[0][...])
        hidden_grad += product(cot[:, part:], down_refs[1][...])
        sigmoid = 1.0 / (1.0 + jnp.exp(-gate))
        silu = gate * sigmoid
        hidden_ref[...] = (silu * up).astype(LOW)
        slope = sigmoid * (1.0 + gate * (1.0 - sigmoid))
        gate_grad_ref[...] = (hidden_grad * up * slope).astype(LOW)
        up_grad_ref[...] = (hidden_grad * silu).astype(LOW)

    wide = pl.BlockSpec((block, features), lambda i: (i, 0))
    narrow = pl.BlockSpec((block, unit), lambda i: (i, 0))
    once = pl.Buffered(1)
    half = pl.BlockSpec((part, unit), lambda i: (0, 0), pipeline_mode=once)
    return pl.pallas_call(
        kernel,
        grid=(steps,),
        out_shape=[jax.ShapeDtypeStruct((rows, features), LOW)]
        + [jax.ShapeDtypeStruct((rows, unit), LOW)] * 3,
        in_specs=[pl.BlockSpec(memory_space=pltpu.HBM)] * len(pieces)
        + [wide, half, half, half, half, half, half],
        out_specs=[wide, narrow, narrow, narrow],
        scratch_shapes=[
            pltpu.VMEM((rows, features), LOW),
            pltpu.SemaphoreType.DMA((len(pieces),)),
        ],
        compiler_params=pltpu.CompilerParams(
            dimension_semantics=("arbitrary",), vmem_limit_bytes=32 << 20
        ),
        cost_estimate=pl.CostEstimate(
            flops=6 * rows * features * unit,
            transcendentals=rows * unit,
            bytes_accessed=6 * rows * features + 6 * features * unit + 6 * rows * unit,
        ),
    )(*(in_main(piece) for piece in pieces), cotangent, *gates, *ups, *downs)


def swapped(values):
    lane = lax.broadcasted_iota(jnp.int32, values.shape, 1)
    size = values.shape[1]
    back, forth = pltpu.roll(values, size - HD // 2, 1), pltpu.roll(values, HD // 2, 1)
    return jnp.where(lane % HD < HD // 2, back, forth)


def of_heads(parts, shape):
    lane = lax.broadcasted_iota(jnp.int32, shape, 1)
    result = parts[0]
    for index in range(1, len(parts)):
        result = jnp.where(lane // HD == index, parts[index], result)
    return result


def only_head(values, index):
    lane = lax.broadcasted_iota(jnp.int32, values.shape, 1)
    return jnp.where(lane // HD == index, values, jnp.zeros_like(values))


def attention(pieces, tokens, token_places, own, other, cosine, sine, column, line):
    total_width, features = own.shape[2], tokens.shape[1]
    width, depth, steps = total_width // 3, own.shape[1] - 16, 4
    given = [piece for piece in pieces if piece is not None]
    count = given[0].shape[0]
    rows = count * len(pieces)
    block, group = rows // steps, len(pieces) // steps
    f32 = jnp.float32

    def kernel(at_ref, *refs):
        ins, tokens_ref, refs = refs[: len(given)], refs[len(given)], refs[len(given) + 1 :]
        own_ref, other_ref, cos_ref, sin_ref, col_ref, line_ref = refs[:6]
        normed_ref, q_ref, k_ref, v_ref, mixed_ref, numerator_ref, total_ref = refs[6:13]
        held, w_ref, gain_ref, sems = refs[13:]
        step = pl.program_id(0)

        def copy(i):
            before = sum(piece is not None for piece in pieces[:i])
            if pieces[i] is not None:
                source = ins[before]
            else:
                first = pl.multiple_of(at_ref[i - before] * count, count)
                source = tokens_ref.at[pl.ds(first, count)]
            return pltpu.make_async_copy(source, held.at[pl.ds(i * count, count)], sems.at[i])

        for at in range(steps):

            @pl.when(step == at)
            def _(at=at):
                if at == 0:
                    for i in range(len(pieces)):
                        copy(i).start()
                    for i in range(8):
                        ref, j = (own_ref, other_ref)[i // 4], i % 4
                        w_ref[i * depth : (i + 1) * depth, :] = ref[j, :depth, :]
                        gain_ref[:, i * depth : (i + 1) * depth] = ref[j, depth:, :depth].astype(f32)[:8]
                for i in range(at * group, (at + 1) * group):
                    copy(i).wait()

        @pl.when(step < steps)
        def _():
            at = pl.ds(pl.multiple_of(step * block, block), block)
            values = held[at, :].astype(f32)
            scale = lax.rsqrt(jnp.mean(values * values, axis=1, keepdims=True) + EPS)
            normed = (values * scale * gain_ref[0:1, :]).astype(LOW)
            normed_ref[...] = normed
            projected = product(normed, w_ref[...])
            cos, sin = cos_ref[at, :], sin_ref[at, :]
            for i, ref in enumerate((q_ref, k_ref)):
                u = projected[:, i * width : (i + 1) * width]
                ref[at, :] = (u * cos + swapped(u) * sin).astype(LOW)
            v_ref[at, :] = projected[:, 2 * width :].astype(LOW)

        @pl.when(step >= steps)
        def _():
            at = pl.ds(pl.multiple_of((step - steps) * block, block), block)
            allowed = col_ref[...] >= line_ref[...]
            queries, keys, values = q_ref[at, :] * 0.125, k_ref[...], v_ref[...]
            numerators, totals = [], []
            for index in range(width // HD):
                scores = contract_cols(only_head(queries, index), keys)
                weights = jnp.where(allowed, jnp.exp(scores), 0.0)
                totals.append(jnp.sum(weights, axis=1, keepdims=True))
                numerators.append(product(weights.astype(LOW), values))
            numerator = of_heads(numerators, (block, width))
            total = of_heads(totals, (block, width))
            numerator_ref[...] = numerator
            total_ref[...] = total
            mixed_ref[...] = (numerator / total).astype(LOW)

    early = lambda i: (jnp.minimum(i, steps - 1), 0)
    late = lambda i: (jnp.maximum(i - steps, 0), 0)
    once = dict(pipeline_mode=pl.Buffered(1))

    def still(shape):
        return pl.BlockSpec(shape, lambda i: (0,) * len(shape), **once)

    full = pl.BlockSpec((rows, width), lambda i: (0, 0))
    late_block = pl.BlockSpec((block, width), late)
    in_hbm = pl.BlockSpec(memory_space=pltpu.HBM)
    return pl.pallas_call(
        kernel,
        grid=(2 * steps,),
        out_shape=[pltpu.HBM((rows, features), LOW)]
        + [pltpu.HBM((rows, width), LOW)] * 4
        + [pltpu.HBM((rows, width), f32)] * 2,
        in_specs=[pl.BlockSpec(memory_space=pltpu.SMEM)]
        + [in_hbm] * (len(given) + 1)
        + [
            still(own.shape),
            still(other.shape),
            still((rows, width)),
            still((rows, width)),
            pl.BlockSpec((block, 1), late),
            still((1, rows)),
        ],
        out_specs=[pl.BlockSpec((block, features), early)]
        + [full] * 3
        + [late_block] * 3,
        scratch_shapes=[
            pltpu.VMEM((rows, features), LOW),
            pltpu.VMEM((features, total_width), LOW),
            pltpu.VMEM((8, features), f32),
            pltpu.SemaphoreType.DMA((len(pieces),)),
        ],
        compiler_params=pltpu.CompilerParams(
            dimension_semantics=("arbitrary",), vmem_limit_bytes=40 << 20
        ),
        cost_estimate=pl.CostEstimate(
            flops=2 * rows * features * total_width + 8 * rows * rows * width,
            transcendentals=2 * rows * rows,
            bytes_accessed=4 * rows * features + 4 * features * total_width + 20 * rows * width,
        ),
    )(token_places, *(in_main(a) for a in (*given, tokens)), own, other, *(in_main(a) for a in (cosine, sine, column, line)))


def project(mixed, outs):
    rows, width = mixed.shape
    depth, block = outs[0].shape[2], rows // 4

    def kernel(mixed_ref, own_ref, other_ref, *refs):
        for i, ref in enumerate(refs):
            values = mixed_ref[i * block : (i + 1) * block, :]
            for j in range(8):
                weight = (own_ref, other_ref)[j // 4][j % 4]
                ref[:, j * depth : (j + 1) * depth] = product(values, weight).astype(LOW)

    whole = pl.BlockSpec(memory_space=pltpu.VMEM)
    return pl.pallas_call(
        kernel,
        out_shape=[jax.ShapeDtypeStruct((block, 8 * depth), LOW)] * 4,
        in_specs=[whole] * 3,
        out_specs=[whole] * 4,
        cost_estimate=pl.CostEstimate(
            flops=16 * rows * width * depth, transcendentals=0, bytes_accessed=20 * rows * depth
        ),
    )(mixed, *outs)


def attention_back(pieces, output, queries, keys, values, mixed, numerator, total, *places):
    rows, width = queries.shape
    features, count, steps = output.shape[1], pieces[0].shape[0], 4
    block, group = rows // steps, len(pieces) // steps
    cosine, sine, column, line = places
    f32 = jnp.float32

    def kernel(*refs):
        ins, refs = refs[: len(pieces)], refs[len(pieces) :]
        w_ref, q_ref, k_ref, v_ref, mixed_ref, num_ref, total_ref, *refs = refs
        cos_ref, sin_ref, col_ref, line_ref, grad_ref, keep_ref, give_ref, *refs = refs
        held, key_sum, value_sum, output_sum, sems = refs
        step = pl.program_id(0)

        def copy(i):
            return pltpu.make_async_copy(ins[i], held.at[pl.ds(i * count, count)], sems.at[i])

        for at in range(steps):

            @pl.when(step == at)
            def _(at=at):
                if at == 0:
                    for i in range(len(pieces)):
                        copy(i).start()
                    key_sum[...] = jnp.zeros_like(key_sum)
                    value_sum[...] = jnp.zeros_like(value_sum)
                    output_sum[...] = jnp.zeros_like(output_sum)
                for i in range(at * group, (at + 1) * group):
                    copy(i).wait()

        at = pl.ds(pl.multiple_of(step * block, block), block)
        branch = held[at, :]
        output_sum[...] += contract_rows(mixed_ref[...], branch)
        mixed_grad = contract_cols(branch, w_ref[...])
        totals = total_ref[...]
        numerator_grad = (mixed_grad / totals).astype(LOW)
        shares = mixed_grad * num_ref[...] / (totals * totals)
        allowed = col_ref[...] >= line_ref[...]
        query_parts = []
        all_keys, all_values = k_ref[...], v_ref[...]
        for index in range(width // HD):
            query = only_head(q_ref[...], index) * 0.125
            grad = only_head(numerator_grad, index)
            total_grad = -jnp.sum(only_head(shares, index), axis=1, keepdims=True)
            weights = jnp.where(allowed, jnp.exp(contract_cols(query, all_keys)), 0.0)
            through = contract_cols(grad, all_values)
            slopes = (weights * (through + total_grad)).astype(LOW)
            query_parts.append(product(slopes, all_keys))
            key_sum[...] += contract_rows(query, slopes)
            value_sum[...] += contract_rows(grad, weights.astype(LOW))
        query_grad = of_heads(query_parts, (block, width)) * 0.125

        def unturned(u, where):
            return (u * cos_ref[where, :] - swapped(u) * sin_ref[where, :]).astype(LOW)

        grad_ref[at, :width] = unturned(query_grad, at)

        @pl.when(step == steps - 1)
        def _():
            everywhere = pl.ds(0, rows)
            grad_ref[:, width : 2 * width] = unturned(key_sum[...].T, everywhere)
            grad_ref[:, 2 * width :] = value_sum[...].T.astype(LOW)
            keep_ref[...] = output_sum[:, : features // 2].T.astype(LOW)
            give_ref[...] = output_sum[:, features // 2 :].T.astype(LOW)

    def still(shape):
        return pl.BlockSpec(shape, lambda i: (0,) * len(shape), pipeline_mode=pl.Buffered(1))

    def whole(shape):
        return pl.BlockSpec(shape, lambda i: (0,) * len(shape))

    moving = pl.BlockSpec((block, width), lambda i: (i, 0))
    half = (features // 2, width)
    return pl.pallas_call(
        kernel,
        grid=(steps,),
        out_shape=[
            jax.ShapeDtypeStruct((rows, 3 * width), LOW),
            jax.ShapeDtypeStruct(half, LOW),
            jax.ShapeDtypeStruct(half, LOW),
        ],
        in_specs=[pl.BlockSpec(memory_space=pltpu.HBM)] * len(pieces)
        + [still(output.shape), moving, still((rows, width)), still((rows, width))]
        + [moving, moving, moving, still((rows, width)), still((rows, width))]
        + [pl.BlockSpec((block, 1), lambda i: (i, 0)), still((1, rows))],
        out_specs=[whole((rows, 3 * width)), whole(half), whole(half)],
        scratch_shapes=[
            pltpu.VMEM((rows, features), LOW),
            pltpu.VMEM((width, rows), f32),
            pltpu.VMEM((width, rows), f32),
            pltpu.VMEM((width, features), f32),
            pltpu.SemaphoreType.DMA((len(pieces),)),
        ],
        compiler_params=pltpu.CompilerParams(
            dimension_semantics=("arbitrary",), vmem_limit_bytes=32 << 20
        ),
        cost_estimate=pl.CostEstimate(
            flops=4 * rows * features * width + 20 * rows * rows * width,
            transcendentals=2 * rows * rows,
            bytes_accessed=2 * rows * features + 24 * rows * width,
        ),
    )(*(in_main(a) for a in (*pieces, output, queries, keys, values, mixed, numerator, total, *places)))


def turned_pieces(value):
    total, rows, columns = value.shape

    def kernel(value_ref, out_ref):
        out_ref[0] = value_ref[0].T

    size = value.size * value.dtype.itemsize
    return pl.pallas_call(
        kernel,
        grid=(total,),
        out_shape=jax.ShapeDtypeStruct((total, columns, rows), value.dtype),
        in_specs=[pl.BlockSpec((1, rows, columns), lambda i: (i, 0, 0))],
        out_specs=pl.BlockSpec((1, columns, rows), lambda i: (i, 0, 0)),
        cost_estimate=pl.CostEstimate(flops=0, transcendentals=0, bytes_accessed=2 * size),
    )(value)


def place_rows(pieces, places, dtype):
    count, features = pieces[0].shape

    def kernel(at_ref, *refs):
        for i, ref in enumerate(refs[:-1]):
            first = pl.multiple_of(at_ref[i] * count, count)
            refs[-1][pl.ds(first, count), :] = ref[...].astype(dtype)

    whole = pl.BlockSpec(memory_space=pltpu.VMEM)
    shape = jax.ShapeDtypeStruct((len(pieces) * count, features), dtype)
    return pl.pallas_call(
        kernel,
        out_shape=shape,
        in_specs=[pl.BlockSpec(memory_space=pltpu.SMEM)] + [whole] * len(pieces),
        out_specs=whole,
        cost_estimate=pl.CostEstimate(
            flops=0, transcendentals=0, bytes_accessed=6 * shape.size
        ),
    )(places, *pieces)


def both_of(one, two, start, stop):
    return one[start:stop].astype(jnp.float32) + two[start:stop].astype(jnp.float32)


class Stages:
    def step(self, *flying):
        names = [name for name in vars(self) if name not in flying]
        for name, value in zip(names, tie(*(getattr(self, name) for name in names))):
            setattr(self, name, value)

    def take(self, *names):
        values = [getattr(self, name) for name in names]
        for name in names:
            delattr(self, name)
        return values

    def scatter_0(self, p, rows, rows_of):
        setattr(self, p + "in", swap(rows_of(3), CORE))
        setattr(self, p + "keep", rows_of(1))

    def scatter_1(self, p, rows, rows_of):
        count = rows // 16
        keep, arrived = self.take(p + "keep", p + "in")
        third, middle, first = (
            both_of(keep, arrived, start * count, stop * count).astype(LOW)
            for start, stop in ((3, 4), (1, 3), (0, 1))
        )
        setattr(self, p + "third", swap(third, X))
        setattr(self, p + "middle", swap(middle, X))
        setattr(self, p + "first", first)
        setattr(self, p + "in", swap(rows_of(2), CORE))
        setattr(self, p + "keep", rows_of(0))

    def scatter_2(self, p):
        first, third = self.take(p + "first", p + "third")
        keep, arrived = getattr(self, p + "keep"), getattr(self, p + "in")
        count = first.shape[0]
        last = both_of(keep, arrived, 3 * count, 4 * count) + third.astype(jnp.float32)
        setattr(self, p + "last", swap(last.astype(LOW), CTX, 1))
        setattr(self, p + "first", swap(first, X))

    def scatter_3(self, p):
        middle, last = self.take(p + "middle", p + "last")
        keep, arrived = getattr(self, p + "keep"), getattr(self, p + "in")
        count = last.shape[0]
        far = both_of(keep, arrived, 2 * count, 3 * count) + last.astype(jnp.float32)
        far = far + middle[count:].astype(jnp.float32)
        near = both_of(keep, arrived, count, 2 * count) + middle[:count].astype(jnp.float32)
        setattr(self, p + "far", swap(far.astype(LOW), CTX, 2))
        setattr(self, p + "near", swap(near.astype(LOW), CTX, 1))

    def scatter_4(self, p):
        keep, arrived, *values = self.take(
            p + "keep", p + "in", p + "first", p + "near", p + "far"
        )
        total = both_of(keep, arrived, 0, values[0].shape[0])
        return total + sum(value.astype(jnp.float32) for value in values)

    def gather_0(self, shard):
        self.g0 = shard
        self.g1, self.g2 = swap(shard, CTX, 1), swap(shard, CTX, 2)
        self.x0, self.c0 = swap(shard, X), swap(shard, CORE)

    def gather_1(self):
        self.g3 = swap(self.g2, CTX, 1)
        self.x1, self.x2 = swap(self.g1, X), swap(self.g2, X)

    def gather_2(self):
        self.x3 = swap(self.g3, X)
        self.c1, self.c2, self.c3 = (swap(g, CORE) for g in (self.g1, self.g2, self.g3))
        self.c4 = swap(self.x0, CORE)

    def gather_3(self):
        self.c5, self.c6, self.c7 = (swap(x, CORE) for x in (self.x1, self.x2, self.x3))
        names = [k + str(j) for k in "gx" for j in range(4)] + ["c" + str(j) for j in range(8)]
        return self.take(*names)


def spread(pieces):
    return lax.all_to_all(pieces, CTX, 0, 0, tiled=True)


def side_by_side(pieces):
    return jnp.concatenate(list(pieces), axis=1)


def by_columns(weight, extent):
    return jnp.stack([weight[:, j * extent : (j + 1) * extent] for j in range(4)])


def both(own):
    return jnp.concatenate([own, swap(own, SEQ)])


def halves(left, right):
    grad = contract_rows(left, right).astype(LOW)
    half = grad.shape[0] // 2
    return grad[:half], grad[half:]


def added(keep, arrived):
    return (keep.astype(jnp.float32) + arrived.astype(jnp.float32)).astype(LOW)


def fast_device(
    tokens,
    query_weight,
    key_weight,
    value_weight,
    output_weight,
    gate_weight,
    up_weight,
    down_weight,
    attention_gain,
    feedforward_gain,
    order,
    cotangent,
):
    f32 = jnp.float32
    seq, ctx = lax.axis_index(SEQ), lax.axis_index(CTX)
    x, core = lax.axis_index(X), lax.axis_index(CORE)
    local_rows = tokens.shape[0]
    count = local_rows // 4
    rows = 16 * count
    width = query_weight.shape[1] // 4
    unit = gate_weight.shape[1] // 4
    depth = query_weight.shape[0]

    def turned(values):
        middle_column = values.shape[1] // 2
        other_way = jnp.concatenate([values[:, middle_column:], values[:, :middle_column]], axis=1)
        return jnp.where(seq == 0, values, other_way)

    own_places = jnp.stack([(x ^ a) * 2 + (core ^ b) for b in range(2) for a in range(2)])

    def local(values, a, b):
        return lax.dynamic_slice_in_dim(values, ((x ^ a) * 2 + (core ^ b)) * count, count, 0)

    features = tokens.shape[1]
    v = Stages()

    qkv_pieces = first_pieces(
        query_weight, key_weight, value_weight, attention_gain, feedforward_gain
    )
    v.qkv_own, v.tokens = tie(qkv_pieces, tokens)
    v.qkv_own = spread(v.qkv_own)
    v.tokens = turned(v.tokens)
    shard = local(v.tokens, 0, 0)
    v.g1, v.g2 = swap(shard, CTX, 1), swap(shard, CTX, 2)
    v.cotangent, v.order = cotangent, order
    v.gate, v.up, v.down, v.output = gate_weight, up_weight, down_weight, output_weight
    v.step("qkv_own")

    v.g3, v.x1, v.x2 = swap(v.g2, CTX, 1), swap(v.g1, X), swap(v.g2, X)
    v.output = v.output.reshape(4, width, depth)
    blocks = jnp.arange(16, dtype=jnp.int32)
    stored = (
        (ctx ^ (blocks & 3)) * local_rows
        + (x ^ ((blocks >> 2) & 1)) * (2 * count)
        + (core ^ (blocks >> 3)) * count
    )
    stored = (stored[:, None] + jnp.arange(count, dtype=jnp.int32)[None, :]).reshape(-1)
    slots = jnp.arange(order.shape[0], dtype=jnp.int32)
    places = jnp.sum(
        jnp.where((stored // BLOCK)[:, None] == slots[None, :], v.order[None, :], 0), axis=1
    )
    places = places * BLOCK + stored % BLOCK
    v.column, v.line = places[:, None], places[None, :]
    entry = jnp.arange(width, dtype=jnp.int32) % (HD // 2)
    inverse = THETA ** (-(entry.astype(f32) * 2.0) / HD)
    sign = jnp.where(jnp.arange(width) % HD < HD // 2, -1.0, 1.0).astype(f32)
    angle = places.astype(f32)[:, None] * inverse[None, :]
    v.cosine, v.sine = jnp.cos(angle), jnp.sin(angle) * sign[None, :]
    del v.order
    v.step("qkv_own", "x1", "x2")

    v.x3 = swap(v.g3, X)
    v.cotangent = turned(v.cotangent)
    v.shard = local(v.cotangent, 0, 0)
    v.up = by_columns(v.up, unit)
    v.step("x3")

    v.qkv_o = swap(v.qkv_own, SEQ)
    v.output = spread(v.output)
    v.down = turned_pieces(v.down.reshape(4, unit, depth))
    v.c1, v.c2, v.c3 = (swap(g, CORE) for g in (v.g1, v.g2, v.g3))
    v.c4, v.c5 = swap(v.x1, CORE), swap(v.x2, CORE)
    v.step("qkv_o")

    def whole(values, line, line_x, other, other_x):
        return stack_rows(
            [None, *line, None, *line_x, None, *other, None, *other_x], values, own_places
        )

    v.d1, v.d2 = swap(v.shard, CTX, 1), swap(v.shard, CTX, 2)
    v.gate = spread(by_columns(v.gate, unit))
    del v.shard
    v.c6 = swap(v.x3, CORE)
    v.step("gate", "d1", "d2")

    v.gain_first, v.gain_second = (
        jnp.concatenate([half[:, depth + i, :depth] for half in (v.qkv_own, v.qkv_o)])
        .reshape(1, 8 * depth)
        .astype(f32)
        for i in range(2)
    )
    g1, g2, g3, x1, x2, x3 = v.take("g1", "g2", "g3", "x1", "x2", "x3")
    c1, c2, c3, c4, c5, c6 = v.take("c1", "c2", "c3", "c4", "c5", "c6")
    outputs = attention(
        [None, g1, g2, g3, None, x1, x2, x3, None, c1, c2, c3, None, c4, c5, c6],
        v.tokens,
        own_places,
        v.qkv_own,
        v.qkv_o,
        v.cosine,
        v.sine,
        v.column,
        v.line,
    )
    v.normed, v.queries, v.keys, v.values, v.mixed, v.numerator, v.total = outputs
    v.output_other = swap(v.output, SEQ)
    v.step("gate")

    def attended(index):
        return v.take("part%d" % index)[0]

    v.e1, v.e2 = swap(v.d1, X), swap(v.d2, X)
    v.part0, v.part1, v.part2, v.part3 = project(v.mixed, [v.output, v.output_other])
    v.scatter_0("s_", rows, attended)
    v.step("e1", "e2")
    v.up = spread(v.up)
    v.gate_o = swap(v.gate, SEQ)
    v.scatter_1("s_", rows, attended)
    v.d3 = swap(v.d2, CTX, 1)
    v.f1, v.f2 = swap(v.d1, CORE), swap(v.d2, CORE)
    v.step("up", "gate_o", "d3", "s_middle")
    v.scatter_2("s_")
    v.step("s_first")
    v.scatter_3("s_")
    v.up_o = swap(v.up, SEQ)
    v.e3, v.f3 = swap(v.d3, X), swap(v.d3, CORE)
    v.step("up_o", "e3")
    v.down = spread(v.down)
    v.middle = local(v.tokens, 0, 0).astype(f32) + v.scatter_4("s_")
    v.scale_second = lax.rsqrt(jnp.mean(v.middle * v.middle, axis=1, keepdims=True) + EPS)
    v.gather_0((v.middle * v.scale_second * v.gain_second).astype(LOW))
    v.f4, v.f5, v.f6 = (swap(e, CORE) for e in (v.e1, v.e2, v.e3))
    v.step("x0", "up_o")
    v.gather_1()
    v.down_o = swap(v.down, SEQ)
    d1, d2, d3, e1, e2, e3 = v.take("d1", "d2", "d3", "e1", "e2", "e3")
    f1, f2, f3, f4, f5, f6 = v.take("f1", "f2", "f3", "f4", "f5", "f6")
    v.every_cotangent = whole(v.cotangent, [d1, d2, d3], [e1, e2, e3], [f1, f2, f3], [f4, f5, f6])
    v.step("x1", "x2", "down_o")
    v.gather_2()
    v.output_full = side_by_side(jnp.concatenate(v.take("output", "output_other")))
    v.gate_full = jnp.concatenate([v.gate, v.gate_o]).reshape(8 * depth, unit)
    v.up_full = jnp.concatenate([v.up, v.up_o]).reshape(8 * depth, unit)
    v.step("down_o")
    pieces = v.gather_3()
    for i, piece in enumerate(pieces):
        setattr(v, "piece%d" % i, piece)
    v.step()

    v.normed_two, v.hidden, v.gate_grad, v.up_grad = feed_forward(
        v.take(*("piece%d" % i for i in range(16))),
        v.every_cotangent,
        [own.reshape(4 * depth, unit) for own in v.take("gate", "gate_o")],
        [own.reshape(4 * depth, unit) for own in v.take("up", "up_o")],
        [own.reshape(4 * depth, unit) for own in (v.down, v.down_o)],
    )
    v.down_k, v.down_g = halves(v.every_cotangent, v.hidden)
    del v.every_cotangent
    v.step()

    def quarter(values, index):
        size = rows // 4
        return values[index * size : (index + 1) * size]

    def normed_grads(index):
        gate, up = quarter(v.gate_grad, index), quarter(v.up_grad, index)
        return (contract_cols(gate, v.gate_full) + contract_cols(up, v.up_full)).astype(LOW)

    v.down_g = swap(v.down_g, SEQ)
    v.scatter_0("s_", rows, normed_grads)
    v.step("down_g")
    v.scatter_1("s_", rows, normed_grads)
    v.gate_k, v.gate_g = halves(v.normed_two, v.gate_grad)
    v.step("down_g", "s_middle")
    del v.gate_full, v.up_full
    v.scatter_2("s_")
    v.gate_g = swap(v.gate_g, SEQ)
    v.up_k, v.up_g = halves(v.normed_two, v.up_grad)
    v.step("s_first", "gate_g", "down_g")
    del v.normed_two, v.gate_grad, v.up_grad
    v.scatter_3("s_")
    v.up_g = swap(v.up_g, SEQ)
    v.down_full = jnp.concatenate(v.take("down", "down_o")).reshape(8 * depth, unit)
    v.step("gate_g", "up_g")
    normed_two_grad = v.scatter_4("s_")
    middle, scale_second = v.middle, v.scale_second
    scaled = normed_two_grad * v.gain_second
    v.middle_grad = (
        local(v.cotangent, 0, 0).astype(f32)
        + scale_second * scaled
        - middle * scale_second**3 * jnp.mean(scaled * middle, axis=1, keepdims=True)
    )
    del v.cotangent, v.scale_second, v.gain_second
    v.gather_0(v.middle_grad.astype(LOW))
    v.qkv_full = jnp.concatenate([v.qkv_own, v.qkv_o])[:, :depth].reshape(8 * depth, 3 * width)
    del v.qkv_own, v.qkv_o
    v.step("gate_g", "up_g", "x0")
    v.gather_1()
    v.step("up_g", "x1", "x2")

    def fed(index):
        return contract_cols(quarter(v.hidden, index), v.down_full).astype(LOW)

    def projected_grads(index):
        return contract_cols(quarter(v.projected_grad, index), v.qkv_full).astype(LOW)

    v.gather_2()
    v.down = spread(added(*v.take("down_k", "down_g")).reshape(4, depth, unit))
    v.gate_sum = added(*v.take("gate_k", "gate_g")).reshape(4, depth, unit)
    v.step("down", "up_g")
    pieces = v.gather_3()
    for i, piece in enumerate(pieces):
        setattr(v, "piece%d" % i, piece)
    v.step()

    v.gate = spread(v.take("gate_sum")[0])
    v.projected_grad, v.out_k, v.out_g = attention_back(
        v.take(*("piece%d" % i for i in range(16))),
        *v.take("output_full", "queries", "keys", "values", "mixed", "numerator", "total"),
        *v.take("cosine", "sine", "column", "line"),
    )
    v.step("gate")
    v.out_g = swap(v.out_g, SEQ)
    v.scatter_0("s_", rows, projected_grads)
    v.step("out_g")
    v.scatter_1("s_", rows, projected_grads)
    v.scatter_0("p_", rows, fed)
    v.step("out_g", "s_middle")
    v.scatter_2("s_")
    v.up = spread(added(*v.take("up_k", "up_g")).reshape(4, depth, unit))
    v.qkv_k, v.qkv_g = halves(v.normed, v.projected_grad)
    del v.projected_grad, v.qkv_full, v.normed
    v.scatter_1("p_", rows, fed)
    v.step("up", "s_first", "p_middle")
    del v.hidden, v.down_full
    v.scatter_3("s_")
    v.qkv_g = swap(v.qkv_g, SEQ)
    v.scatter_2("p_")
    v.down_wgrad = v.take("down")[0].transpose(0, 2, 1).reshape(4 * unit, depth).astype(f32)
    v.step("p_first", "qkv_g")
    v.scatter_3("p_")
    sums = [added(*v.take(kind + "_k", kind + "_g")) for kind in ("qkv", "out")]
    v.qkv_sum = jnp.concatenate(sums, axis=1).reshape(4, depth, 4 * width)
    own_input = local(v.tokens, 0, 0).astype(f32)
    normed_grad = v.scatter_4("s_")
    scale_own = lax.rsqrt(jnp.mean(own_input * own_input, axis=1, keepdims=True) + EPS)
    scaled = normed_grad * v.gain_first
    input_grad = (
        v.middle_grad
        + scale_own * scaled
        - own_input * scale_own**3 * jnp.mean(scaled * own_input, axis=1, keepdims=True)
    )
    v.input_grad = turned(input_grad.astype(LOW))
    v.step()
    v.qkv = spread(v.take("qkv_sum")[0])
    v.produced = turned((v.take("middle")[0] + v.scatter_4("p_")).astype(LOW))
    v.input_x, v.input_core = swap(v.input_grad, X), swap(v.input_grad, CORE)
    v.produced_x, v.produced_core = swap(v.produced, X), swap(v.produced, CORE)
    v.gate_wgrad = side_by_side(v.take("gate")[0]).astype(f32)
    v.up_wgrad = side_by_side(v.take("up")[0]).astype(f32)
    v.step("qkv")
    v.input_far = swap(v.input_x, CORE)
    v.produced_far = swap(v.produced_x, CORE)
    v.step("qkv")
    input_pieces = v.take("input_grad", "input_x", "input_core", "input_far")
    v.input_out = place_rows(input_pieces, own_places, f32)
    produced_pieces = v.take("produced", "produced_x", "produced_core", "produced_far")
    v.block_output = place_rows(produced_pieces, own_places, LOW)
    v.step()
    block_output, input_grad = v.block_output, v.input_out
    qkv_pieces, output_pieces = v.qkv[:, :, : 3 * width], v.qkv[:, :, 3 * width :]

    query_wgrad, key_wgrad, value_wgrad = (
        side_by_side(qkv_pieces[:, :, first : first + width]).astype(f32)
        for first in (0, width, 2 * width)
    )
    gate_wgrad, up_wgrad = v.gate_wgrad, v.up_wgrad

    def gain_grad(gain, *pairs):
        part = sum(jnp.sum(w.astype(f32) * g, axis=1) for w, g in pairs)
        return part / gain.astype(f32)

    gain_grads = jnp.stack(
        [
            gain_grad(
                attention_gain,
                (query_weight, query_wgrad),
                (key_weight, key_wgrad),
                (value_weight, value_wgrad),
            ),
            gain_grad(feedforward_gain, (gate_weight, gate_wgrad), (up_weight, up_wgrad)),
        ]
    )
    gain_grads = gain_grads + swap(gain_grads, CORE)
    gain_grads = gain_grads + swap(gain_grads, X)
    return (
        block_output,
        input_grad,
        query_wgrad,
        key_wgrad,
        value_wgrad,
        output_pieces.transpose(0, 2, 1).reshape(4 * width, depth).astype(f32),
        gate_wgrad,
        up_wgrad,
        v.down_wgrad,
        gain_grads[0],
        gain_grads[1],
    )


def fast_solution(mesh):
    sizes = mesh.shape
    lines = Mesh(
        mesh.devices.reshape(sizes[SEQ], sizes[CTX], 2, 2), (SEQ, CTX, X, CORE)
    )
    rows, heads = (SEQ, CTX), (X, CORE)
    wide, tall = P(rows, heads), P(heads, rows)
    return jax.shard_map(
        fast_device,
        mesh=lines,
        in_specs=(
            P(rows, None),
            wide,
            wide,
            wide,
            tall,
            wide,
            wide,
            tall,
            P(rows),
            P(rows),
            P(),
            P(rows, None),
        ),
        out_specs=(
            P(rows, None),
            P(rows, None),
            wide,
            wide,
            wide,
            tall,
            wide,
            wide,
            tall,
            P(rows),
            P(rows),
        ),
        check_vma=False,
    )


def solution(mesh):
    sizes = mesh.shape
    if mesh.axis_names == (SEQ, CTX, TP) and tuple(sizes.values()) == (2, 4, 4):
        return fast_solution(mesh)
    return general_solution(mesh)
```

```python
from functools import partial

import jax
import jax.numpy as jnp
from jax import lax
from jax.experimental import pallas as pl
from jax.experimental.pallas import tpu as pltpu
from jax.sharding import Mesh, PartitionSpec as P

HD = 64
SEQ, CTX, TP, X, CORE = ("seq", "ctx", "tp", "x", "core")
BLOCK = 128


THETA = 130000.0
EPS = 1e-05


def shifted(block, axis, distance):
    devices = range(lax.axis_size(axis))
    route = [((i - distance) % len(devices), i) for i in devices]
    return lax.ppermute(block, axis, route)


def rms_norm(hidden, gain):
    return hidden * lax.rsqrt(jnp.mean(hidden * hidden, axis=-1, keepdims=True) + EPS) * gain


def rotary(values, places):
    row_count = values.shape[0]
    by_heads = values.reshape(row_count, -1, HD)
    halfway = HD // 2
    inverse = THETA ** (-(jnp.arange(halfway, dtype=jnp.float32) * 2.0) / HD)
    angle = places.astype(jnp.float32)[:, None] * inverse[None, :]
    angle = jnp.concatenate([angle, angle], axis=1)
    cosine = jnp.cos(angle)[:, None, :]
    sine = jnp.sin(angle)[:, None, :]
    turned = jnp.concatenate([-by_heads[..., halfway:], by_heads[..., :halfway]], axis=-1)
    return (by_heads * cosine + turned * sine).reshape(row_count, -1)


def gated(gate, upward):
    return jax.nn.silu(gate) * upward


def product(left, right):
    return jnp.dot(left, right, preferred_element_type=jnp.float32)


def contract_rows(left, right):
    return lax.dot_general(
        left, right, (((0,), (0,)), ((), ())), preferred_element_type=jnp.float32
    )


def contract_cols(left, right):
    return lax.dot_general(
        left, right, (((1,), (1,)), ((), ())), preferred_element_type=jnp.float32
    )


def key_places(order, first_row, row_total):
    stored = first_row + jnp.arange(row_total, dtype=jnp.int32)
    group_slot = stored // BLOCK
    slot_table = jnp.arange(order.shape[0], dtype=jnp.int32)
    block_place = jnp.sum(
        jnp.where(group_slot[:, None] == slot_table[None, :], order[None, :], 0), axis=1
    )
    return block_place * BLOCK + stored % BLOCK


def exp_scores(query_heads, query_places, key_rows, key_pos):
    row_total = key_rows.shape[0]
    key_heads = key_rows.reshape(row_total, -1, HD)
    scores = (
        jnp.einsum("qhd,khd->hqk", query_heads, key_heads, preferred_element_type=jnp.float32)
        * 0.125
    )
    allowed = query_places[:, None] >= key_pos[None, :]
    return (jnp.where(allowed[None], jnp.exp(scores), 0.0), key_heads)


def general_device(
    tokens,
    query_weight,
    key_weight,
    value_weight,
    output_weight,
    gate_weight,
    up_weight,
    down_weight,
    attention_gain,
    feedforward_gain,
    order,
    cotangent,
):
    rows_local = tokens.shape[0]
    ctx_index = lax.axis_index(CTX)
    ctx_total = lax.axis_size(CTX)
    gathered = (
        lax.all_gather(query_weight, (SEQ, CTX), axis=0, tiled=True),
        lax.all_gather(key_weight, (SEQ, CTX), axis=0, tiled=True),
        lax.all_gather(value_weight, (SEQ, CTX), axis=0, tiled=True),
        lax.all_gather(output_weight, (SEQ, CTX), axis=1, tiled=True),
        lax.all_gather(gate_weight, (SEQ, CTX), axis=0, tiled=True),
        lax.all_gather(up_weight, (SEQ, CTX), axis=0, tiled=True),
        lax.all_gather(down_weight, (SEQ, CTX), axis=1, tiled=True),
        lax.all_gather(attention_gain, (SEQ, CTX), axis=0, tiled=True),
        lax.all_gather(feedforward_gain, (SEQ, CTX), axis=0, tiled=True),
    )
    (
        full_query,
        full_key,
        full_value,
        full_output,
        full_gate,
        full_up,
        full_down,
        gain_first,
        gain_second,
    ) = gathered
    inputs = tokens.astype(jnp.float32)
    query_places = key_places(order, ctx_index * rows_local, rows_local)
    normed_value, norm_back_first = jax.vjp(rms_norm, inputs, gain_first.astype(jnp.float32))
    normed = normed_value.astype(jnp.bfloat16)
    rope_here = partial(rotary, places=query_places)
    query_rot, query_back = jax.vjp(rope_here, product(normed, full_query))
    key_rot, key_back = jax.vjp(rope_here, product(normed, full_key))
    value_rows = product(normed, full_value).astype(jnp.bfloat16)
    query_rows = query_rot.astype(jnp.bfloat16)
    key_rows = key_rot.astype(jnp.bfloat16)
    width = query_rows.shape[1]
    head_count = width // HD
    query_heads = query_rows.reshape(rows_local, head_count, HD)
    packed = jnp.stack([key_rows, value_rows])
    empty_totals = jnp.zeros((rows_local, head_count), jnp.float32)
    empty_numerator = jnp.zeros((rows_local, width), jnp.float32)
    arrived = lax.all_gather(packed, CTX, axis=1, tiled=True)
    row_total = arrived.shape[1]

    def one_block(block_index, partial_state):
        first_row = block_index * rows_local
        section = lax.dynamic_slice_in_dim(arrived, first_row, rows_local, 1)
        key_pos = key_places(order, first_row, rows_local)
        weights, key_heads = exp_scores(query_heads, query_places, section[0], key_pos)
        value_heads = section[1].reshape(rows_local, -1, HD)
        totals, numerator = partial_state
        totals = totals + jnp.sum(weights, axis=2).T
        numerator = numerator + jnp.einsum(
            "hqk,khd->qhd",
            weights.astype(jnp.bfloat16),
            value_heads,
            preferred_element_type=jnp.float32,
        ).reshape(rows_local, width)
        return (totals, numerator)

    totals, numerator = lax.fori_loop(
        0, row_total // rows_local, one_block, (empty_totals, empty_numerator)
    )
    numerator_heads = numerator.reshape(rows_local, head_count, HD)
    mixed = (numerator_heads / totals[:, :, None]).astype(jnp.bfloat16).reshape(rows_local, width)
    middle = inputs + lax.psum(product(mixed, full_output), TP)
    normed_two_value, norm_back_second = jax.vjp(rms_norm, middle, gain_second.astype(jnp.float32))
    normed_two = normed_two_value.astype(jnp.bfloat16)
    activated, gated_back = jax.vjp(
        gated, product(normed_two, full_gate), product(normed_two, full_up)
    )
    hidden = activated.astype(jnp.bfloat16)
    block_output = middle + lax.psum(product(hidden, full_down).astype(jnp.bfloat16), TP).astype(
        jnp.float32
    )
    back_weights = (
        lax.all_gather(query_weight, (SEQ, CTX), axis=0, tiled=True),
        lax.all_gather(key_weight, (SEQ, CTX), axis=0, tiled=True),
        lax.all_gather(value_weight, (SEQ, CTX), axis=0, tiled=True),
        lax.all_gather(output_weight, (SEQ, CTX), axis=1, tiled=True),
        lax.all_gather(gate_weight, (SEQ, CTX), axis=0, tiled=True),
        lax.all_gather(up_weight, (SEQ, CTX), axis=0, tiled=True),
        lax.all_gather(down_weight, (SEQ, CTX), axis=1, tiled=True),
        lax.all_gather(attention_gain, (SEQ, CTX), axis=0, tiled=True),
        lax.all_gather(feedforward_gain, (SEQ, CTX), axis=0, tiled=True),
    )
    (
        back_query,
        back_key,
        back_value,
        back_output,
        back_gate,
        back_up,
        back_down,
        gain_unused,
        gain_spare,
    ) = back_weights
    down_grad = contract_rows(hidden, cotangent)
    hidden_grad = contract_cols(cotangent, back_down)
    gate_grad, upward_grad = gated_back(hidden_grad)
    gate_grad = gate_grad.astype(jnp.bfloat16)
    upward_grad = upward_grad.astype(jnp.bfloat16)
    gate_wgrad = contract_rows(normed_two, gate_grad)
    upward_wgrad = contract_rows(normed_two, upward_grad)
    normed_two_grad = lax.psum(
        contract_cols(gate_grad, back_gate) + contract_cols(upward_grad, back_up), TP
    )
    middle_norm_grad, second_gain_grad = norm_back_second(normed_two_grad)
    middle_grad = cotangent.astype(jnp.float32) + middle_norm_grad
    branch_grad = middle_grad.astype(jnp.bfloat16)
    output_wgrad = contract_rows(mixed, branch_grad)
    mixed_grad = contract_cols(branch_grad, back_output).reshape(rows_local, head_count, HD)
    numerator_grad = (mixed_grad / totals[:, :, None]).astype(jnp.bfloat16)
    totals_grad = -jnp.sum(mixed_grad * numerator_heads, axis=2) / (totals * totals)
    totals_grad_heads = totals_grad.T[:, :, None]

    def visit(turn_index, state):
        visiting, carried, query_acc = state
        source = (ctx_index - turn_index) % ctx_total
        key_pos = key_places(order, source * rows_local, rows_local)
        weights, key_heads = exp_scores(query_heads, query_places, visiting[0], key_pos)
        value_heads = visiting[1].reshape(rows_local, -1, HD)
        through = jnp.einsum(
            "qhd,khd->hqk", numerator_grad, value_heads, preferred_element_type=jnp.float32
        )
        slopes = (weights * (through + totals_grad_heads)).astype(jnp.bfloat16)
        query_acc = (
            query_acc
            + jnp.einsum("hqk,khd->qhd", slopes, key_heads, preferred_element_type=jnp.float32)
            * 0.125
        )
        key_term = (
            jnp.einsum("hqk,qhd->khd", slopes, query_heads, preferred_element_type=jnp.float32)
            * 0.125
        )
        value_term = jnp.einsum(
            "hqk,qhd->khd",
            weights.astype(jnp.bfloat16),
            numerator_grad,
            preferred_element_type=jnp.float32,
        )
        carried = carried + jnp.stack(
            [key_term.reshape(rows_local, width), value_term.reshape(rows_local, width)]
        )
        visiting = shifted(visiting, CTX, 1)
        carried = shifted(carried, CTX, 1)
        return (visiting, carried, query_acc)

    start_state = (
        packed,
        jnp.zeros((2, rows_local, width), jnp.float32),
        jnp.zeros((rows_local, head_count, HD), jnp.float32),
    )
    ended, key_value_grad, query_acc = lax.fori_loop(0, ctx_total, visit, start_state)
    query_proj_grad = query_back(query_acc.reshape(rows_local, width))[0].astype(jnp.bfloat16)
    key_proj_grad = key_back(key_value_grad[0])[0].astype(jnp.bfloat16)
    value_grad = key_value_grad[1].astype(jnp.bfloat16)
    query_wgrad = contract_rows(normed, query_proj_grad)
    key_wgrad = contract_rows(normed, key_proj_grad)
    value_wgrad = contract_rows(normed, value_grad)
    normed_grad = lax.psum(
        (
            contract_cols(query_proj_grad, back_query)
            + contract_cols(key_proj_grad, back_key)
            + contract_cols(value_grad, back_value)
        ).astype(jnp.bfloat16),
        TP,
    ).astype(jnp.float32)
    input_norm_grad, first_gain_grad = norm_back_first(normed_grad)
    input_grad = middle_grad + input_norm_grad
    scattered = (
        lax.psum_scatter(
            query_wgrad.astype(jnp.bfloat16), (SEQ, CTX), scatter_dimension=0, tiled=True
        ).astype(jnp.float32),
        lax.psum_scatter(
            key_wgrad.astype(jnp.bfloat16), (SEQ, CTX), scatter_dimension=0, tiled=True
        ).astype(jnp.float32),
        lax.psum_scatter(
            value_wgrad.astype(jnp.bfloat16), (SEQ, CTX), scatter_dimension=0, tiled=True
        ).astype(jnp.float32),
        lax.psum_scatter(
            output_wgrad.astype(jnp.bfloat16), (SEQ, CTX), scatter_dimension=1, tiled=True
        ).astype(jnp.float32),
        lax.psum_scatter(
            gate_wgrad.astype(jnp.bfloat16), (SEQ, CTX), scatter_dimension=0, tiled=True
        ).astype(jnp.float32),
        lax.psum_scatter(
            upward_wgrad.astype(jnp.bfloat16), (SEQ, CTX), scatter_dimension=0, tiled=True
        ).astype(jnp.float32),
        lax.psum_scatter(
            down_grad.astype(jnp.bfloat16), (SEQ, CTX), scatter_dimension=1, tiled=True
        ).astype(jnp.float32),
        lax.psum_scatter(
            first_gain_grad.astype(jnp.bfloat16), (SEQ, CTX), scatter_dimension=0, tiled=True
        ).astype(jnp.float32),
        lax.psum_scatter(
            second_gain_grad.astype(jnp.bfloat16), (SEQ, CTX), scatter_dimension=0, tiled=True
        ).astype(jnp.float32),
    )
    return (
        block_output.astype(jnp.bfloat16),
        input_grad,
        scattered[0],
        scattered[1],
        scattered[2],
        scattered[3],
        scattered[4],
        scattered[5],
        scattered[6],
        scattered[7],
        scattered[8],
    )


def general_solution(mesh):
    placed = (
        P((SEQ, CTX), None),
        P((SEQ, CTX), TP),
        P((SEQ, CTX), TP),
        P((SEQ, CTX), TP),
        P(TP, (SEQ, CTX)),
        P((SEQ, CTX), TP),
        P((SEQ, CTX), TP),
        P(TP, (SEQ, CTX)),
        P((SEQ, CTX)),
        P((SEQ, CTX)),
        P(),
        P((SEQ, CTX), None),
    )
    return jax.shard_map(
        general_device,
        mesh=mesh,
        in_specs=placed,
        out_specs=(
            P((SEQ, CTX), None),
            P((SEQ, CTX), None),
            P((SEQ, CTX), TP),
            P((SEQ, CTX), TP),
            P((SEQ, CTX), TP),
            P(TP, (SEQ, CTX)),
            P((SEQ, CTX), TP),
            P((SEQ, CTX), TP),
            P(TP, (SEQ, CTX)),
            P((SEQ, CTX)),
            P((SEQ, CTX)),
        ),
        check_vma=False,
    )


LOW = jnp.bfloat16


def swap(value, axis, mask=1):
    pairs = [(i, i ^ mask) for i in range(lax.axis_size(axis))]
    return lax.ppermute(value, axis, pairs)


def tie(*values):
    return lax.optimization_barrier(values)


def in_main(value):
    return pltpu.with_memory_space_constraint(value, pltpu.HBM)


def stack_rows(pieces, local=None, places=None):
    pieces = list(pieces)
    own = [i for i, piece in enumerate(pieces) if piece is None]
    given = [piece for piece in pieces if piece is not None]
    like = given[0]
    total, count = len(pieces), like.shape[0]
    shape = jax.ShapeDtypeStruct((total * count, like.shape[1]), like.dtype)

    def kernel(*refs):
        at_ref, *refs = refs
        *ins, out, sems = refs
        source = iter(ins)
        copies = []
        for i in range(total):
            if i in own:
                first = pl.multiple_of(at_ref[own.index(i)] * count, count)
                block = ins[-1].at[pl.ds(first, count)]
            else:
                block = next(source)
            copies.append(
                pltpu.make_async_copy(block, out.at[pl.ds(i * count, count)], sems.at[i])
            )
        for copy in copies:
            copy.start()
        for copy in copies:
            copy.wait()

    operands = given + ([local] if own else [])
    at = places if own else jnp.zeros((1,), jnp.int32)
    size = shape.size * shape.dtype.itemsize
    return pl.pallas_call(
        kernel,
        out_shape=shape,
        in_specs=[pl.BlockSpec(memory_space=pltpu.SMEM)]
        + [pl.BlockSpec(memory_space=pltpu.HBM)] * len(operands),
        out_specs=pl.BlockSpec(memory_space=pltpu.VMEM),
        scratch_shapes=[pltpu.SemaphoreType.DMA((total,))],
        cost_estimate=pl.CostEstimate(flops=0, transcendentals=0, bytes_accessed=2 * size),
    )(at.astype(jnp.int32), *(in_main(operand) for operand in operands))


def first_pieces(query, key, value, gain_one, gain_two):
    depth, width = query.shape[0], query.shape[1] // 4
    f32 = jnp.float32

    def kernel(q_ref, k_ref, v_ref, one_ref, two_ref, out_ref):
        line = lax.broadcasted_iota(jnp.int32, (16, depth), 0)
        one, two = (
            jnp.broadcast_to(ref[...].astype(f32)[None], (16, depth)) for ref in (one_ref, two_ref)
        )
        gains = jnp.where(line == 0, one, jnp.where(line == 1, two, 0.0)).astype(LOW)
        for j in range(4):
            for i, ref in enumerate((q_ref, k_ref, v_ref)):
                out_ref[j, :depth, i * width : (i + 1) * width] = ref[:, j * width : (j + 1) * width]
            out_ref[j, depth:, :depth] = gains
            out_ref[j, depth:, depth:] = jnp.zeros((16, 3 * width - depth), LOW)

    whole = pl.BlockSpec(memory_space=pltpu.VMEM)
    size = 4 * (depth + 16) * 3 * width
    return pl.pallas_call(
        kernel,
        out_shape=jax.ShapeDtypeStruct((4, depth + 16, 3 * width), LOW),
        in_specs=[whole] * 5,
        out_specs=whole,
        cost_estimate=pl.CostEstimate(flops=0, transcendentals=0, bytes_accessed=4 * size),
    )(query, key, value, gain_one, gain_two)


def feed_forward(pieces, gates, ups):
    features, count, steps = pieces[0].shape[1], pieces[0].shape[0], 4
    rows, unit, part = count * len(pieces), gates[0].shape[1], features // 2
    block, group = rows // steps, len(pieces) // steps
    f32 = jnp.float32

    def kernel(*refs):
        ins, refs = refs[: len(pieces)], refs[len(pieces) :]
        gate_refs, up_refs = refs[:2], refs[2:4]
        rows_ref, hidden_ref, gate_slope_ref, up_slope_ref, held, sems = refs[4:]
        step = pl.program_id(0)

        def copy(i):
            return pltpu.make_async_copy(ins[i], held.at[pl.ds(i * count, count)], sems.at[i])

        for at in range(steps):

            @pl.when(step == at)
            def _(at=at):
                if at == 0:
                    for i in range(len(pieces)):
                        copy(i).start()
                for i in range(at * group, (at + 1) * group):
                    copy(i).wait()

        values = held[pl.ds(pl.multiple_of(step * block, block), block), :]
        rows_ref[...] = values
        gate, up = (
            product(values[:, :part], first[...]) + product(values[:, part:], second[...])
            for first, second in (gate_refs, up_refs)
        )
        sigmoid = 1.0 / (1.0 + jnp.exp(-gate))
        silu = gate * sigmoid
        hidden_ref[...] = (silu * up).astype(LOW)
        gate_slope_ref[...] = (up * (sigmoid * (1.0 + gate * (1.0 - sigmoid)))).astype(LOW)
        up_slope_ref[...] = silu.astype(LOW)

    wide = pl.BlockSpec((block, features), lambda i: (i, 0))
    narrow = pl.BlockSpec((block, unit), lambda i: (i, 0))
    half = pl.BlockSpec((part, unit), lambda i: (0, 0), pipeline_mode=pl.Buffered(1))
    return pl.pallas_call(
        kernel,
        grid=(steps,),
        out_shape=[pltpu.HBM((rows, features), LOW), jax.ShapeDtypeStruct((rows, unit), LOW)]
        + [pltpu.HBM((rows, unit), LOW)] * 2,
        in_specs=[pl.BlockSpec(memory_space=pltpu.HBM)] * len(pieces) + [half] * 4,
        out_specs=[wide, narrow, narrow, narrow],
        scratch_shapes=[
            pltpu.VMEM((rows, features), LOW),
            pltpu.SemaphoreType.DMA((len(pieces),)),
        ],
        compiler_params=pltpu.CompilerParams(
            dimension_semantics=("arbitrary",), vmem_limit_bytes=32 << 20
        ),
        cost_estimate=pl.CostEstimate(
            flops=4 * rows * features * unit,
            transcendentals=rows * unit,
            bytes_accessed=4 * rows * features + 4 * features * unit + 10 * rows * unit,
        ),
    )(*(in_main(piece) for piece in pieces), *gates, *ups)


def feed_back(cotangent, downs, gate_slope, up_slope):
    rows, features = cotangent.shape
    unit, steps, part = gate_slope.shape[1], 4, features // 2
    block = rows // steps

    def kernel(cot_ref, *refs):
        gate_slope_ref, up_slope_ref, gate_ref, up_ref = refs[4:]
        for i in range(2):
            at = slice(i * unit // 2, (i + 1) * unit // 2)
            hidden_grad = product(cot_ref[:, :part], refs[2 * i][...])
            hidden_grad += product(cot_ref[:, part:], refs[2 * i + 1][...])
            gate_ref[:, at] = (hidden_grad * gate_slope_ref[:, at].astype(jnp.float32)).astype(LOW)
            up_ref[:, at] = (hidden_grad * up_slope_ref[:, at].astype(jnp.float32)).astype(LOW)

    wide = pl.BlockSpec((block, features), lambda i: (i, 0))
    narrow = pl.BlockSpec((block, unit), lambda i: (i, 0))
    half = pl.BlockSpec((part, unit // 2), lambda i: (0, 0), pipeline_mode=pl.Buffered(1))
    return pl.pallas_call(
        kernel,
        grid=(steps,),
        out_shape=[jax.ShapeDtypeStruct((rows, unit), LOW)] * 2,
        in_specs=[wide, half, half, half, half, narrow, narrow],
        out_specs=[narrow, narrow],
        compiler_params=pltpu.CompilerParams(dimension_semantics=("arbitrary",)),
        cost_estimate=pl.CostEstimate(
            flops=2 * rows * features * unit,
            transcendentals=0,
            bytes_accessed=2 * rows * features + 2 * features * unit + 12 * rows * unit,
        ),
    )(in_main(cotangent), *downs, gate_slope, up_slope)


def swapped(values):
    lane = lax.broadcasted_iota(jnp.int32, values.shape, 1)
    size = values.shape[1]
    back, forth = pltpu.roll(values, size - HD // 2, 1), pltpu.roll(values, HD // 2, 1)
    return jnp.where(lane % HD < HD // 2, back, forth)


def of_heads(parts, shape):
    lane = lax.broadcasted_iota(jnp.int32, shape, 1)
    result = parts[0]
    for index in range(1, len(parts)):
        result = jnp.where(lane // HD == index, parts[index], result)
    return result


def only_head(values, index):
    lane = lax.broadcasted_iota(jnp.int32, values.shape, 1)
    return jnp.where(lane // HD == index, values, jnp.zeros_like(values))


def attention(pieces, tokens, token_places, own, other, cosine, sine, column, line):
    total_width, features = own.shape[2], tokens.shape[1]
    width, depth, steps = total_width // 3, own.shape[1] - 16, 4
    given = [piece for piece in pieces if piece is not None]
    count = given[0].shape[0]
    rows = count * len(pieces)
    block, group = rows // steps, len(pieces) // steps
    f32 = jnp.float32

    def kernel(at_ref, *refs):
        ins, tokens_ref, refs = refs[: len(given)], refs[len(given)], refs[len(given) + 1 :]
        own_ref, other_ref, cos_ref, sin_ref, col_ref, line_ref = refs[:6]
        normed_ref, q_ref, k_ref, v_ref, mixed_ref, numerator_ref, total_ref = refs[6:13]
        held, w_ref, gain_ref, sems = refs[13:]
        step = pl.program_id(0)

        def copy(i):
            before = sum(piece is not None for piece in pieces[:i])
            if pieces[i] is not None:
                source = ins[before]
            else:
                first = pl.multiple_of(at_ref[i - before] * count, count)
                source = tokens_ref.at[pl.ds(first, count)]
            return pltpu.make_async_copy(source, held.at[pl.ds(i * count, count)], sems.at[i])

        for at in range(steps):

            @pl.when(step == at)
            def _(at=at):
                if at == 0:
                    for i in range(len(pieces)):
                        copy(i).start()
                    for i in range(8):
                        ref, j = (own_ref, other_ref)[i // 4], i % 4
                        w_ref[i * depth : (i + 1) * depth, :] = ref[j, :depth, :]
                        gain_ref[:, i * depth : (i + 1) * depth] = ref[j, depth:, :depth].astype(f32)[:8]
                for i in range(at * group, (at + 1) * group):
                    copy(i).wait()

        @pl.when(step < steps)
        def _():
            at = pl.ds(pl.multiple_of(step * block, block), block)
            values = held[at, :].astype(f32)
            scale = lax.rsqrt(jnp.mean(values * values, axis=1, keepdims=True) + EPS)
            normed = (values * scale * gain_ref[0:1, :]).astype(LOW)
            normed_ref[...] = normed
            projected = product(normed, w_ref[...])
            cos, sin = cos_ref[at, :], sin_ref[at, :]
            for i, ref in enumerate((q_ref, k_ref)):
                u = projected[:, i * width : (i + 1) * width]
                ref[at, :] = (u * cos + swapped(u) * sin).astype(LOW)
            v_ref[at, :] = projected[:, 2 * width :].astype(LOW)

        @pl.when(step >= steps)
        def _():
            at = pl.ds(pl.multiple_of((step - steps) * block, block), block)
            allowed = col_ref[...] >= line_ref[...]
            queries, keys, values = q_ref[at, :] * 0.125, k_ref[...], v_ref[...]
            numerators, totals = [], []
            for index in range(width // HD):
                scores = contract_cols(only_head(queries, index), keys)
                weights = jnp.where(allowed, jnp.exp(scores), 0.0)
                totals.append(jnp.sum(weights, axis=1, keepdims=True))
                numerators.append(product(weights.astype(LOW), values))
            numerator = of_heads(numerators, (block, width))
            total = of_heads(totals, (block, width))
            numerator_ref[...] = numerator
            total_ref[...] = total
            mixed_ref[...] = (numerator / total).astype(LOW)

    early = lambda i: (jnp.minimum(i, steps - 1), 0)
    late = lambda i: (jnp.maximum(i - steps, 0), 0)
    once = dict(pipeline_mode=pl.Buffered(1))

    def still(shape):
        return pl.BlockSpec(shape, lambda i: (0,) * len(shape), **once)

    full = pl.BlockSpec((rows, width), lambda i: (0, 0))
    late_block = pl.BlockSpec((block, width), late)
    in_hbm = pl.BlockSpec(memory_space=pltpu.HBM)
    return pl.pallas_call(
        kernel,
        grid=(2 * steps,),
        out_shape=[pltpu.HBM((rows, features), LOW)]
        + [pltpu.HBM((rows, width), LOW)] * 4
        + [pltpu.HBM((rows, width), f32)] * 2,
        in_specs=[pl.BlockSpec(memory_space=pltpu.SMEM)]
        + [in_hbm] * (len(given) + 1)
        + [
            still(own.shape),
            still(other.shape),
            still((rows, width)),
            still((rows, width)),
            pl.BlockSpec((block, 1), late),
            still((1, rows)),
        ],
        out_specs=[pl.BlockSpec((block, features), early)]
        + [full] * 3
        + [late_block] * 3,
        scratch_shapes=[
            pltpu.VMEM((rows, features), LOW),
            pltpu.VMEM((features, total_width), LOW),
            pltpu.VMEM((8, features), f32),
            pltpu.SemaphoreType.DMA((len(pieces),)),
        ],
        compiler_params=pltpu.CompilerParams(
            dimension_semantics=("arbitrary",), vmem_limit_bytes=40 << 20
        ),
        cost_estimate=pl.CostEstimate(
            flops=2 * rows * features * total_width + 8 * rows * rows * width,
            transcendentals=2 * rows * rows,
            bytes_accessed=4 * rows * features + 4 * features * total_width + 20 * rows * width,
        ),
    )(token_places, *(in_main(a) for a in (*given, tokens)), own, other, *(in_main(a) for a in (cosine, sine, column, line)))


def project(mixed, outs):
    rows, width = mixed.shape
    depth, block = outs[0].shape[2], rows // 4

    def kernel(mixed_ref, own_ref, other_ref, *refs):
        for i, ref in enumerate(refs):
            values = mixed_ref[i * block : (i + 1) * block, :]
            for j in range(8):
                weight = (own_ref, other_ref)[j // 4][j % 4]
                ref[:, j * depth : (j + 1) * depth] = product(values, weight).astype(LOW)

    whole = pl.BlockSpec(memory_space=pltpu.VMEM)
    return pl.pallas_call(
        kernel,
        out_shape=[jax.ShapeDtypeStruct((block, 8 * depth), LOW)] * 4,
        in_specs=[whole] * 3,
        out_specs=[whole] * 4,
        cost_estimate=pl.CostEstimate(
            flops=16 * rows * width * depth, transcendentals=0, bytes_accessed=20 * rows * depth
        ),
    )(mixed, *outs)


def attention_back(pieces, outs, queries, keys, values, mixed, numerator, total, *places):
    rows, width = queries.shape
    depth, count, steps = outs[0].shape[2], pieces[0].shape[0], 4
    features = 8 * depth
    block, group = rows // steps, len(pieces) // steps
    cosine, sine, column, line = places
    f32 = jnp.float32

    def kernel(*refs):
        ins, refs = refs[: len(pieces)], refs[len(pieces) :]
        out_refs, refs = refs[:2], refs[2:]
        q_ref, k_ref, v_ref, mixed_ref, num_ref, total_ref, *refs = refs
        cos_ref, sin_ref, col_ref, line_ref, grad_ref, keep_ref, give_ref, *refs = refs
        held, w_ref, key_sum, value_sum, output_sum, sems = refs
        step = pl.program_id(0)

        def copy(i):
            return pltpu.make_async_copy(ins[i], held.at[pl.ds(i * count, count)], sems.at[i])

        for at in range(steps):

            @pl.when(step == at)
            def _(at=at):
                if at == 0:
                    for i in range(len(pieces)):
                        copy(i).start()
                    for i in range(8):
                        w_ref[:, i * depth : (i + 1) * depth] = out_refs[i // 4][i % 4]
                    key_sum[...] = jnp.zeros_like(key_sum)
                    value_sum[...] = jnp.zeros_like(value_sum)
                    output_sum[...] = jnp.zeros_like(output_sum)
                for i in range(at * group, (at + 1) * group):
                    copy(i).wait()

        at = pl.ds(pl.multiple_of(step * block, block), block)
        branch = held[at, :]
        output_sum[...] += contract_rows(mixed_ref[...], branch)
        mixed_grad = contract_cols(branch, w_ref[...])
        totals = total_ref[...]
        numerator_grad = (mixed_grad / totals).astype(LOW)
        shares = mixed_grad * num_ref[...] / (totals * totals)
        allowed = col_ref[...] >= line_ref[...]
        query_parts = []
        all_keys, all_values = k_ref[...], v_ref[...]
        for index in range(width // HD):
            query = only_head(q_ref[...], index) * 0.125
            grad = only_head(numerator_grad, index)
            total_grad = -jnp.sum(only_head(shares, index), axis=1, keepdims=True)
            weights = jnp.where(allowed, jnp.exp(contract_cols(query, all_keys)), 0.0)
            through = contract_cols(grad, all_values)
            slopes = (weights * (through + total_grad)).astype(LOW)
            query_parts.append(product(slopes, all_keys))
            key_sum[...] += contract_rows(query, slopes)
            value_sum[...] += contract_rows(grad, weights.astype(LOW))
        query_grad = of_heads(query_parts, (block, width)) * 0.125

        def unturned(u, where):
            return (u * cos_ref[where, :] - swapped(u) * sin_ref[where, :]).astype(LOW)

        grad_ref[at, :width] = unturned(query_grad, at)

        @pl.when(step == steps - 1)
        def _():
            everywhere = pl.ds(0, rows)
            grad_ref[:, width : 2 * width] = unturned(key_sum[...].T, everywhere)
            grad_ref[:, 2 * width :] = value_sum[...].T.astype(LOW)
            keep_ref[...] = output_sum[:, : features // 2].T.astype(LOW)
            give_ref[...] = output_sum[:, features // 2 :].T.astype(LOW)

    def still(shape):
        return pl.BlockSpec(shape, lambda i: (0,) * len(shape), pipeline_mode=pl.Buffered(1))

    def whole(shape):
        return pl.BlockSpec(shape, lambda i: (0,) * len(shape))

    moving = pl.BlockSpec((block, width), lambda i: (i, 0))
    half = (features // 2, width)
    return pl.pallas_call(
        kernel,
        grid=(steps,),
        out_shape=[
            jax.ShapeDtypeStruct((rows, 3 * width), LOW),
            jax.ShapeDtypeStruct(half, LOW),
            jax.ShapeDtypeStruct(half, LOW),
        ],
        in_specs=[pl.BlockSpec(memory_space=pltpu.HBM)] * len(pieces)
        + [still(outs[0].shape), still(outs[1].shape), moving, still((rows, width)), still((rows, width))]
        + [moving, moving, moving, still((rows, width)), still((rows, width))]
        + [pl.BlockSpec((block, 1), lambda i: (i, 0)), still((1, rows))],
        out_specs=[whole((rows, 3 * width)), whole(half), whole(half)],
        scratch_shapes=[
            pltpu.VMEM((rows, features), LOW),
            pltpu.VMEM((width, features), LOW),
            pltpu.VMEM((width, rows), f32),
            pltpu.VMEM((width, rows), f32),
            pltpu.VMEM((width, features), f32),
            pltpu.SemaphoreType.DMA((len(pieces),)),
        ],
        compiler_params=pltpu.CompilerParams(
            dimension_semantics=("arbitrary",), vmem_limit_bytes=32 << 20
        ),
        cost_estimate=pl.CostEstimate(
            flops=4 * rows * features * width + 20 * rows * rows * width,
            transcendentals=2 * rows * rows,
            bytes_accessed=2 * rows * features + 24 * rows * width,
        ),
    )(*(in_main(a) for a in (*pieces, *outs, queries, keys, values, mixed, numerator, total, *places)))


def turned_pieces(value):
    total, rows, columns = value.shape
    half = rows // 2

    def kernel(value_ref, first_ref, second_ref):
        first_ref[0] = value_ref[0, :half].T
        second_ref[0] = value_ref[0, half:].T

    size = value.size * value.dtype.itemsize
    return pl.pallas_call(
        kernel,
        grid=(total,),
        out_shape=[jax.ShapeDtypeStruct((total, columns, half), value.dtype)] * 2,
        in_specs=[pl.BlockSpec((1, rows, columns), lambda i: (i, 0, 0))],
        out_specs=[pl.BlockSpec((1, columns, half), lambda i: (i, 0, 0))] * 2,
        cost_estimate=pl.CostEstimate(flops=0, transcendentals=0, bytes_accessed=2 * size),
    )(value)


def place_rows(pieces, places, dtype):
    count, features = pieces[0].shape

    def kernel(at_ref, *refs):
        for i, ref in enumerate(refs[:-1]):
            first = pl.multiple_of(at_ref[i] * count, count)
            refs[-1][pl.ds(first, count), :] = ref[...].astype(dtype)

    whole = pl.BlockSpec(memory_space=pltpu.VMEM)
    shape = jax.ShapeDtypeStruct((len(pieces) * count, features), dtype)
    return pl.pallas_call(
        kernel,
        out_shape=shape,
        in_specs=[pl.BlockSpec(memory_space=pltpu.SMEM)] + [whole] * len(pieces),
        out_specs=whole,
        cost_estimate=pl.CostEstimate(
            flops=0, transcendentals=0, bytes_accessed=6 * shape.size
        ),
    )(places, *pieces)


def both_of(one, two, start, stop):
    return one[start:stop].astype(jnp.float32) + two[start:stop].astype(jnp.float32)


class Stages:
    def step(self, *flying):
        names = [name for name in vars(self) if name not in flying]
        for name, value in zip(names, tie(*(getattr(self, name) for name in names))):
            setattr(self, name, value)

    def take(self, *names):
        values = [getattr(self, name) for name in names]
        for name in names:
            delattr(self, name)
        return values

    def scatter_0(self, p, rows, rows_of):
        setattr(self, p + "in", swap(rows_of(3), CORE))
        setattr(self, p + "keep", rows_of(1))

    def scatter_1(self, p, rows, rows_of):
        count = rows // 16
        keep, arrived = self.take(p + "keep", p + "in")
        third, middle, first = (
            both_of(keep, arrived, start * count, stop * count).astype(LOW)
            for start, stop in ((3, 4), (1, 3), (0, 1))
        )
        setattr(self, p + "third", swap(third, X))
        setattr(self, p + "middle", swap(middle, X))
        setattr(self, p + "first", first)
        setattr(self, p + "in", swap(rows_of(2), CORE))
        setattr(self, p + "keep", rows_of(0))

    def scatter_2(self, p):
        first, third = self.take(p + "first", p + "third")
        keep, arrived = getattr(self, p + "keep"), getattr(self, p + "in")
        count = first.shape[0]
        last = both_of(keep, arrived, 3 * count, 4 * count) + third.astype(jnp.float32)
        setattr(self, p + "last", swap(last.astype(LOW), CTX, 1))
        setattr(self, p + "first", swap(first, X))

    def scatter_3(self, p):
        middle, last = self.take(p + "middle", p + "last")
        keep, arrived = getattr(self, p + "keep"), getattr(self, p + "in")
        count = last.shape[0]
        far = both_of(keep, arrived, 2 * count, 3 * count) + last.astype(jnp.float32)
        far = far + middle[count:].astype(jnp.float32)
        near = both_of(keep, arrived, count, 2 * count) + middle[:count].astype(jnp.float32)
        setattr(self, p + "far", swap(far.astype(LOW), CTX, 2))
        setattr(self, p + "near", swap(near.astype(LOW), CTX, 1))

    def scatter_4(self, p):
        keep, arrived, *values = self.take(
            p + "keep", p + "in", p + "first", p + "near", p + "far"
        )
        total = both_of(keep, arrived, 0, values[0].shape[0])
        return total + sum(value.astype(jnp.float32) for value in values)

    def gather_0(self, shard):
        self.g0 = shard
        self.g1, self.g2 = swap(shard, CTX, 1), swap(shard, CTX, 2)
        self.x0, self.c0 = swap(shard, X), swap(shard, CORE)

    def gather_1(self):
        self.g3 = swap(self.g2, CTX, 1)
        self.x1, self.x2 = swap(self.g1, X), swap(self.g2, X)

    def gather_2(self):
        self.x3 = swap(self.g3, X)
        self.c1, self.c2, self.c3 = (swap(g, CORE) for g in (self.g1, self.g2, self.g3))
        self.c4 = swap(self.x0, CORE)

    def gather_3(self):
        self.c5, self.c6, self.c7 = (swap(x, CORE) for x in (self.x1, self.x2, self.x3))
        names = [k + str(j) for k in "gx" for j in range(4)] + ["c" + str(j) for j in range(8)]
        return self.take(*names)


def spread(pieces):
    return lax.all_to_all(pieces, CTX, 0, 0, tiled=True)


def side_by_side(pieces):
    return jnp.concatenate(list(pieces), axis=1)


def by_columns(weight, extent):
    return jnp.stack([weight[:, j * extent : (j + 1) * extent] for j in range(4)])


def both(own):
    return jnp.concatenate([own, swap(own, SEQ)])


def halves(left, right):
    grad = contract_rows(left, right).astype(LOW)
    half = grad.shape[0] // 2
    return grad[:half], grad[half:]


def added(keep, arrived):
    return (keep.astype(jnp.float32) + arrived.astype(jnp.float32)).astype(LOW)


def fast_device(
    tokens,
    query_weight,
    key_weight,
    value_weight,
    output_weight,
    gate_weight,
    up_weight,
    down_weight,
    attention_gain,
    feedforward_gain,
    order,
    cotangent,
):
    f32 = jnp.float32
    seq, ctx = lax.axis_index(SEQ), lax.axis_index(CTX)
    x, core = lax.axis_index(X), lax.axis_index(CORE)
    local_rows = tokens.shape[0]
    count = local_rows // 4
    rows = 16 * count
    width = query_weight.shape[1] // 4
    unit = gate_weight.shape[1] // 4
    depth = query_weight.shape[0]

    def turned(values):
        middle_column = values.shape[1] // 2
        other_way = jnp.concatenate([values[:, middle_column:], values[:, :middle_column]], axis=1)
        return jnp.where(seq == 0, values, other_way)

    own_places = jnp.stack([(x ^ a) * 2 + (core ^ b) for b in range(2) for a in range(2)])

    def local(values, a, b):
        return lax.dynamic_slice_in_dim(values, ((x ^ a) * 2 + (core ^ b)) * count, count, 0)

    features = tokens.shape[1]
    v = Stages()

    qkv_pieces = first_pieces(
        query_weight, key_weight, value_weight, attention_gain, feedforward_gain
    )
    v.qkv_own, v.tokens = tie(qkv_pieces, tokens)
    v.qkv_own = spread(v.qkv_own)
    v.tokens = turned(v.tokens)
    shard = local(v.tokens, 0, 0)
    v.g1, v.g2 = swap(shard, CTX, 1), swap(shard, CTX, 2)
    v.cotangent, v.order = cotangent, order
    v.gate, v.up, v.down, v.output = gate_weight, up_weight, down_weight, output_weight
    v.step("qkv_own")

    v.g3, v.x1, v.x2 = swap(v.g2, CTX, 1), swap(v.g1, X), swap(v.g2, X)
    v.output = v.output.reshape(4, width, depth)
    blocks = jnp.arange(16, dtype=jnp.int32)
    stored = (
        (ctx ^ (blocks & 3)) * local_rows
        + (x ^ ((blocks >> 2) & 1)) * (2 * count)
        + (core ^ (blocks >> 3)) * count
    )
    stored = (stored[:, None] + jnp.arange(count, dtype=jnp.int32)[None, :]).reshape(-1)
    slots = jnp.arange(order.shape[0], dtype=jnp.int32)
    places = jnp.sum(
        jnp.where((stored // BLOCK)[:, None] == slots[None, :], v.order[None, :], 0), axis=1
    )
    places = places * BLOCK + stored % BLOCK
    v.column, v.line = places[:, None], places[None, :]
    entry = jnp.arange(width, dtype=jnp.int32) % (HD // 2)
    inverse = THETA ** (-(entry.astype(f32) * 2.0) / HD)
    sign = jnp.where(jnp.arange(width) % HD < HD // 2, -1.0, 1.0).astype(f32)
    angle = places.astype(f32)[:, None] * inverse[None, :]
    v.cosine, v.sine = jnp.cos(angle), jnp.sin(angle) * sign[None, :]
    del v.order
    v.step("qkv_own", "x1", "x2")

    v.x3 = swap(v.g3, X)
    v.cotangent = turned(v.cotangent)
    v.shard = local(v.cotangent, 0, 0)
    v.up = by_columns(v.up, unit)
    v.step("x3")

    v.qkv_o = swap(v.qkv_own, SEQ)
    v.output = spread(v.output)
    v.down, v.down_late = turned_pieces(v.down.reshape(4, unit, depth))
    v.c1, v.c2, v.c3 = (swap(g, CORE) for g in (v.g1, v.g2, v.g3))
    v.c4, v.c5 = swap(v.x1, CORE), swap(v.x2, CORE)
    v.step("qkv_o")

    def whole(values, line, line_x, other, other_x):
        return stack_rows(
            [None, *line, None, *line_x, None, *other, None, *other_x], values, own_places
        )

    v.d1, v.d2 = swap(v.shard, CTX, 1), swap(v.shard, CTX, 2)
    v.gate = spread(by_columns(v.gate, unit))
    del v.shard
    v.c6 = swap(v.x3, CORE)
    v.step("gate", "d1", "d2")

    v.gain_first, v.gain_second = (
        jnp.concatenate([half[:, depth + i, :depth] for half in (v.qkv_own, v.qkv_o)])
        .reshape(1, 8 * depth)
        .astype(f32)
        for i in range(2)
    )
    g1, g2, g3, x1, x2, x3 = v.take("g1", "g2", "g3", "x1", "x2", "x3")
    c1, c2, c3, c4, c5, c6 = v.take("c1", "c2", "c3", "c4", "c5", "c6")
    outputs = attention(
        [None, g1, g2, g3, None, x1, x2, x3, None, c1, c2, c3, None, c4, c5, c6],
        v.tokens,
        own_places,
        v.qkv_own,
        v.qkv_o,
        v.cosine,
        v.sine,
        v.column,
        v.line,
    )
    v.normed, v.queries, v.keys, v.values, v.mixed, v.numerator, v.total = outputs
    v.output_other = swap(v.output, SEQ)
    v.step("gate")

    def attended(index):
        return v.take("part%d" % index)[0]

    v.e1, v.e2 = swap(v.d1, X), swap(v.d2, X)
    v.part0, v.part1, v.part2, v.part3 = project(v.mixed, [v.output, v.output_other])
    v.scatter_0("s_", rows, attended)
    v.step("e1", "e2")
    v.up = spread(v.up)
    v.gate_o = swap(v.gate, SEQ)
    v.scatter_1("s_", rows, attended)
    v.d3 = swap(v.d2, CTX, 1)
    v.f1, v.f2 = swap(v.d1, CORE), swap(v.d2, CORE)
    v.step("up", "gate_o", "d3", "s_middle")
    v.scatter_2("s_")
    v.step("s_first", "gate_o")
    v.scatter_3("s_")
    v.up_o = swap(v.up, SEQ)
    v.e3, v.f3 = swap(v.d3, X), swap(v.d3, CORE)
    v.step("up_o", "e3")
    v.middle = local(v.tokens, 0, 0).astype(f32) + v.scatter_4("s_")
    v.scale_second = lax.rsqrt(jnp.mean(v.middle * v.middle, axis=1, keepdims=True) + EPS)
    v.gather_0((v.middle * v.scale_second * v.gain_second).astype(LOW))
    v.f4, v.f5, v.f6 = (swap(e, CORE) for e in (v.e1, v.e2, v.e3))
    v.step("x0", "up_o")
    v.gather_1()
    d1, d2, d3, e1, e2, e3 = v.take("d1", "d2", "d3", "e1", "e2", "e3")
    f1, f2, f3, f4, f5, f6 = v.take("f1", "f2", "f3", "f4", "f5", "f6")
    v.every_cotangent = whole(v.cotangent, [d1, d2, d3], [e1, e2, e3], [f1, f2, f3], [f4, f5, f6])
    v.step("x1", "x2")
    v.gather_2()
    v.down = spread(v.down)
    v.step("down")
    pieces = v.gather_3()
    for i, piece in enumerate(pieces):
        setattr(v, "piece%d" % i, piece)
    v.step()

    v.down_late = spread(v.down_late)
    v.down_o = swap(v.down, SEQ)
    v.normed_two, v.hidden, v.gate_slope, v.up_slope = feed_forward(
        v.take(*("piece%d" % i for i in range(16))),
        [own.reshape(4 * depth, unit) for own in (v.gate, v.gate_o)],
        [own.reshape(4 * depth, unit) for own in (v.up, v.up_o)],
    )
    v.step("down_o")
    v.late_other = swap(v.down_late, SEQ)
    v.down_k, v.down_g = halves(v.every_cotangent, v.hidden)
    v.gate_full = jnp.concatenate(v.take("gate", "gate_o")).reshape(8 * depth, unit)
    v.up_full = jnp.concatenate(v.take("up", "up_o")).reshape(8 * depth, unit)
    v.step()
    v.gate_grad, v.up_grad = feed_back(
        v.take("every_cotangent")[0],
        [
            own.reshape(4 * depth, unit // 2)
            for own in (v.down, v.down_o, v.down_late, v.late_other)
        ],
        *v.take("gate_slope", "up_slope"),
    )
    v.down_g = swap(v.down_g, SEQ)
    v.step("down_g")

    def quarter(values, index):
        size = rows // 4
        return values[index * size : (index + 1) * size]

    def normed_grads(index):
        gate, up = quarter(v.gate_grad, index), quarter(v.up_grad, index)
        return (contract_cols(gate, v.gate_full) + contract_cols(up, v.up_full)).astype(LOW)

    v.scatter_0("s_", rows, normed_grads)
    v.step("down_g")
    v.scatter_1("s_", rows, normed_grads)
    v.gate_k, v.gate_g = halves(v.normed_two, v.gate_grad)
    v.step("down_g", "s_middle")
    del v.gate_full, v.up_full
    v.scatter_2("s_")
    v.gate_g = swap(v.gate_g, SEQ)
    v.up_k, v.up_g = halves(v.normed_two, v.up_grad)
    v.step("s_first", "gate_g", "down_g")
    del v.normed_two, v.gate_grad, v.up_grad
    v.scatter_3("s_")
    v.up_g = swap(v.up_g, SEQ)
    v.down_full = jnp.concatenate(
        [
            jnp.concatenate(v.take("down", "down_o")),
            jnp.concatenate(v.take("down_late", "late_other")),
        ],
        axis=2,
    ).reshape(8 * depth, unit)
    v.step("gate_g", "up_g")
    normed_two_grad = v.scatter_4("s_")
    middle, scale_second = v.middle, v.scale_second
    scaled = normed_two_grad * v.gain_second
    v.middle_grad = (
        local(v.cotangent, 0, 0).astype(f32)
        + scale_second * scaled
        - middle * scale_second**3 * jnp.mean(scaled * middle, axis=1, keepdims=True)
    )
    del v.cotangent, v.scale_second, v.gain_second
    v.gather_0(v.middle_grad.astype(LOW))
    v.qkv_full = jnp.concatenate([v.qkv_own, v.qkv_o])[:, :depth].reshape(8 * depth, 3 * width)
    del v.qkv_own, v.qkv_o
    v.step("gate_g", "up_g", "x0")
    v.gather_1()
    v.step("up_g", "x1", "x2")

    def fed(index):
        return contract_cols(quarter(v.hidden, index), v.down_full).astype(LOW)

    def projected_grads(index):
        return contract_cols(quarter(v.projected_grad, index), v.qkv_full).astype(LOW)

    v.gather_2()
    v.down = spread(added(*v.take("down_k", "down_g")).reshape(4, depth, unit))
    v.gate_sum = added(*v.take("gate_k", "gate_g")).reshape(4, depth, unit)
    v.step("down")
    pieces = v.gather_3()
    for i, piece in enumerate(pieces):
        setattr(v, "piece%d" % i, piece)
    v.step()

    v.gate = spread(v.take("gate_sum")[0])
    v.projected_grad, v.out_k, v.out_g = attention_back(
        v.take(*("piece%d" % i for i in range(16))),
        v.take("output", "output_other"),
        *v.take("queries", "keys", "values", "mixed", "numerator", "total"),
        *v.take("cosine", "sine", "column", "line"),
    )
    v.step("gate")
    v.out_g = swap(v.out_g, SEQ)
    v.scatter_0("s_", rows, projected_grads)
    v.step("out_g")
    v.scatter_1("s_", rows, projected_grads)
    v.scatter_0("p_", rows, fed)
    v.step("out_g", "s_middle")
    v.scatter_2("s_")
    v.up = spread(added(*v.take("up_k", "up_g")).reshape(4, depth, unit))
    v.qkv_k, v.qkv_g = halves(v.normed, v.projected_grad)
    del v.projected_grad, v.qkv_full, v.normed
    v.scatter_1("p_", rows, fed)
    v.step("up", "s_first", "p_middle")
    del v.hidden, v.down_full
    v.scatter_3("s_")
    v.qkv_g = swap(v.qkv_g, SEQ)
    v.scatter_2("p_")
    v.down_wgrad = v.take("down")[0].transpose(0, 2, 1).reshape(4 * unit, depth).astype(f32)
    v.step("p_first", "qkv_g")
    v.scatter_3("p_")
    sums = [added(*v.take(kind + "_k", kind + "_g")) for kind in ("qkv", "out")]
    v.qkv_sum = jnp.concatenate(sums, axis=1).reshape(4, depth, 4 * width)
    own_input = local(v.tokens, 0, 0).astype(f32)
    normed_grad = v.scatter_4("s_")
    scale_own = lax.rsqrt(jnp.mean(own_input * own_input, axis=1, keepdims=True) + EPS)
    scaled = normed_grad * v.gain_first
    input_grad = (
        v.middle_grad
        + scale_own * scaled
        - own_input * scale_own**3 * jnp.mean(scaled * own_input, axis=1, keepdims=True)
    )
    v.input_grad = input_grad.astype(LOW)
    v.step()
    v.qkv = spread(v.take("qkv_sum")[0])
    v.produced = turned((v.take("middle")[0] + v.scatter_4("p_")).astype(LOW))
    v.input_grad = turned(v.input_grad)
    v.input_x, v.input_core = swap(v.input_grad, X), swap(v.input_grad, CORE)
    v.produced_x, v.produced_core = swap(v.produced, X), swap(v.produced, CORE)
    v.gate_wgrad = side_by_side(v.take("gate")[0]).astype(f32)
    v.up_wgrad = side_by_side(v.take("up")[0]).astype(f32)

    def gain_grad(gain, *pairs):
        part = sum(jnp.sum(w.astype(f32) * g, axis=1) for w, g in pairs)
        return part / gain.astype(f32)

    v.second_gain = gain_grad(
        feedforward_gain, (gate_weight, v.gate_wgrad), (up_weight, v.up_wgrad)
    )
    v.step("qkv")
    v.input_far = swap(v.input_x, CORE)
    v.produced_far = swap(v.produced_x, CORE)
    v.step("qkv")
    input_pieces = v.take("input_grad", "input_x", "input_core", "input_far")
    v.input_out = place_rows(input_pieces, own_places, f32)
    produced_pieces = v.take("produced", "produced_x", "produced_core", "produced_far")
    v.block_output = place_rows(produced_pieces, own_places, LOW)
    v.step()
    block_output, input_grad = v.block_output, v.input_out
    qkv_pieces, output_pieces = v.qkv[:, :, : 3 * width], v.qkv[:, :, 3 * width :]

    query_wgrad, key_wgrad, value_wgrad = (
        side_by_side(qkv_pieces[:, :, first : first + width]).astype(f32)
        for first in (0, width, 2 * width)
    )
    gate_wgrad, up_wgrad = v.gate_wgrad, v.up_wgrad

    gain_grads = jnp.stack(
        [
            gain_grad(
                attention_gain,
                (query_weight, query_wgrad),
                (key_weight, key_wgrad),
                (value_weight, value_wgrad),
            ),
            v.second_gain,
        ]
    )
    gain_grads = gain_grads + swap(gain_grads, CORE)
    gain_grads = gain_grads + swap(gain_grads, X)
    return (
        block_output,
        input_grad,
        query_wgrad,
        key_wgrad,
        value_wgrad,
        output_pieces.transpose(0, 2, 1).reshape(4 * width, depth).astype(f32),
        gate_wgrad,
        up_wgrad,
        v.down_wgrad,
        gain_grads[0],
        gain_grads[1],
    )


def fast_solution(mesh):
    sizes = mesh.shape
    lines = Mesh(
        mesh.devices.reshape(sizes[SEQ], sizes[CTX], 2, 2), (SEQ, CTX, X, CORE)
    )
    rows, heads = (SEQ, CTX), (X, CORE)
    wide, tall = P(rows, heads), P(heads, rows)
    return jax.shard_map(
        fast_device,
        mesh=lines,
        in_specs=(
            P(rows, None),
            wide,
            wide,
            wide,
            tall,
            wide,
            wide,
            tall,
            P(rows),
            P(rows),
            P(),
            P(rows, None),
        ),
        out_specs=(
            P(rows, None),
            P(rows, None),
            wide,
            wide,
            wide,
            tall,
            wide,
            wide,
            tall,
            P(rows),
            P(rows),
        ),
        check_vma=False,
    )


def solution(mesh):
    sizes = mesh.shape
    if mesh.axis_names == (SEQ, CTX, TP) and tuple(sizes.values()) == (2, 4, 4):
        return fast_solution(mesh)
    return general_solution(mesh)
```

```python
from functools import partial

import jax
import jax.numpy as jnp
from jax import lax
from jax.experimental import pallas as pl
from jax.experimental.pallas import tpu as pltpu
from jax.sharding import Mesh, PartitionSpec as P

HD = 64
SEQ, CTX, TP, X, CORE = ("seq", "ctx", "tp", "x", "core")
BLOCK = 128


THETA = 130000.0
EPS = 1e-05


def shifted(block, axis, distance):
    devices = range(lax.axis_size(axis))
    route = [((i - distance) % len(devices), i) for i in devices]
    return lax.ppermute(block, axis, route)


def rms_norm(hidden, gain):
    return hidden * lax.rsqrt(jnp.mean(hidden * hidden, axis=-1, keepdims=True) + EPS) * gain


def rotary(values, places):
    row_count = values.shape[0]
    by_heads = values.reshape(row_count, -1, HD)
    halfway = HD // 2
    inverse = THETA ** (-(jnp.arange(halfway, dtype=jnp.float32) * 2.0) / HD)
    angle = places.astype(jnp.float32)[:, None] * inverse[None, :]
    angle = jnp.concatenate([angle, angle], axis=1)
    cosine = jnp.cos(angle)[:, None, :]
    sine = jnp.sin(angle)[:, None, :]
    turned = jnp.concatenate([-by_heads[..., halfway:], by_heads[..., :halfway]], axis=-1)
    return (by_heads * cosine + turned * sine).reshape(row_count, -1)


def gated(gate, upward):
    return jax.nn.silu(gate) * upward


def product(left, right):
    return jnp.dot(left, right, preferred_element_type=jnp.float32)


def contract_rows(left, right):
    return lax.dot_general(
        left, right, (((0,), (0,)), ((), ())), preferred_element_type=jnp.float32
    )


def contract_cols(left, right):
    return lax.dot_general(
        left, right, (((1,), (1,)), ((), ())), preferred_element_type=jnp.float32
    )


def key_places(order, first_row, row_total):
    stored = first_row + jnp.arange(row_total, dtype=jnp.int32)
    group_slot = stored // BLOCK
    slot_table = jnp.arange(order.shape[0], dtype=jnp.int32)
    block_place = jnp.sum(
        jnp.where(group_slot[:, None] == slot_table[None, :], order[None, :], 0), axis=1
    )
    return block_place * BLOCK + stored % BLOCK


def exp_scores(query_heads, query_places, key_rows, key_pos):
    row_total = key_rows.shape[0]
    key_heads = key_rows.reshape(row_total, -1, HD)
    scores = (
        jnp.einsum("qhd,khd->hqk", query_heads, key_heads, preferred_element_type=jnp.float32)
        * 0.125
    )
    allowed = query_places[:, None] >= key_pos[None, :]
    return (jnp.where(allowed[None], jnp.exp(scores), 0.0), key_heads)


def general_device(
    tokens,
    query_weight,
    key_weight,
    value_weight,
    output_weight,
    gate_weight,
    up_weight,
    down_weight,
    attention_gain,
    feedforward_gain,
    order,
    cotangent,
):
    rows_local = tokens.shape[0]
    ctx_index = lax.axis_index(CTX)
    ctx_total = lax.axis_size(CTX)
    gathered = (
        lax.all_gather(query_weight, (SEQ, CTX), axis=0, tiled=True),
        lax.all_gather(key_weight, (SEQ, CTX), axis=0, tiled=True),
        lax.all_gather(value_weight, (SEQ, CTX), axis=0, tiled=True),
        lax.all_gather(output_weight, (SEQ, CTX), axis=1, tiled=True),
        lax.all_gather(gate_weight, (SEQ, CTX), axis=0, tiled=True),
        lax.all_gather(up_weight, (SEQ, CTX), axis=0, tiled=True),
        lax.all_gather(down_weight, (SEQ, CTX), axis=1, tiled=True),
        lax.all_gather(attention_gain, (SEQ, CTX), axis=0, tiled=True),
        lax.all_gather(feedforward_gain, (SEQ, CTX), axis=0, tiled=True),
    )
    (
        full_query,
        full_key,
        full_value,
        full_output,
        full_gate,
        full_up,
        full_down,
        gain_first,
        gain_second,
    ) = gathered
    inputs = tokens.astype(jnp.float32)
    query_places = key_places(order, ctx_index * rows_local, rows_local)
    normed_value, norm_back_first = jax.vjp(rms_norm, inputs, gain_first.astype(jnp.float32))
    normed = normed_value.astype(jnp.bfloat16)
    rope_here = partial(rotary, places=query_places)
    query_rot, query_back = jax.vjp(rope_here, product(normed, full_query))
    key_rot, key_back = jax.vjp(rope_here, product(normed, full_key))
    value_rows = product(normed, full_value).astype(jnp.bfloat16)
    query_rows = query_rot.astype(jnp.bfloat16)
    key_rows = key_rot.astype(jnp.bfloat16)
    width = query_rows.shape[1]
    head_count = width // HD
    query_heads = query_rows.reshape(rows_local, head_count, HD)
    packed = jnp.stack([key_rows, value_rows])
    empty_totals = jnp.zeros((rows_local, head_count), jnp.float32)
    empty_numerator = jnp.zeros((rows_local, width), jnp.float32)
    arrived = lax.all_gather(packed, CTX, axis=1, tiled=True)
    row_total = arrived.shape[1]

    def one_block(block_index, partial_state):
        first_row = block_index * rows_local
        section = lax.dynamic_slice_in_dim(arrived, first_row, rows_local, 1)
        key_pos = key_places(order, first_row, rows_local)
        weights, key_heads = exp_scores(query_heads, query_places, section[0], key_pos)
        value_heads = section[1].reshape(rows_local, -1, HD)
        totals, numerator = partial_state
        totals = totals + jnp.sum(weights, axis=2).T
        numerator = numerator + jnp.einsum(
            "hqk,khd->qhd",
            weights.astype(jnp.bfloat16),
            value_heads,
            preferred_element_type=jnp.float32,
        ).reshape(rows_local, width)
        return (totals, numerator)

    totals, numerator = lax.fori_loop(
        0, row_total // rows_local, one_block, (empty_totals, empty_numerator)
    )
    numerator_heads = numerator.reshape(rows_local, head_count, HD)
    mixed = (numerator_heads / totals[:, :, None]).astype(jnp.bfloat16).reshape(rows_local, width)
    middle = inputs + lax.psum(product(mixed, full_output), TP)
    normed_two_value, norm_back_second = jax.vjp(rms_norm, middle, gain_second.astype(jnp.float32))
    normed_two = normed_two_value.astype(jnp.bfloat16)
    activated, gated_back = jax.vjp(
        gated, product(normed_two, full_gate), product(normed_two, full_up)
    )
    hidden = activated.astype(jnp.bfloat16)
    block_output = middle + lax.psum(product(hidden, full_down).astype(jnp.bfloat16), TP).astype(
        jnp.float32
    )
    back_weights = (
        lax.all_gather(query_weight, (SEQ, CTX), axis=0, tiled=True),
        lax.all_gather(key_weight, (SEQ, CTX), axis=0, tiled=True),
        lax.all_gather(value_weight, (SEQ, CTX), axis=0, tiled=True),
        lax.all_gather(output_weight, (SEQ, CTX), axis=1, tiled=True),
        lax.all_gather(gate_weight, (SEQ, CTX), axis=0, tiled=True),
        lax.all_gather(up_weight, (SEQ, CTX), axis=0, tiled=True),
        lax.all_gather(down_weight, (SEQ, CTX), axis=1, tiled=True),
        lax.all_gather(attention_gain, (SEQ, CTX), axis=0, tiled=True),
        lax.all_gather(feedforward_gain, (SEQ, CTX), axis=0, tiled=True),
    )
    (
        back_query,
        back_key,
        back_value,
        back_output,
        back_gate,
        back_up,
        back_down,
        gain_unused,
        gain_spare,
    ) = back_weights
    down_grad = contract_rows(hidden, cotangent)
    hidden_grad = contract_cols(cotangent, back_down)
    gate_grad, upward_grad = gated_back(hidden_grad)
    gate_grad = gate_grad.astype(jnp.bfloat16)
    upward_grad = upward_grad.astype(jnp.bfloat16)
    gate_wgrad = contract_rows(normed_two, gate_grad)
    upward_wgrad = contract_rows(normed_two, upward_grad)
    normed_two_grad = lax.psum(
        contract_cols(gate_grad, back_gate) + contract_cols(upward_grad, back_up), TP
    )
    middle_norm_grad, second_gain_grad = norm_back_second(normed_two_grad)
    middle_grad = cotangent.astype(jnp.float32) + middle_norm_grad
    branch_grad = middle_grad.astype(jnp.bfloat16)
    output_wgrad = contract_rows(mixed, branch_grad)
    mixed_grad = contract_cols(branch_grad, back_output).reshape(rows_local, head_count, HD)
    numerator_grad = (mixed_grad / totals[:, :, None]).astype(jnp.bfloat16)
    totals_grad = -jnp.sum(mixed_grad * numerator_heads, axis=2) / (totals * totals)
    totals_grad_heads = totals_grad.T[:, :, None]

    def visit(turn_index, state):
        visiting, carried, query_acc = state
        source = (ctx_index - turn_index) % ctx_total
        key_pos = key_places(order, source * rows_local, rows_local)
        weights, key_heads = exp_scores(query_heads, query_places, visiting[0], key_pos)
        value_heads = visiting[1].reshape(rows_local, -1, HD)
        through = jnp.einsum(
            "qhd,khd->hqk", numerator_grad, value_heads, preferred_element_type=jnp.float32
        )
        slopes = (weights * (through + totals_grad_heads)).astype(jnp.bfloat16)
        query_acc = (
            query_acc
            + jnp.einsum("hqk,khd->qhd", slopes, key_heads, preferred_element_type=jnp.float32)
            * 0.125
        )
        key_term = (
            jnp.einsum("hqk,qhd->khd", slopes, query_heads, preferred_element_type=jnp.float32)
            * 0.125
        )
        value_term = jnp.einsum(
            "hqk,qhd->khd",
            weights.astype(jnp.bfloat16),
            numerator_grad,
            preferred_element_type=jnp.float32,
        )
        carried = carried + jnp.stack(
            [key_term.reshape(rows_local, width), value_term.reshape(rows_local, width)]
        )
        visiting = shifted(visiting, CTX, 1)
        carried = shifted(carried, CTX, 1)
        return (visiting, carried, query_acc)

    start_state = (
        packed,
        jnp.zeros((2, rows_local, width), jnp.float32),
        jnp.zeros((rows_local, head_count, HD), jnp.float32),
    )
    ended, key_value_grad, query_acc = lax.fori_loop(0, ctx_total, visit, start_state)
    query_proj_grad = query_back(query_acc.reshape(rows_local, width))[0].astype(jnp.bfloat16)
    key_proj_grad = key_back(key_value_grad[0])[0].astype(jnp.bfloat16)
    value_grad = key_value_grad[1].astype(jnp.bfloat16)
    query_wgrad = contract_rows(normed, query_proj_grad)
    key_wgrad = contract_rows(normed, key_proj_grad)
    value_wgrad = contract_rows(normed, value_grad)
    normed_grad = lax.psum(
        (
            contract_cols(query_proj_grad, back_query)
            + contract_cols(key_proj_grad, back_key)
            + contract_cols(value_grad, back_value)
        ).astype(jnp.bfloat16),
        TP,
    ).astype(jnp.float32)
    input_norm_grad, first_gain_grad = norm_back_first(normed_grad)
    input_grad = middle_grad + input_norm_grad
    scattered = (
        lax.psum_scatter(
            query_wgrad.astype(jnp.bfloat16), (SEQ, CTX), scatter_dimension=0, tiled=True
        ).astype(jnp.float32),
        lax.psum_scatter(
            key_wgrad.astype(jnp.bfloat16), (SEQ, CTX), scatter_dimension=0, tiled=True
        ).astype(jnp.float32),
        lax.psum_scatter(
            value_wgrad.astype(jnp.bfloat16), (SEQ, CTX), scatter_dimension=0, tiled=True
        ).astype(jnp.float32),
        lax.psum_scatter(
            output_wgrad.astype(jnp.bfloat16), (SEQ, CTX), scatter_dimension=1, tiled=True
        ).astype(jnp.float32),
        lax.psum_scatter(
            gate_wgrad.astype(jnp.bfloat16), (SEQ, CTX), scatter_dimension=0, tiled=True
        ).astype(jnp.float32),
        lax.psum_scatter(
            upward_wgrad.astype(jnp.bfloat16), (SEQ, CTX), scatter_dimension=0, tiled=True
        ).astype(jnp.float32),
        lax.psum_scatter(
            down_grad.astype(jnp.bfloat16), (SEQ, CTX), scatter_dimension=1, tiled=True
        ).astype(jnp.float32),
        lax.psum_scatter(
            first_gain_grad.astype(jnp.bfloat16), (SEQ, CTX), scatter_dimension=0, tiled=True
        ).astype(jnp.float32),
        lax.psum_scatter(
            second_gain_grad.astype(jnp.bfloat16), (SEQ, CTX), scatter_dimension=0, tiled=True
        ).astype(jnp.float32),
    )
    return (
        block_output.astype(jnp.bfloat16),
        input_grad,
        scattered[0],
        scattered[1],
        scattered[2],
        scattered[3],
        scattered[4],
        scattered[5],
        scattered[6],
        scattered[7],
        scattered[8],
    )


def general_solution(mesh):
    placed = (
        P((SEQ, CTX), None),
        P((SEQ, CTX), TP),
        P((SEQ, CTX), TP),
        P((SEQ, CTX), TP),
        P(TP, (SEQ, CTX)),
        P((SEQ, CTX), TP),
        P((SEQ, CTX), TP),
        P(TP, (SEQ, CTX)),
        P((SEQ, CTX)),
        P((SEQ, CTX)),
        P(),
        P((SEQ, CTX), None),
    )
    return jax.shard_map(
        general_device,
        mesh=mesh,
        in_specs=placed,
        out_specs=(
            P((SEQ, CTX), None),
            P((SEQ, CTX), None),
            P((SEQ, CTX), TP),
            P((SEQ, CTX), TP),
            P((SEQ, CTX), TP),
            P(TP, (SEQ, CTX)),
            P((SEQ, CTX), TP),
            P((SEQ, CTX), TP),
            P(TP, (SEQ, CTX)),
            P((SEQ, CTX)),
            P((SEQ, CTX)),
        ),
        check_vma=False,
    )


LOW = jnp.bfloat16


def swap(value, axis, mask=1):
    pairs = [(i, i ^ mask) for i in range(lax.axis_size(axis))]
    return lax.ppermute(value, axis, pairs)


def tie(*values):
    return lax.optimization_barrier(values)


def in_main(value):
    return pltpu.with_memory_space_constraint(value, pltpu.HBM)


def stack_rows(pieces, local=None, places=None):
    pieces = list(pieces)
    own = [i for i, piece in enumerate(pieces) if piece is None]
    given = [piece for piece in pieces if piece is not None]
    like = given[0]
    total, count = len(pieces), like.shape[0]
    shape = jax.ShapeDtypeStruct((total * count, like.shape[1]), like.dtype)

    def kernel(*refs):
        at_ref, *refs = refs
        *ins, out, sems = refs
        source = iter(ins)
        copies = []
        for i in range(total):
            if i in own:
                first = pl.multiple_of(at_ref[own.index(i)] * count, count)
                block = ins[-1].at[pl.ds(first, count)]
            else:
                block = next(source)
            copies.append(
                pltpu.make_async_copy(block, out.at[pl.ds(i * count, count)], sems.at[i])
            )
        for copy in copies:
            copy.start()
        for copy in copies:
            copy.wait()

    operands = given + ([local] if own else [])
    at = places if own else jnp.zeros((1,), jnp.int32)
    size = shape.size * shape.dtype.itemsize
    return pl.pallas_call(
        kernel,
        out_shape=shape,
        in_specs=[pl.BlockSpec(memory_space=pltpu.SMEM)]
        + [pl.BlockSpec(memory_space=pltpu.HBM)] * len(operands),
        out_specs=pl.BlockSpec(memory_space=pltpu.VMEM),
        scratch_shapes=[pltpu.SemaphoreType.DMA((total,))],
        cost_estimate=pl.CostEstimate(flops=0, transcendentals=0, bytes_accessed=2 * size),
    )(at.astype(jnp.int32), *(in_main(operand) for operand in operands))


def first_pieces(query, key, value, gain_one, gain_two):
    depth, width = query.shape[0], query.shape[1] // 4
    f32 = jnp.float32

    def kernel(q_ref, k_ref, v_ref, one_ref, two_ref, out_ref):
        line = lax.broadcasted_iota(jnp.int32, (16, depth), 0)
        one, two = (
            jnp.broadcast_to(ref[...].astype(f32)[None], (16, depth)) for ref in (one_ref, two_ref)
        )
        gains = jnp.where(line == 0, one, jnp.where(line == 1, two, 0.0)).astype(LOW)
        for j in range(4):
            for i, ref in enumerate((q_ref, k_ref, v_ref)):
                out_ref[j, :depth, i * width : (i + 1) * width] = ref[:, j * width : (j + 1) * width]
            out_ref[j, depth:, :depth] = gains
            out_ref[j, depth:, depth:] = jnp.zeros((16, 3 * width - depth), LOW)

    whole = pl.BlockSpec(memory_space=pltpu.VMEM)
    size = 4 * (depth + 16) * 3 * width
    return pl.pallas_call(
        kernel,
        out_shape=jax.ShapeDtypeStruct((4, depth + 16, 3 * width), LOW),
        in_specs=[whole] * 5,
        out_specs=whole,
        cost_estimate=pl.CostEstimate(flops=0, transcendentals=0, bytes_accessed=4 * size),
    )(query, key, value, gain_one, gain_two)


def feed_forward(pieces, gates, ups):
    features, count, steps = pieces[0].shape[1], pieces[0].shape[0], 4
    rows, unit, part = count * len(pieces), gates[0].shape[1], features // 2
    block, group = rows // steps, len(pieces) // steps
    f32 = jnp.float32

    def kernel(*refs):
        ins, refs = refs[: len(pieces)], refs[len(pieces) :]
        gate_refs, up_refs = refs[:2], refs[2:4]
        rows_ref, hidden_ref, gate_slope_ref, up_slope_ref, held, sems = refs[4:]
        step = pl.program_id(0)

        def copy(i):
            return pltpu.make_async_copy(ins[i], held.at[pl.ds(i * count, count)], sems.at[i])

        for at in range(steps):

            @pl.when(step == at)
            def _(at=at):
                if at == 0:
                    for i in range(len(pieces)):
                        copy(i).start()
                for i in range(at * group, (at + 1) * group):
                    copy(i).wait()

        values = held[pl.ds(pl.multiple_of(step * block, block), block), :]
        rows_ref[...] = values
        gate, up = (
            product(values[:, :part], first[...]) + product(values[:, part:], second[...])
            for first, second in (gate_refs, up_refs)
        )
        sigmoid = 1.0 / (1.0 + jnp.exp(-gate))
        silu = gate * sigmoid
        hidden_ref[...] = (silu * up).astype(LOW)
        gate_slope_ref[...] = (up * (sigmoid * (1.0 + gate * (1.0 - sigmoid)))).astype(LOW)
        up_slope_ref[...] = silu.astype(LOW)

    wide = pl.BlockSpec((block, features), lambda i: (i, 0))
    narrow = pl.BlockSpec((block, unit), lambda i: (i, 0))
    half = pl.BlockSpec((part, unit), lambda i: (0, 0), pipeline_mode=pl.Buffered(1))
    return pl.pallas_call(
        kernel,
        grid=(steps,),
        out_shape=[pltpu.HBM((rows, features), LOW), jax.ShapeDtypeStruct((rows, unit), LOW)]
        + [pltpu.HBM((rows, unit), LOW)] * 2,
        in_specs=[pl.BlockSpec(memory_space=pltpu.HBM)] * len(pieces) + [half] * 4,
        out_specs=[wide, narrow, narrow, narrow],
        scratch_shapes=[
            pltpu.VMEM((rows, features), LOW),
            pltpu.SemaphoreType.DMA((len(pieces),)),
        ],
        compiler_params=pltpu.CompilerParams(
            dimension_semantics=("arbitrary",), vmem_limit_bytes=32 << 20
        ),
        cost_estimate=pl.CostEstimate(
            flops=4 * rows * features * unit,
            transcendentals=rows * unit,
            bytes_accessed=4 * rows * features + 4 * features * unit + 10 * rows * unit,
        ),
    )(*(in_main(piece) for piece in pieces), *gates, *ups)


def feed_back(cotangent, downs, gate_slope, up_slope):
    rows, features = cotangent.shape
    unit, steps, part = gate_slope.shape[1], 4, features // 2
    block = rows // steps

    def kernel(cot_ref, *refs):
        gate_slope_ref, up_slope_ref, gate_ref, up_ref = refs[4:]
        for i in range(2):
            at = slice(i * unit // 2, (i + 1) * unit // 2)
            hidden_grad = product(cot_ref[:, :part], refs[2 * i][...])
            hidden_grad += product(cot_ref[:, part:], refs[2 * i + 1][...])
            gate_ref[:, at] = (hidden_grad * gate_slope_ref[:, at].astype(jnp.float32)).astype(LOW)
            up_ref[:, at] = (hidden_grad * up_slope_ref[:, at].astype(jnp.float32)).astype(LOW)

    wide = pl.BlockSpec((block, features), lambda i: (i, 0))
    narrow = pl.BlockSpec((block, unit), lambda i: (i, 0))
    half = pl.BlockSpec((part, unit // 2), lambda i: (0, 0), pipeline_mode=pl.Buffered(1))
    return pl.pallas_call(
        kernel,
        grid=(steps,),
        out_shape=[jax.ShapeDtypeStruct((rows, unit), LOW)] * 2,
        in_specs=[wide, half, half, half, half, narrow, narrow],
        out_specs=[narrow, narrow],
        compiler_params=pltpu.CompilerParams(dimension_semantics=("arbitrary",)),
        cost_estimate=pl.CostEstimate(
            flops=2 * rows * features * unit,
            transcendentals=0,
            bytes_accessed=2 * rows * features + 2 * features * unit + 12 * rows * unit,
        ),
    )(in_main(cotangent), *downs, gate_slope, up_slope)


def swapped(values):
    lane = lax.broadcasted_iota(jnp.int32, values.shape, 1)
    size = values.shape[1]
    back, forth = pltpu.roll(values, size - HD // 2, 1), pltpu.roll(values, HD // 2, 1)
    return jnp.where(lane % HD < HD // 2, back, forth)


def of_heads(parts, shape):
    lane = lax.broadcasted_iota(jnp.int32, shape, 1)
    result = parts[0]
    for index in range(1, len(parts)):
        result = jnp.where(lane // HD == index, parts[index], result)
    return result


def only_head(values, index):
    lane = lax.broadcasted_iota(jnp.int32, values.shape, 1)
    return jnp.where(lane // HD == index, values, jnp.zeros_like(values))


def attention(pieces, tokens, token_places, own, other, cosine, sine, column, line):
    total_width, features = own.shape[2], tokens.shape[1]
    width, depth, steps = total_width // 3, own.shape[1] - 16, 4
    given = [piece for piece in pieces if piece is not None]
    count = given[0].shape[0]
    rows = count * len(pieces)
    block, group = rows // steps, len(pieces) // steps
    f32 = jnp.float32

    def kernel(at_ref, *refs):
        ins, tokens_ref, refs = refs[: len(given)], refs[len(given)], refs[len(given) + 1 :]
        own_ref, other_ref, cos_ref, sin_ref, col_ref, line_ref = refs[:6]
        normed_ref, q_ref, k_ref, v_ref, mixed_ref, numerator_ref, total_ref = refs[6:13]
        held, w_ref, gain_ref, sems = refs[13:]
        step = pl.program_id(0)

        def copy(i):
            before = sum(piece is not None for piece in pieces[:i])
            if pieces[i] is not None:
                source = ins[before]
            else:
                first = pl.multiple_of(at_ref[i - before] * count, count)
                source = tokens_ref.at[pl.ds(first, count)]
            return pltpu.make_async_copy(source, held.at[pl.ds(i * count, count)], sems.at[i])

        for at in range(steps):

            @pl.when(step == at)
            def _(at=at):
                if at == 0:
                    for i in range(len(pieces)):
                        copy(i).start()
                    for i in range(8):
                        ref, j = (own_ref, other_ref)[i // 4], i % 4
                        w_ref[i * depth : (i + 1) * depth, :] = ref[j, :depth, :]
                        gain_ref[:, i * depth : (i + 1) * depth] = ref[j, depth:, :depth].astype(f32)[:8]
                for i in range(at * group, (at + 1) * group):
                    copy(i).wait()

        @pl.when(step < steps)
        def _():
            at = pl.ds(pl.multiple_of(step * block, block), block)
            values = held[at, :].astype(f32)
            scale = lax.rsqrt(jnp.mean(values * values, axis=1, keepdims=True) + EPS)
            normed = (values * scale * gain_ref[0:1, :]).astype(LOW)
            normed_ref[...] = normed
            projected = product(normed, w_ref[...])
            cos, sin = cos_ref[at, :], sin_ref[at, :]
            for i, ref in enumerate((q_ref, k_ref)):
                u = projected[:, i * width : (i + 1) * width]
                ref[at, :] = (u * cos + swapped(u) * sin).astype(LOW)
            v_ref[at, :] = projected[:, 2 * width :].astype(LOW)

        @pl.when(step >= steps)
        def _():
            at = pl.ds(pl.multiple_of((step - steps) * block, block), block)
            allowed = col_ref[...] >= line_ref[...]
            queries, keys, values = q_ref[at, :] * 0.125, k_ref[...], v_ref[...]
            numerators, totals = [], []
            for index in range(width // HD):
                scores = contract_cols(only_head(queries, index), keys)
                weights = jnp.where(allowed, jnp.exp(scores), 0.0)
                totals.append(jnp.sum(weights, axis=1, keepdims=True))
                numerators.append(product(weights.astype(LOW), values))
            numerator = of_heads(numerators, (block, width))
            total = of_heads(totals, (block, width))
            numerator_ref[...] = numerator
            total_ref[...] = total
            mixed_ref[...] = (numerator / total).astype(LOW)

    early = lambda i: (jnp.minimum(i, steps - 1), 0)
    late = lambda i: (jnp.maximum(i - steps, 0), 0)
    once = dict(pipeline_mode=pl.Buffered(1))

    def still(shape):
        return pl.BlockSpec(shape, lambda i: (0,) * len(shape), **once)

    full = pl.BlockSpec((rows, width), lambda i: (0, 0))
    late_block = pl.BlockSpec((block, width), late)
    in_hbm = pl.BlockSpec(memory_space=pltpu.HBM)
    return pl.pallas_call(
        kernel,
        grid=(2 * steps,),
        out_shape=[pltpu.HBM((rows, features), LOW)]
        + [pltpu.HBM((rows, width), LOW)] * 4
        + [pltpu.HBM((rows, width), f32)] * 2,
        in_specs=[pl.BlockSpec(memory_space=pltpu.SMEM)]
        + [in_hbm] * (len(given) + 1)
        + [
            still(own.shape),
            still(other.shape),
            still((rows, width)),
            still((rows, width)),
            pl.BlockSpec((block, 1), late),
            still((1, rows)),
        ],
        out_specs=[pl.BlockSpec((block, features), early)]
        + [full] * 3
        + [late_block] * 3,
        scratch_shapes=[
            pltpu.VMEM((rows, features), LOW),
            pltpu.VMEM((features, total_width), LOW),
            pltpu.VMEM((8, features), f32),
            pltpu.SemaphoreType.DMA((len(pieces),)),
        ],
        compiler_params=pltpu.CompilerParams(
            dimension_semantics=("arbitrary",), vmem_limit_bytes=40 << 20
        ),
        cost_estimate=pl.CostEstimate(
            flops=2 * rows * features * total_width + 8 * rows * rows * width,
            transcendentals=2 * rows * rows,
            bytes_accessed=4 * rows * features + 4 * features * total_width + 20 * rows * width,
        ),
    )(token_places, *(in_main(a) for a in (*given, tokens)), own, other, *(in_main(a) for a in (cosine, sine, column, line)))


def project(mixed, outs):
    rows, width = mixed.shape
    depth, block = outs[0].shape[2], rows // 4

    def kernel(mixed_ref, own_ref, other_ref, *refs):
        for i, ref in enumerate(refs):
            values = mixed_ref[i * block : (i + 1) * block, :]
            for j in range(8):
                weight = (own_ref, other_ref)[j // 4][j % 4]
                ref[:, j * depth : (j + 1) * depth] = product(values, weight).astype(LOW)

    whole = pl.BlockSpec(memory_space=pltpu.VMEM)
    return pl.pallas_call(
        kernel,
        out_shape=[jax.ShapeDtypeStruct((block, 8 * depth), LOW)] * 4,
        in_specs=[whole] * 3,
        out_specs=[whole] * 4,
        cost_estimate=pl.CostEstimate(
            flops=16 * rows * width * depth, transcendentals=0, bytes_accessed=20 * rows * depth
        ),
    )(mixed, *outs)


def attention_back(pieces, outs, queries, keys, values, mixed, numerator, total, *places):
    rows, width = queries.shape
    depth, count, steps = outs[0].shape[2], pieces[0].shape[0], 4
    features = 8 * depth
    block, group = rows // steps, len(pieces) // steps
    cosine, sine, column, line = places
    f32 = jnp.float32

    def kernel(*refs):
        ins, refs = refs[: len(pieces)], refs[len(pieces) :]
        out_refs, refs = refs[:2], refs[2:]
        q_ref, k_ref, v_ref, mixed_ref, num_ref, total_ref, *refs = refs
        cos_ref, sin_ref, col_ref, line_ref, grad_ref, keep_ref, give_ref, *refs = refs
        held, w_ref, key_sum, value_sum, output_sum, sems = refs
        step = pl.program_id(0)

        def copy(i):
            return pltpu.make_async_copy(ins[i], held.at[pl.ds(i * count, count)], sems.at[i])

        for at in range(steps):

            @pl.when(step == at)
            def _(at=at):
                if at == 0:
                    for i in range(len(pieces)):
                        copy(i).start()
                    for i in range(8):
                        w_ref[:, i * depth : (i + 1) * depth] = out_refs[i // 4][i % 4]
                    key_sum[...] = jnp.zeros_like(key_sum)
                    value_sum[...] = jnp.zeros_like(value_sum)
                    output_sum[...] = jnp.zeros_like(output_sum)
                for i in range(at * group, (at + 1) * group):
                    copy(i).wait()

        at = pl.ds(pl.multiple_of(step * block, block), block)
        branch = held[at, :]
        output_sum[...] += contract_rows(mixed_ref[...], branch)
        mixed_grad = contract_cols(branch, w_ref[...])
        totals = total_ref[...]
        numerator_grad = (mixed_grad / totals).astype(LOW)
        shares = mixed_grad * num_ref[...] / (totals * totals)
        allowed = col_ref[...] >= line_ref[...]
        query_parts = []
        all_keys, all_values = k_ref[...], v_ref[...]
        for index in range(width // HD):
            query = only_head(q_ref[...], index) * 0.125
            grad = only_head(numerator_grad, index)
            total_grad = -jnp.sum(only_head(shares, index), axis=1, keepdims=True)
            weights = jnp.where(allowed, jnp.exp(contract_cols(query, all_keys)), 0.0)
            through = contract_cols(grad, all_values)
            slopes = (weights * (through + total_grad)).astype(LOW)
            query_parts.append(product(slopes, all_keys))
            key_sum[...] += contract_rows(query, slopes)
            value_sum[...] += contract_rows(grad, weights.astype(LOW))
        query_grad = of_heads(query_parts, (block, width)) * 0.125

        def unturned(u, where):
            return (u * cos_ref[where, :] - swapped(u) * sin_ref[where, :]).astype(LOW)

        grad_ref[at, :width] = unturned(query_grad, at)

        @pl.when(step == steps - 1)
        def _():
            everywhere = pl.ds(0, rows)
            grad_ref[:, width : 2 * width] = unturned(key_sum[...].T, everywhere)
            grad_ref[:, 2 * width :] = value_sum[...].T.astype(LOW)
            keep_ref[...] = output_sum[:, : features // 2].T.astype(LOW)
            give_ref[...] = output_sum[:, features // 2 :].T.astype(LOW)

    def still(shape):
        return pl.BlockSpec(shape, lambda i: (0,) * len(shape), pipeline_mode=pl.Buffered(1))

    def whole(shape):
        return pl.BlockSpec(shape, lambda i: (0,) * len(shape))

    moving = pl.BlockSpec((block, width), lambda i: (i, 0))
    half = (features // 2, width)
    return pl.pallas_call(
        kernel,
        grid=(steps,),
        out_shape=[
            jax.ShapeDtypeStruct((rows, 3 * width), LOW),
            jax.ShapeDtypeStruct(half, LOW),
            jax.ShapeDtypeStruct(half, LOW),
        ],
        in_specs=[pl.BlockSpec(memory_space=pltpu.HBM)] * len(pieces)
        + [still(outs[0].shape), still(outs[1].shape), moving, still((rows, width)), still((rows, width))]
        + [moving, moving, moving, still((rows, width)), still((rows, width))]
        + [pl.BlockSpec((block, 1), lambda i: (i, 0)), still((1, rows))],
        out_specs=[whole((rows, 3 * width)), whole(half), whole(half)],
        scratch_shapes=[
            pltpu.VMEM((rows, features), LOW),
            pltpu.VMEM((width, features), LOW),
            pltpu.VMEM((width, rows), f32),
            pltpu.VMEM((width, rows), f32),
            pltpu.VMEM((width, features), f32),
            pltpu.SemaphoreType.DMA((len(pieces),)),
        ],
        compiler_params=pltpu.CompilerParams(
            dimension_semantics=("arbitrary",), vmem_limit_bytes=32 << 20
        ),
        cost_estimate=pl.CostEstimate(
            flops=4 * rows * features * width + 20 * rows * rows * width,
            transcendentals=2 * rows * rows,
            bytes_accessed=2 * rows * features + 24 * rows * width,
        ),
    )(*(in_main(a) for a in (*pieces, *outs, queries, keys, values, mixed, numerator, total, *places)))


def turned_pieces(value):
    total, rows, columns = value.shape
    half = rows // 2

    def kernel(value_ref, first_ref, second_ref):
        first_ref[0] = value_ref[0, :half].T
        second_ref[0] = value_ref[0, half:].T

    size = value.size * value.dtype.itemsize
    return pl.pallas_call(
        kernel,
        grid=(total,),
        out_shape=[jax.ShapeDtypeStruct((total, columns, half), value.dtype)] * 2,
        in_specs=[pl.BlockSpec((1, rows, columns), lambda i: (i, 0, 0))],
        out_specs=[pl.BlockSpec((1, columns, half), lambda i: (i, 0, 0))] * 2,
        cost_estimate=pl.CostEstimate(flops=0, transcendentals=0, bytes_accessed=2 * size),
    )(value)


def place_rows(pieces, places, dtype):
    count, features = pieces[0].shape

    def kernel(at_ref, *refs):
        for i, ref in enumerate(refs[:-1]):
            first = pl.multiple_of(at_ref[i] * count, count)
            refs[-1][pl.ds(first, count), :] = ref[...].astype(dtype)

    whole = pl.BlockSpec(memory_space=pltpu.VMEM)
    shape = jax.ShapeDtypeStruct((len(pieces) * count, features), dtype)
    return pl.pallas_call(
        kernel,
        out_shape=shape,
        in_specs=[pl.BlockSpec(memory_space=pltpu.SMEM)] + [whole] * len(pieces),
        out_specs=whole,
        cost_estimate=pl.CostEstimate(
            flops=0, transcendentals=0, bytes_accessed=6 * shape.size
        ),
    )(places, *pieces)


def both_of(one, two, start, stop):
    return one[start:stop].astype(jnp.float32) + two[start:stop].astype(jnp.float32)


class Stages:
    def step(self, *flying):
        names = [name for name in vars(self) if name not in flying]
        for name, value in zip(names, tie(*(getattr(self, name) for name in names))):
            setattr(self, name, value)

    def take(self, *names):
        values = [getattr(self, name) for name in names]
        for name in names:
            delattr(self, name)
        return values

    def scatter_0(self, p, rows, rows_of):
        setattr(self, p + "in", swap(rows_of(3), CORE))
        setattr(self, p + "keep", rows_of(1))

    def scatter_1(self, p, rows, rows_of):
        count = rows // 16
        keep, arrived = self.take(p + "keep", p + "in")
        third, middle, first = (
            both_of(keep, arrived, start * count, stop * count).astype(LOW)
            for start, stop in ((3, 4), (1, 3), (0, 1))
        )
        setattr(self, p + "third", swap(third, X))
        setattr(self, p + "middle", swap(middle, X))
        setattr(self, p + "first", first)
        setattr(self, p + "in", swap(rows_of(2), CORE))
        setattr(self, p + "keep", rows_of(0))

    def scatter_2(self, p):
        first, third = self.take(p + "first", p + "third")
        keep, arrived = getattr(self, p + "keep"), getattr(self, p + "in")
        count = first.shape[0]
        last = both_of(keep, arrived, 3 * count, 4 * count) + third.astype(jnp.float32)
        setattr(self, p + "last", swap(last.astype(LOW), CTX, 1))
        setattr(self, p + "first", swap(first, X))

    def scatter_3(self, p):
        middle, last = self.take(p + "middle", p + "last")
        keep, arrived = getattr(self, p + "keep"), getattr(self, p + "in")
        count = last.shape[0]
        far = both_of(keep, arrived, 2 * count, 3 * count) + last.astype(jnp.float32)
        far = far + middle[count:].astype(jnp.float32)
        near = both_of(keep, arrived, count, 2 * count) + middle[:count].astype(jnp.float32)
        setattr(self, p + "far", swap(far.astype(LOW), CTX, 2))
        setattr(self, p + "near", swap(near.astype(LOW), CTX, 1))

    def scatter_4(self, p):
        keep, arrived, *values = self.take(
            p + "keep", p + "in", p + "first", p + "near", p + "far"
        )
        total = both_of(keep, arrived, 0, values[0].shape[0])
        return total + sum(value.astype(jnp.float32) for value in values)

    def gather_0(self, shard):
        self.g0 = shard
        self.g1, self.g2 = swap(shard, CTX, 1), swap(shard, CTX, 2)
        self.x0, self.c0 = swap(shard, X), swap(shard, CORE)

    def gather_1(self):
        self.g3 = swap(self.g2, CTX, 1)
        self.x1, self.x2 = swap(self.g1, X), swap(self.g2, X)

    def gather_2(self):
        self.x3 = swap(self.g3, X)
        self.c1, self.c2, self.c3 = (swap(g, CORE) for g in (self.g1, self.g2, self.g3))
        self.c4 = swap(self.x0, CORE)

    def gather_3(self):
        self.c5, self.c6, self.c7 = (swap(x, CORE) for x in (self.x1, self.x2, self.x3))
        names = [k + str(j) for k in "gx" for j in range(4)] + ["c" + str(j) for j in range(8)]
        return self.take(*names)


def spread(pieces):
    return lax.all_to_all(pieces, CTX, 0, 0, tiled=True)


def side_by_side(pieces):
    return jnp.concatenate(list(pieces), axis=1)


def by_columns(weight, extent):
    return jnp.stack([weight[:, j * extent : (j + 1) * extent] for j in range(4)])


def both(own):
    return jnp.concatenate([own, swap(own, SEQ)])


def halves(left, right):
    grad = contract_rows(left, right).astype(LOW)
    half = grad.shape[0] // 2
    return grad[:half], grad[half:]


def added(keep, arrived):
    return (keep.astype(jnp.float32) + arrived.astype(jnp.float32)).astype(LOW)


def fast_device(
    tokens,
    query_weight,
    key_weight,
    value_weight,
    output_weight,
    gate_weight,
    up_weight,
    down_weight,
    attention_gain,
    feedforward_gain,
    order,
    cotangent,
):
    f32 = jnp.float32
    seq, ctx = lax.axis_index(SEQ), lax.axis_index(CTX)
    x, core = lax.axis_index(X), lax.axis_index(CORE)
    local_rows = tokens.shape[0]
    count = local_rows // 4
    rows = 16 * count
    width = query_weight.shape[1] // 4
    unit = gate_weight.shape[1] // 4
    depth = query_weight.shape[0]

    def turned(values):
        middle_column = values.shape[1] // 2
        other_way = jnp.concatenate([values[:, middle_column:], values[:, :middle_column]], axis=1)
        return jnp.where(seq == 0, values, other_way)

    own_places = jnp.stack([(x ^ a) * 2 + (core ^ b) for b in range(2) for a in range(2)])

    def local(values, a, b):
        return lax.dynamic_slice_in_dim(values, ((x ^ a) * 2 + (core ^ b)) * count, count, 0)

    features = tokens.shape[1]
    v = Stages()

    qkv_pieces = first_pieces(
        query_weight, key_weight, value_weight, attention_gain, feedforward_gain
    )
    v.qkv_own, v.tokens = tie(qkv_pieces, tokens)
    v.qkv_own = spread(v.qkv_own)
    v.tokens = turned(v.tokens)
    shard = local(v.tokens, 0, 0)
    v.g1, v.g2 = swap(shard, CTX, 1), swap(shard, CTX, 2)
    v.cotangent, v.order = cotangent, order
    v.gate, v.up, v.down, v.output = gate_weight, up_weight, down_weight, output_weight
    v.step("qkv_own")

    v.g3, v.x1, v.x2 = swap(v.g2, CTX, 1), swap(v.g1, X), swap(v.g2, X)
    v.output = v.output.reshape(4, width, depth)
    blocks = jnp.arange(16, dtype=jnp.int32)
    stored = (
        (ctx ^ (blocks & 3)) * local_rows
        + (x ^ ((blocks >> 2) & 1)) * (2 * count)
        + (core ^ (blocks >> 3)) * count
    )
    stored = (stored[:, None] + jnp.arange(count, dtype=jnp.int32)[None, :]).reshape(-1)
    slots = jnp.arange(order.shape[0], dtype=jnp.int32)
    places = jnp.sum(
        jnp.where((stored // BLOCK)[:, None] == slots[None, :], v.order[None, :], 0), axis=1
    )
    places = places * BLOCK + stored % BLOCK
    v.column, v.line = places[:, None], places[None, :]
    entry = jnp.arange(width, dtype=jnp.int32) % (HD // 2)
    inverse = THETA ** (-(entry.astype(f32) * 2.0) / HD)
    sign = jnp.where(jnp.arange(width) % HD < HD // 2, -1.0, 1.0).astype(f32)
    angle = places.astype(f32)[:, None] * inverse[None, :]
    v.cosine, v.sine = jnp.cos(angle), jnp.sin(angle) * sign[None, :]
    del v.order
    v.step("qkv_own", "x1", "x2")

    v.x3 = swap(v.g3, X)
    v.cotangent = turned(v.cotangent)
    v.shard = local(v.cotangent, 0, 0)
    v.up = by_columns(v.up, unit)
    v.step("x3")

    v.qkv_o = swap(v.qkv_own, SEQ)
    v.output = spread(v.output)
    v.down, v.down_late = turned_pieces(v.down.reshape(4, unit, depth))
    v.c1, v.c2, v.c3 = (swap(g, CORE) for g in (v.g1, v.g2, v.g3))
    v.c4, v.c5 = swap(v.x1, CORE), swap(v.x2, CORE)
    v.step("qkv_o")

    def whole(values, line, line_x, other, other_x):
        return stack_rows(
            [None, *line, None, *line_x, None, *other, None, *other_x], values, own_places
        )

    v.d1, v.d2 = swap(v.shard, CTX, 1), swap(v.shard, CTX, 2)
    v.gate = spread(by_columns(v.gate, unit))
    del v.shard
    v.c6 = swap(v.x3, CORE)
    v.step("gate", "d1", "d2")

    v.gain_first, v.gain_second = (
        jnp.concatenate([half[:, depth + i, :depth] for half in (v.qkv_own, v.qkv_o)])
        .reshape(1, 8 * depth)
        .astype(f32)
        for i in range(2)
    )
    g1, g2, g3, x1, x2, x3 = v.take("g1", "g2", "g3", "x1", "x2", "x3")
    c1, c2, c3, c4, c5, c6 = v.take("c1", "c2", "c3", "c4", "c5", "c6")
    outputs = attention(
        [None, g1, g2, g3, None, x1, x2, x3, None, c1, c2, c3, None, c4, c5, c6],
        v.tokens,
        own_places,
        v.qkv_own,
        v.qkv_o,
        v.cosine,
        v.sine,
        v.column,
        v.line,
    )
    v.normed, v.queries, v.keys, v.values, v.mixed, v.numerator, v.total = outputs
    v.output_other = swap(v.output, SEQ)
    v.step("gate")

    def attended(index):
        return v.take("part%d" % index)[0]

    v.e1, v.e2 = swap(v.d1, X), swap(v.d2, X)
    v.part0, v.part1, v.part2, v.part3 = project(v.mixed, [v.output, v.output_other])
    v.scatter_0("s_", rows, attended)
    v.step("e1", "e2")
    v.up = spread(v.up)
    v.gate_o = swap(v.gate, SEQ)
    v.scatter_1("s_", rows, attended)
    v.d3 = swap(v.d2, CTX, 1)
    v.f1, v.f2 = swap(v.d1, CORE), swap(v.d2, CORE)
    v.step("up", "gate_o", "d3", "s_middle")
    v.scatter_2("s_")
    v.step("s_first", "gate_o")
    v.scatter_3("s_")
    v.up_o = swap(v.up, SEQ)
    v.e3, v.f3 = swap(v.d3, X), swap(v.d3, CORE)
    v.step("up_o", "e3")
    v.middle = local(v.tokens, 0, 0).astype(f32) + v.scatter_4("s_")
    v.scale_second = lax.rsqrt(jnp.mean(v.middle * v.middle, axis=1, keepdims=True) + EPS)
    v.gather_0((v.middle * v.scale_second * v.gain_second).astype(LOW))
    v.f4, v.f5, v.f6 = (swap(e, CORE) for e in (v.e1, v.e2, v.e3))
    v.step("x0", "up_o")
    v.gather_1()
    d1, d2, d3, e1, e2, e3 = v.take("d1", "d2", "d3", "e1", "e2", "e3")
    f1, f2, f3, f4, f5, f6 = v.take("f1", "f2", "f3", "f4", "f5", "f6")
    v.every_cotangent = whole(v.cotangent, [d1, d2, d3], [e1, e2, e3], [f1, f2, f3], [f4, f5, f6])
    v.step("x1", "x2")
    v.gather_2()
    v.down = spread(v.down)
    pieces = v.gather_3()
    for i, piece in enumerate(pieces):
        setattr(v, "piece%d" % i, piece)
    v.step()

    v.down_late = spread(v.down_late)
    v.down_o = swap(v.down, SEQ)
    v.normed_two, v.hidden, v.gate_slope, v.up_slope = feed_forward(
        v.take(*("piece%d" % i for i in range(16))),
        [own.reshape(4 * depth, unit) for own in (v.gate, v.gate_o)],
        [own.reshape(4 * depth, unit) for own in (v.up, v.up_o)],
    )
    v.step("down_o")
    v.late_other = swap(v.down_late, SEQ)
    v.down_k, v.down_g = halves(v.every_cotangent, v.hidden)
    v.gate_full = jnp.concatenate(v.take("gate", "gate_o")).reshape(8 * depth, unit)
    v.up_full = jnp.concatenate(v.take("up", "up_o")).reshape(8 * depth, unit)
    v.step()
    v.gate_grad, v.up_grad = feed_back(
        v.take("every_cotangent")[0],
        [
            own.reshape(4 * depth, unit // 2)
            for own in (v.down, v.down_o, v.down_late, v.late_other)
        ],
        *v.take("gate_slope", "up_slope"),
    )
    v.down_g = swap(v.down_g, SEQ)
    v.step("down_g")

    def quarter(values, index):
        size = rows // 4
        return values[index * size : (index + 1) * size]

    def normed_grads(index):
        gate, up = quarter(v.gate_grad, index), quarter(v.up_grad, index)
        return (contract_cols(gate, v.gate_full) + contract_cols(up, v.up_full)).astype(LOW)

    v.scatter_0("s_", rows, normed_grads)
    v.step("down_g")
    v.scatter_1("s_", rows, normed_grads)
    v.gate_k, v.gate_g = halves(v.normed_two, v.gate_grad)
    v.step("down_g", "s_middle")
    del v.gate_full, v.up_full
    v.scatter_2("s_")
    v.gate_g = swap(v.gate_g, SEQ)
    v.up_k, v.up_g = halves(v.normed_two, v.up_grad)
    v.step("s_first", "gate_g", "down_g")
    del v.normed_two, v.gate_grad, v.up_grad
    v.scatter_3("s_")
    v.up_g = swap(v.up_g, SEQ)
    v.down_full = jnp.concatenate(
        [
            jnp.concatenate(v.take("down", "down_o")),
            jnp.concatenate(v.take("down_late", "late_other")),
        ],
        axis=2,
    ).reshape(8 * depth, unit)
    v.step("gate_g", "up_g")
    normed_two_grad = v.scatter_4("s_")
    middle, scale_second = v.middle, v.scale_second
    scaled = normed_two_grad * v.gain_second
    v.middle_grad = (
        local(v.cotangent, 0, 0).astype(f32)
        + scale_second * scaled
        - middle * scale_second**3 * jnp.mean(scaled * middle, axis=1, keepdims=True)
    )
    del v.cotangent, v.scale_second, v.gain_second
    v.gather_0(v.middle_grad.astype(LOW))
    v.qkv_full = jnp.concatenate([v.qkv_own, v.qkv_o])[:, :depth].reshape(8 * depth, 3 * width)
    del v.qkv_own, v.qkv_o
    v.step("up_g", "x0")
    v.gather_1()
    v.down_sum = added(*v.take("down_k", "down_g")).reshape(4, depth, unit)
    v.gate_sum = added(*v.take("gate_k", "gate_g")).reshape(4, depth, unit)
    v.step("up_g", "x1", "x2")

    def fed(index):
        return contract_cols(quarter(v.hidden, index), v.down_full).astype(LOW)

    def projected_grads(index):
        return contract_cols(quarter(v.projected_grad, index), v.qkv_full).astype(LOW)

    v.gather_2()
    v.down = spread(v.take("down_sum")[0])
    v.step("down")
    pieces = v.gather_3()
    for i, piece in enumerate(pieces):
        setattr(v, "piece%d" % i, piece)
    v.step()

    v.gate = spread(v.take("gate_sum")[0])
    v.projected_grad, v.out_k, v.out_g = attention_back(
        v.take(*("piece%d" % i for i in range(16))),
        v.take("output", "output_other"),
        *v.take("queries", "keys", "values", "mixed", "numerator", "total"),
        *v.take("cosine", "sine", "column", "line"),
    )
    v.step("gate")
    v.out_g = swap(v.out_g, SEQ)
    v.scatter_0("s_", rows, projected_grads)
    v.step("out_g")
    v.scatter_1("s_", rows, projected_grads)
    v.scatter_0("p_", rows, fed)
    v.step("out_g", "s_middle")
    v.scatter_2("s_")
    v.up = spread(added(*v.take("up_k", "up_g")).reshape(4, depth, unit))
    v.qkv_k, v.qkv_g = halves(v.normed, v.projected_grad)
    del v.projected_grad, v.qkv_full, v.normed
    v.scatter_1("p_", rows, fed)
    v.step("up", "s_first", "p_middle")
    del v.hidden, v.down_full
    v.scatter_3("s_")
    v.qkv_g = swap(v.qkv_g, SEQ)
    v.scatter_2("p_")
    v.down_wgrad = v.take("down")[0].transpose(0, 2, 1).reshape(4 * unit, depth).astype(f32)
    v.step("p_first", "qkv_g")
    v.scatter_3("p_")
    sums = [added(*v.take(kind + "_k", kind + "_g")) for kind in ("qkv", "out")]
    v.qkv_sum = jnp.concatenate(sums, axis=1).reshape(4, depth, 4 * width)
    own_input = local(v.tokens, 0, 0).astype(f32)
    normed_grad = v.scatter_4("s_")
    scale_own = lax.rsqrt(jnp.mean(own_input * own_input, axis=1, keepdims=True) + EPS)
    scaled = normed_grad * v.gain_first
    input_grad = (
        v.middle_grad
        + scale_own * scaled
        - own_input * scale_own**3 * jnp.mean(scaled * own_input, axis=1, keepdims=True)
    )
    v.input_grad = input_grad.astype(LOW)
    v.step()
    v.qkv = spread(v.take("qkv_sum")[0])
    v.produced = turned((v.take("middle")[0] + v.scatter_4("p_")).astype(LOW))
    v.input_grad = turned(v.input_grad)
    v.input_x, v.input_core = swap(v.input_grad, X), swap(v.input_grad, CORE)
    v.produced_x, v.produced_core = swap(v.produced, X), swap(v.produced, CORE)
    v.gate_wgrad = side_by_side(v.take("gate")[0]).astype(f32)
    v.up_wgrad = side_by_side(v.take("up")[0]).astype(f32)

    def gain_grad(gain, *pairs):
        part = sum(jnp.sum(w.astype(f32) * g, axis=1) for w, g in pairs)
        return part / gain.astype(f32)

    v.second_gain = gain_grad(
        feedforward_gain, (gate_weight, v.gate_wgrad), (up_weight, v.up_wgrad)
    )
    v.step("qkv")
    v.input_far = swap(v.input_x, CORE)
    v.produced_far = swap(v.produced_x, CORE)
    v.step("qkv")
    input_pieces = v.take("input_grad", "input_x", "input_core", "input_far")
    v.input_out = place_rows(input_pieces, own_places, f32)
    produced_pieces = v.take("produced", "produced_x", "produced_core", "produced_far")
    v.block_output = place_rows(produced_pieces, own_places, LOW)
    v.step()
    block_output, input_grad = v.block_output, v.input_out
    qkv_pieces, output_pieces = v.qkv[:, :, : 3 * width], v.qkv[:, :, 3 * width :]

    query_wgrad, key_wgrad, value_wgrad = (
        side_by_side(qkv_pieces[:, :, first : first + width]).astype(f32)
        for first in (0, width, 2 * width)
    )
    gate_wgrad, up_wgrad = v.gate_wgrad, v.up_wgrad

    gain_grads = jnp.stack(
        [
            gain_grad(
                attention_gain,
                (query_weight, query_wgrad),
                (key_weight, key_wgrad),
                (value_weight, value_wgrad),
            ),
            v.second_gain,
        ]
    )
    across = lax.ppermute(gain_grads, (X, CORE), [(i, i ^ 3) for i in range(4)])
    gain_grads = gain_grads + swap(gain_grads, CORE) + swap(gain_grads, X) + across
    return (
        block_output,
        input_grad,
        query_wgrad,
        key_wgrad,
        value_wgrad,
        output_pieces.transpose(0, 2, 1).reshape(4 * width, depth).astype(f32),
        gate_wgrad,
        up_wgrad,
        v.down_wgrad,
        gain_grads[0],
        gain_grads[1],
    )


def fast_solution(mesh):
    sizes = mesh.shape
    lines = Mesh(
        mesh.devices.reshape(sizes[SEQ], sizes[CTX], 2, 2), (SEQ, CTX, X, CORE)
    )
    rows, heads = (SEQ, CTX), (X, CORE)
    wide, tall = P(rows, heads), P(heads, rows)
    return jax.shard_map(
        fast_device,
        mesh=lines,
        in_specs=(
            P(rows, None),
            wide,
            wide,
            wide,
            tall,
            wide,
            wide,
            tall,
            P(rows),
            P(rows),
            P(),
            P(rows, None),
        ),
        out_specs=(
            P(rows, None),
            P(rows, None),
            wide,
            wide,
            wide,
            tall,
            wide,
            wide,
            tall,
            P(rows),
            P(rows),
        ),
        check_vma=False,
    )


def solution(mesh):
    sizes = mesh.shape
    if mesh.axis_names == (SEQ, CTX, TP) and tuple(sizes.values()) == (2, 4, 4):
        return fast_solution(mesh)
    return general_solution(mesh)
```
